256 devices in a mesh: guide: 2 (over z_lo), seq: 32 (over x, y, core), tp: 4 (over z_hi).
Axes of the slice: x: 4, y: 4, z: 8 (z_hi: 4, z_lo: 2; z = z_hi * 2 + z_lo), core: 2. Of those that a mesh axis runs over, the one named last changes fastest.
Arguments:
- hidden: bfloat16 [2048, 3072], P('seq', 'tp'), may hold values from -6 to 6
- seg_ids: int32 [2048], P('seq'), may hold values from 0 to 3, never falling along the last dimension, each value on 1 to 769 neighbouring positions
- modulation: bfloat16 [2, 4, 3, 3072], P('guide'), may hold values from -4 to 4
- qk_gain: float32 [2, 128], replicated, may hold values from 0.5 to 5
- w_qkv: bfloat16 [3072, 3, 1536], P(None, None, 'tp'), may hold values from -0.109375 to 0.109375
- w_mlp_in: bfloat16 [3072, 6144], P('seq', 'tp'), may hold values from -0.109375 to 0.109375
- w_out: bfloat16 [1536, 3072], P('tp'), may hold values from -0.5 to 0.5
- w_mlp_back: bfloat16 [3072, 6144], P('seq', 'tp'), may hold values from -0.078125 to 0.078125
Outputs:
- guided: bfloat16 [2048, 4, 2, 384], P('seq', 'tp', 'guide')
The draws below stay inside these ranges and needn't reach their ends.
Inputs may be any that keep to these rules, and one draw needn't show every extreme that they name: `seg_ids`: 4 requests lie end to end in order; each holds 1 to 769 rows and one holds exactly 769.
All inputs are finite; a program needn't handle non-finite values.
Results may differ from the reference program's by a relative error of at most 0.014.
The reference program's roundings to bfloat16 on the way count: a program that leaves them out, or rounds other values in their place, can miss the bound.
Values may be sent and summed in bfloat16 or wider, within the bound.
A program may use at most 128 MiB of HBM per device.

```python
import math
import jax
import jax.numpy as jnp
import numpy as np
from jax import lax

D = 3072
HEAD = 128
HEADS = 12
MLP = 6144
TOK_DEV = 64
TOKENS = 2048
REQ = 4
MOST = 769
REACH = 12
N_SEQ = 32
N_TP = 4


def draw_qk_gain(key, part):
    low = jnp.log(0.5)
    high = jnp.log(2.0)
    return jnp.exp(jax.random.uniform(key, (2, HEAD), jnp.float32, low, high))


def level_of(stream_key, extent, cuts, smallest, top_value):
    level, own = 1.0, jax.random.fold_in(stream_key, 6)
    for dim, blocks in cuts:
        heights = jnp.exp(jax.random.uniform(jax.random.fold_in(own, dim), (blocks,), jnp.float32, smallest / len(cuts), top_value / len(cuts)))
        level = level * jnp.repeat(heights, extent[dim] // blocks).reshape([-1 if axis == dim else 1 for axis in range(len(extent))])
    return level


def length_profile(amount, total, limit, slope):
    weights = [(1 << 20) // math.isqrt(grade ** slope) + 1 for grade in range(2, amount + 1)]
    surplus, counts = total - limit - (amount - 1), [1] * (amount - 1)
    while surplus > 0:
        movable = [i for i in range(amount - 1) if counts[i] < limit]
        mass, left = sum([weights[i] for i in movable]), surplus
        for i in movable:
            addition = min(limit - counts[i], max(1, left * weights[i] // mass), surplus)
            counts[i] = counts[i] + addition
            surplus = surplus - addition
    return np.array([limit] + counts)


def uneven_parts(rng, number_of, total, limit, slope):
    if number_of == 2:
        one = jax.random.randint(rng, (), max(1, total - limit), min(limit, total - 1) + 1)
        return jnp.stack([one, total - one])
    tallies = jnp.asarray(length_profile(number_of, total, limit, slope), jnp.int32)
    couples = (number_of - 1) // 2
    donor, receiver = tallies[1:1 + 2 * couples:2], tallies[2:2 + 2 * couples:2]
    slack = jnp.minimum(donor - 1, limit - receiver)
    passed = jax.random.randint(jax.random.fold_in(rng, 1), (couples,), 0, 1 << 20) % (slack + 1)
    tallies = tallies.at[1:1 + 2 * couples:2].set(donor - passed).at[2:2 + 2 * couples:2].set(receiver + passed)
    return tallies[jax.random.permutation(jax.random.fold_in(rng, 2), number_of)]


def gaussian(own_key, dims, spread, limit, shards=(), dtype=jnp.bfloat16):
    array = jax.random.normal(own_key, dims, jnp.float32) * spread
    if len(shards) > 0:
        array = level_of(own_key, dims, shards, -0.22, 0.18) * array
    return jnp.clip(array, min=-limit, max=limit).astype(dtype)


def setup_inputs(seed: int = 0) -> dict:
    seeds = jax.random.split(jax.random.key(seed), 9)
    hidden = gaussian(seeds[0], (TOKENS, D), 1.0, 6.0, ((0, 32), (1, 4)))
    seg_ids = jnp.searchsorted(jnp.cumsum(uneven_parts(seeds[1], REQ, TOKENS, MOST, 1)), jnp.arange(TOKENS), side="right").astype(jnp.int32)
    modulation = gaussian(seeds[2], (2, REQ, 3, D), 0.8, 4.0, ((0, 2),))
    qk_gain = draw_qk_gain(jax.random.fold_in(seeds[8], 71), 0)
    w_qkv = gaussian(seeds[4], (D, 3, HEADS * HEAD), D ** -0.5, 0.109375, ((2, 4),))
    w_mlp_in = gaussian(seeds[5], (D, MLP), D ** -0.5, 0.109375, ((0, 32), (1, 4)))
    w_out = gaussian(seeds[6], (HEADS * HEAD, D), HEAD ** -0.5, 0.5, ((0, 4),))
    w_mlp_back = gaussian(seeds[7], (D, MLP), MLP ** -0.5, 0.078125, ((0, 32), (1, 4)))
    return dict(hidden=hidden, seg_ids=seg_ids, modulation=modulation, qk_gain=qk_gain, w_qkv=w_qkv, w_mlp_in=w_mlp_in, w_out=w_out, w_mlp_back=w_mlp_back)


guidance = 3.5

def head_norm(values, gain):
    return values * lax.rsqrt(lax.optimization_barrier(jnp.mean(values * values, axis=-1, keepdims=True)) + 1e-06) * gain

def half_layer(hidden, seg_ids, mod, qk_gain, w_qkv, w_mlp_in, w_out, w_mlp_back):
    width = HEADS * HEAD
    group = width // N_TP
    mlp_group = MLP // N_TP
    xf = hidden.astype(jnp.float32)
    centred = xf - lax.optimization_barrier(jnp.mean(xf, axis=-1, keepdims=True))
    normed = centred * lax.rsqrt(lax.optimization_barrier(jnp.mean(centred * centred, axis=-1, keepdims=True)) + 1e-06)
    shift = mod[:, 0][seg_ids].astype(jnp.float32)
    scale = mod[:, 1][seg_ids].astype(jnp.float32)
    gate = mod[:, 2][seg_ids].astype(jnp.float32)
    xmod = (normed * (1.0 + scale) + shift).astype(jnp.bfloat16)
    proj = jnp.dot(xmod, w_qkv.reshape(D, 3 * width), preferred_element_type=jnp.float32)
    proj = proj.reshape(TOKENS, 3, HEADS, HEAD)
    mlp_pre = jnp.dot(xmod, w_mlp_in, preferred_element_type=jnp.float32)
    mlp_act = jax.nn.gelu(mlp_pre, approximate=True).astype(jnp.bfloat16)
    query = head_norm(proj[:, 0], qk_gain[0]).astype(jnp.bfloat16)
    key = head_norm(proj[:, 1], qk_gain[1]).astype(jnp.bfloat16)
    value = proj[:, 2].astype(jnp.bfloat16)
    margin = REACH * TOK_DEV
    window = (2 * REACH + 1) * TOK_DEV
    key_pad = jnp.pad(key, ((margin, margin), (0, 0), (0, 0)))
    value_pad = jnp.pad(value, ((margin, margin), (0, 0), (0, 0)))
    seg_plus = (seg_ids + 1).astype(jnp.int32)
    seg_pad = jnp.pad(seg_plus, (margin, margin))

    def block(index):
        start = (index * TOK_DEV).astype(jnp.int32)
        q_rows = lax.dynamic_slice_in_dim(query, start, TOK_DEV, 0).astype(jnp.float32)
        q_seg = lax.dynamic_slice_in_dim(seg_plus, start, TOK_DEV, 0)
        k_rows = lax.dynamic_slice_in_dim(key_pad, start, window, 0).astype(jnp.float32)
        v_rows = lax.dynamic_slice_in_dim(value_pad, start, window, 0).astype(jnp.float32)
        k_seg = lax.dynamic_slice_in_dim(seg_pad, start, window, 0)
        score = jnp.einsum('qhe,khe->hqk', q_rows, k_rows) * HEAD ** (-0.5)
        score = jnp.where((q_seg[:, None] == k_seg[None, :])[None], score, -1e+30)
        peak = lax.optimization_barrier(jnp.max(score, axis=-1, keepdims=True))
        weight = jnp.exp(score - peak)
        total = lax.optimization_barrier(jnp.sum(weight, axis=-1))
        rounded = lax.optimization_barrier(weight.astype(jnp.bfloat16)).astype(jnp.float32)
        summed = jnp.einsum('hqk,khe->qhe', rounded, v_rows)
        attended = summed / jnp.transpose(total)[:, :, None]
        return attended.astype(jnp.bfloat16).reshape(TOK_DEV, width)
    attended = lax.map(block, jnp.arange(N_SEQ).astype(jnp.int32)).reshape(TOKENS, width)
    branch = jnp.zeros((TOKENS, D), jnp.float32)
    for index in range(N_TP):
        term = jnp.dot(attended[:, index * group:(index + 1) * group], w_out[index * group:(index + 1) * group], preferred_element_type=jnp.float32)
        back_cols = w_mlp_back[:, index * mlp_group:(index + 1) * mlp_group]
        term = term + jnp.dot(mlp_act[:, index * mlp_group:(index + 1) * mlp_group], jnp.transpose(back_cols), preferred_element_type=jnp.float32)
        branch = branch + lax.optimization_barrier(term.astype(jnp.bfloat16)).astype(jnp.float32)
    return (xf + gate * branch).astype(jnp.bfloat16)

def reference(hidden, seg_ids, modulation, qk_gain, w_qkv, w_mlp_in, w_out, w_mlp_back):
    cond = half_layer(hidden, seg_ids, modulation[0], qk_gain, w_qkv, w_mlp_in, w_out, w_mlp_back).astype(jnp.float32)
    uncond = half_layer(hidden, seg_ids, modulation[1], qk_gain, w_qkv, w_mlp_in, w_out, w_mlp_back).astype(jnp.float32)
    guided = (uncond + guidance * (cond - uncond)).astype(jnp.bfloat16)
    return guided.reshape(TOKENS, N_TP, 2, D // (2 * N_TP))
```

```python
import jax
import jax.numpy as jnp
from jax import lax
from jax.sharding import PartitionSpec as P

D = 3072
HEAD = 128


guidance = 3.5


def from_partner(block, axis, apart):
    count = lax.axis_size(axis)
    route = []
    for low in range(count):
        high = low | 1 << apart
        if high != low and high < count:
            route += [(low, high), (high, low)]
    return lax.ppermute(block, axis, route)


def head_norm(values, gain):
    return values * lax.rsqrt(jnp.mean(values * values, axis=-1, keepdims=True) + 1e-06) * gain


def on_device(hidden, seg_ids, modulation, qk_gain, w_qkv, w_mlp_in, w_out, w_mlp_back):
    rows = hidden.shape[0]
    local_width = hidden.shape[1]
    group = w_out.shape[0]
    heads_here = group // HEAD
    requests = modulation.shape[1]
    tp_index = lax.axis_index("tp")
    full = lax.all_gather(hidden, "tp", axis=1, tiled=True)
    xf = full.astype(jnp.float32)
    centred = xf - jnp.mean(xf, axis=-1, keepdims=True)
    normed = centred * lax.rsqrt(jnp.mean(centred * centred, axis=-1, keepdims=True) + 1e-06)
    one_hot = (seg_ids[:, None] == lax.iota(jnp.int32, requests)[None, :]).astype(jnp.bfloat16)
    table = modulation[0, :, 0:2, :].reshape(requests, 2 * D)
    looked = jnp.dot(one_hot, table, preferred_element_type=jnp.float32)
    xmod = (normed * (1.0 + looked[:, D:]) + looked[:, :D]).astype(jnp.bfloat16)
    gate_table = lax.dynamic_slice_in_dim(
        modulation[0, :, 2, :], tp_index * local_width, local_width, 1
    )
    gate = jnp.dot(one_hot, gate_table, preferred_element_type=jnp.float32)
    mlp_pre = jnp.dot(
        xmod,
        lax.all_gather(w_mlp_in, "seq", axis=0, tiled=True),
        preferred_element_type=jnp.float32,
    )
    mlp_act = jax.nn.gelu(mlp_pre, approximate=True).astype(jnp.bfloat16)
    proj = jnp.einsum("td,dck->tck", xmod, w_qkv, preferred_element_type=jnp.float32)
    query = head_norm(proj[:, 0].reshape(rows, heads_here, HEAD), qk_gain[0]).astype(jnp.bfloat16)
    key_rows = head_norm(proj[:, 1].reshape(rows, heads_here, HEAD), qk_gain[1]).astype(
        jnp.bfloat16
    )
    value_rows = proj[:, 2].astype(jnp.bfloat16)
    packed = jnp.concatenate([key_rows.reshape(rows, group), value_rows], axis=1)
    seg_plus = seg_ids + 1

    keys_all = lax.all_gather(packed, "seq", axis=0, tiled=True)
    seg_all = lax.all_gather(seg_plus, "seq", axis=0, tiled=True)
    count = keys_all.shape[0]
    keys = keys_all[:, :group].reshape(count, heads_here, HEAD)
    values = keys_all[:, group:].reshape(count, heads_here, HEAD)
    score = jnp.einsum(
        "qhe,khe->hqk", query, keys, preferred_element_type=jnp.float32
    ) * HEAD ** (-0.5)
    score = jnp.where((seg_plus[:, None] == seg_all[None, :])[None], score, -1e30)
    peak = jnp.max(score, axis=-1, keepdims=True)
    weight = jnp.exp(score - peak)
    total = jnp.sum(weight, axis=-1)
    summed = jnp.einsum(
        "hqk,khe->hqe", weight.astype(jnp.bfloat16), values, preferred_element_type=jnp.float32
    )
    attended = (summed / total[:, :, None]).astype(jnp.bfloat16)
    attended = jnp.transpose(attended, (1, 0, 2)).reshape(rows, group)
    mlp_term = lax.dot_general(
        mlp_act,
        lax.all_gather(w_mlp_back, "seq", axis=0, tiled=True),
        (((1,), (1,)), ((), ())),
        preferred_element_type=jnp.float32,
    )
    partial_term = jnp.dot(attended, w_out, preferred_element_type=jnp.float32) + mlp_term
    branch = lax.psum_scatter(
        partial_term.astype(jnp.bfloat16), "tp", scatter_dimension=1, tiled=True
    ).astype(jnp.float32)
    own_half = (hidden.astype(jnp.float32) + gate * branch).astype(jnp.bfloat16)
    split_width = local_width // 2
    guide_index = lax.axis_index("guide")
    kept = lax.dynamic_slice_in_dim(own_half, guide_index * split_width, split_width, 1)
    handed = lax.dynamic_slice_in_dim(own_half, (1 - guide_index) * split_width, split_width, 1)
    other_half = from_partner(handed, "guide", 0)
    is_cond = guide_index == 0
    cond = jnp.where(is_cond, kept, other_half).astype(jnp.float32)
    uncond = jnp.where(is_cond, other_half, kept).astype(jnp.float32)
    guided = (uncond + guidance * (cond - uncond)).astype(jnp.bfloat16)
    return guided.reshape(rows, 1, 1, split_width)


def solution(mesh):
    in_specs = (
        P("seq", "tp"),
        P("seq"),
        P("guide", None, None, None),
        P(),
        P(None, None, "tp"),
        P("seq", "tp"),
        P("tp", None),
        P("seq", "tp"),
    )
    out_specs = P("seq", "tp", "guide", None)
    return jax.shard_map(
        on_device, mesh=mesh, in_specs=in_specs, out_specs=out_specs, check_vma=False
    )
```

```python
import jax
import jax.numpy as jnp
from jax import lax
from jax.experimental import pallas as pl
from jax.experimental.pallas import tpu as pltpu
from jax.sharding import PartitionSpec as P

D = 3072
HEAD = 128
ROWS = 64
WIDE = 768
GROUP = 384
SLAB = 96
HEADS_HERE = 3
REQUESTS = 4
KV = 2 * GROUP + HEAD
GUIDANCE = 3.5
COPIES = 132
LOCALS = 10

F32 = jnp.float32
BF16 = jnp.bfloat16


def dot(a, b):
    return jnp.dot(a, b, preferred_element_type=F32)


def dot_t(a, b):
    return lax.dot_general(a, b, (((1,), (1,)), ((), ())), preferred_element_type=F32)


class Links:
    def __init__(self, send_sems, recv_sems):
        self.send_sems, self.recv_sems = send_sems, recv_sems
        self.used = 0
        self.sent = []

    def copy(self, src, dst, device):
        i = self.used
        self.used += 1
        made = pltpu.make_async_remote_copy(
            src_ref=src,
            dst_ref=dst,
            send_sem=self.send_sems.at[i],
            recv_sem=self.recv_sems.at[i],
            device_id=device,
            device_id_type=pl.DeviceIdType.MESH,
        )
        self.sent.append(made)
        return made

    def drain(self):
        for made in self.sent:
            made.wait_send()


class RingGather:
    def __init__(self, links, right, left, own, at_right, at_left, from_left, from_right, on_right, on_left):
        self.first = [
            links.copy(own(0), at_right(0), right),
            links.copy(own(1), at_left(1), left),
            links.copy(own(1), at_right(1), right),
            links.copy(own(0), at_left(0), left),
        ]
        self.onward = [
            links.copy(from_left(0), on_right(0), right),
            links.copy(from_right(1), on_left(1), left),
        ]

    def start(self):
        for made in self.first:
            made.start()

    def forward(self):
        self.first[0].wait_recv()
        self.onward[0].start()
        self.first[1].wait_recv()
        self.onward[1].start()

    def finish(self):
        self.first[2].wait_recv()
        self.first[3].wait_recv()
        self.onward[0].wait_recv()
        self.onward[1].wait_recv()


def body(
    hidden, seg, modulation, qk_gain, w_qkv, w_in, w_out, w_back,
    result,
    hid, xm, win, wback, relay, kv, wqkv_v, wout_v, mod_v, gain_v, seg_v, q_v, act_v,
    pacc, rs_out, rs_opp, rs_left, rs_right, z_out, z_in, own_out, other_out,
    send_sems, recv_sems, local_sems,
):
    g = lax.axis_index("guide")
    s = lax.axis_index("seq")
    t = lax.axis_index("tp")
    x, y, c = s // 8, (s % 8) // 2, s % 2
    yr, yl, yo = (y + 1) % 4, (y + 3) % 4, (y + 2) % 4

    def at_seq(xx, yy, cc):
        return {"seq": xx * 8 + yy * 2 + cc}

    x_right, x_left = at_seq((x + 1) % 4, y, c), at_seq((x + 3) % 4, y, c)
    y_right, y_left = at_seq(x, yr, c), at_seq(x, yl, c)
    mate = at_seq(x, y, 1 - c)
    t_right, t_left, t_far = {"tp": (t + 1) % 4}, {"tp": (t + 3) % 4}, {"tp": (t + 2) % 4}
    partner = {"guide": 1 - g}

    barrier = pltpu.get_barrier_semaphore()
    everyone = (x_right, x_left, y_right, y_left, mate, t_right, t_left, t_far, partner)
    for device in everyone:
        pl.semaphore_signal(barrier, inc=1, device_id=device, device_id_type=pl.DeviceIdType.MESH)

    pairs = [
        (hidden, hid.at[0]),
        (seg, seg_v),
        (modulation, mod_v),
        (qk_gain, gain_v),
        (w_qkv.at[1], wqkv_v.at[1]),
        (w_qkv.at[2], wqkv_v.at[2]),
        (w_qkv.at[0], wqkv_v.at[0]),
        (w_out, wout_v),
        (w_in.at[:, pl.ds(pl.multiple_of(x * GROUP, GROUP), GROUP)], win.at[0, y, c]),
        (w_back.at[:, pl.ds(pl.multiple_of(x * GROUP, GROUP), GROUP)], wback.at[0, y, c]),
    ]
    local = [pltpu.make_async_copy(a, b, local_sems.at[i]) for i, (a, b) in enumerate(pairs)]
    for made in local:
        made.start()
    pl.semaphore_wait(barrier, len(everyone))

    links = Links(send_sems, recv_sems)

    half32 = lambda h: pl.ds(h * 32, 32)
    half48 = lambda h: pl.ds(h * 48, 48)

    def x_gather(buffer, own=None):
        spot = lambda d: (lambda h: buffer.at[d, half32(h)])
        return RingGather(
            links, x_right, x_left, own or spot(0), spot(3), spot(1), spot(3), spot(1), spot(2), spot(2)
        )

    tp_spot = lambda d: (lambda h: hid.at[d, half32(h)])
    hid_gather = RingGather(
        links, t_right, t_left, lambda h: hidden.at[half32(h)], tp_spot(3), tp_spot(1), tp_spot(3), tp_spot(1),
        tp_spot(2), tp_spot(2),
    )

    def y_gather(buffer, low, high, half, own=None):
        spot = lambda yy: (lambda h: buffer.at[low:high, yy, c, half(h)])
        return RingGather(
            links, y_right, y_left, own or spot(y), spot(y), spot(y), spot(yl), spot(yr), spot(yl), spot(yr)
        )

    def columns(weight, dx, h=None):
        cols = pl.ds(pl.multiple_of(((x + dx) % 4) * GROUP, GROUP), GROUP)
        return weight.at[:, cols] if h is None else weight.at[half48(h), cols]

    class Weights:
        def __init__(self, source, buffer, which):
            self.to_right = links.copy(columns(source, 1), buffer.at[3, y, c], x_right)
            self.to_left = links.copy(columns(source, 3), buffer.at[1, y, c], x_left)
            self.far = [
                links.copy(columns(source, 2, 0), relay.at[which, 0], x_right),
                links.copy(columns(source, 2, 1), relay.at[which, 1], x_left),
            ]
            self.onward = [
                links.copy(relay.at[which, 0], buffer.at[2, y, c, half48(0)], x_right),
                links.copy(relay.at[which, 1], buffer.at[2, y, c, half48(1)], x_left),
            ]
            self.near = y_gather(buffer, 0, 1, half48)
            self.rest = y_gather(buffer, 1, 4, half48)
            self.over = [
                links.copy(buffer.at[0:1, :, c], buffer.at[0:1, :, c], mate),
                links.copy(buffer.at[1:4, :, c], buffer.at[1:4, :, c], mate),
            ]

        def start(self):
            for made in self.far:
                made.start()
            self.to_right.start()
            self.to_left.start()

        def relay(self):
            for arrived, onward in zip(self.far, self.onward):
                arrived.wait_recv()
                onward.start()

        def second(self):
            self.to_right.wait_recv()
            self.to_left.wait_recv()
            for made in self.onward:
                made.wait_recv()
            self.rest.start()

    weights_in = Weights(w_in, win, 0)
    weights_back = Weights(w_back, wback, 1)
    xm_gather = x_gather(xm)
    kv_x = RingGather(
        links, x_right, x_left, *[
            (lambda d: (lambda h: kv.at[d, y, c, half32(h)]))(d) for d in (0, 3, 1, 3, 1, 2, 2)
        ]
    )
    kv_near = y_gather(kv, 0, 1, half32)
    kv_rest = y_gather(kv, 1, 4, half32)
    kv_over = [
        links.copy(kv.at[0:1, :, c], kv.at[0:1, :, c], mate),
        links.copy(kv.at[1:4, :, c], kv.at[1:4, :, c], mate),
    ]

    hid_gather.start()
    weights_in.start()
    local[8].wait()
    weights_in.near.start()
    weights_back.start()
    local[9].wait()
    weights_back.near.start()

    for made in local[:4]:
        made.wait()
    hid_gather.forward()
    weights_in.relay()
    weights_in.near.forward()
    weights_in.second()
    hid_gather.finish()

    seg_row = jnp.broadcast_to(seg_v[...].astype(F32), (ROWS, ROWS))
    at_row = lax.broadcasted_iota(jnp.int32, (ROWS, ROWS), 0)
    at_col = lax.broadcasted_iota(jnp.int32, (ROWS, ROWS), 1)
    seg_col = jnp.sum(jnp.where(at_row == at_col, seg_row, 0.0), axis=-1, keepdims=True)

    def look_up(kind, offset):
        table = mod_v[kind, :, pl.ds(pl.multiple_of(offset, WIDE), WIDE)].astype(F32)
        found = jnp.broadcast_to(table[0:1], (ROWS, WIDE))
        for r in range(1, REQUESTS):
            found = jnp.where(seg_col == float(r), table[r : r + 1], found)
        return found

    total = sum(jnp.sum(hid[d].astype(F32), axis=-1, keepdims=True) for d in range(4))
    mean = total * (1.0 / D)
    squares = jnp.zeros((ROWS, 1), F32)
    for d in range(4):
        centred = hid[d].astype(F32) - mean
        squares += jnp.sum(centred * centred, axis=-1, keepdims=True)
    scale_rows = lax.rsqrt(squares * (1.0 / D) + 1e-06)
    for d in range(4):
        offset = ((t + d) % 4) * WIDE
        normed = (hid[d].astype(F32) - mean) * scale_rows
        xm[0, :, pl.ds(pl.multiple_of(offset, WIDE), WIDE)] = (
            normed * (1.0 + look_up(1, offset)) + look_up(0, offset)
        ).astype(BF16)
    xm_gather.start()

    weights_back.relay()
    weights_back.near.forward()
    weights_back.second()

    def head_norm(values, gain):
        return values * lax.rsqrt(jnp.mean(values * values, axis=-1, keepdims=True) + 1e-06) * gain

    rows_own = xm[0]
    local[4].wait()
    keys = dot(rows_own, wqkv_v[1])
    for h in range(HEADS_HERE):
        cols = slice(h * HEAD, (h + 1) * HEAD)
        kv[0, y, c, :, cols] = head_norm(keys[:, cols], gain_v[1:2, :]).astype(BF16)
    local[5].wait()
    kv[0, y, c, :, GROUP : 2 * GROUP] = dot(rows_own, wqkv_v[2]).astype(BF16)
    lane = lax.broadcasted_iota(jnp.int32, (ROWS, HEAD), 1).astype(F32)
    one_hot = jnp.where(seg_col == lane, 1.0, 0.0).astype(BF16)
    kv[0, y, c, :, 2 * GROUP :] = one_hot
    kv_x.start()
    kv_near.start()

    weights_in.rest.forward()
    weights_in.near.finish()
    weights_in.over[0].start()

    local[6].wait()
    query = dot(rows_own, wqkv_v[0])
    for h in range(HEADS_HERE):
        cols = slice(h * HEAD, (h + 1) * HEAD)
        q_v[:, cols] = head_norm(query[:, cols], gain_v[0:1, :]).astype(BF16)

    weights_back.near.finish()
    weights_back.over[0].start()
    weights_back.rest.forward()
    weights_in.rest.finish()
    weights_in.over[1].start()
    xm_gather.forward()
    kv_x.forward()
    kv_near.forward()
    kv_x.finish()
    kv_rest.start()
    weights_back.rest.finish()
    weights_back.over[1].start()
    xm_gather.finish()
    for made in weights_in.over:
        made.wait_recv()

    pre = jnp.zeros((4 * ROWS, GROUP), F32)
    for d in range(4):
        cols = pl.ds(pl.multiple_of(((x + d) % 4) * WIDE, WIDE), WIDE)
        pre += dot(xm[:, :, cols].reshape(4 * ROWS, WIDE), win[d].reshape(WIDE, GROUP))
    act_v[...] = jax.nn.gelu(pre, approximate=True).astype(BF16)

    kv_near.finish()
    kv_over[0].start()
    for made in weights_back.over:
        made.wait_recv()

    low, high = slice(0, GROUP), slice(GROUP, WIDE)
    chunks = []
    for k, step in enumerate((2, 1, 3, 0)):
        e = (t + step) % 4
        part = dot_t(act_v[...], wback[(e - x + 4) % 4].reshape(WIDE, GROUP))
        pacc[k] = part.reshape(4, ROWS, WIDE)
        rs_out[k, 0] = part[2 * ROWS : 3 * ROWS, low].astype(BF16)
        rs_out[k, 1] = part[2 * ROWS : 3 * ROWS, high].astype(BF16)
        rs_out[k, 2] = part[ROWS : 2 * ROWS, high].astype(BF16)
        rs_out[k, 3] = part[3 * ROWS :, low].astype(BF16)
        first = [
            links.copy(rs_out.at[k, 0], rs_opp.at[k, 0], x_right),
            links.copy(rs_out.at[k, 1], rs_opp.at[k, 1], x_left),
            links.copy(rs_out.at[k, 2], rs_left.at[k, 1], x_right),
            links.copy(rs_out.at[k, 3], rs_right.at[k, 0], x_left),
        ]
        second = [
            links.copy(rs_out.at[k, 4], rs_left.at[k, 0], x_right),
            links.copy(rs_out.at[k, 5], rs_right.at[k, 1], x_left),
        ]
        chunks.append((first, second))
        for made in first:
            made.start()

    def merge(k):
        first, second = chunks[k]
        first[0].wait_recv()
        rs_out[k, 4] = (pacc[k, 1, :, low] + rs_opp[k, 0].astype(F32)).astype(BF16)
        second[0].start()
        first[1].wait_recv()
        rs_out[k, 5] = (pacc[k, 3, :, high] + rs_opp[k, 1].astype(F32)).astype(BF16)
        second[1].start()

    kv_rest.forward()
    merge(0)
    merge(1)
    kv_rest.finish()
    kv_over[1].start()
    merge(2)
    merge(3)
    for made in kv_over:
        made.wait_recv()

    everything = kv.reshape(32 * ROWS, KV)
    same = dot_t(one_hot, everything[:, 2 * GROUP :]) > 0.5
    attended = []
    for h in range(HEADS_HERE):
        k_cols = slice(h * HEAD, (h + 1) * HEAD)
        v_cols = slice(GROUP + h * HEAD, GROUP + (h + 1) * HEAD)
        score = dot_t(q_v[:, k_cols], everything[:, k_cols]) * HEAD ** (-0.5)
        score = jnp.where(same, score, -1e30)
        weight = jnp.exp(score - jnp.max(score, axis=-1, keepdims=True))
        summed = dot(weight.astype(BF16), everything[:, v_cols])
        attended.append((summed / jnp.sum(weight, axis=-1, keepdims=True)).astype(BF16))
    attended = jnp.concatenate(attended, axis=1)
    local[7].wait()

    branch = jnp.zeros((ROWS, WIDE), F32)
    sends = []
    for k, step in enumerate((2, 1, 3, 0)):
        e = (t + step) % 4
        term = dot(attended, wout_v[:, pl.ds(pl.multiple_of(e * WIDE, WIDE), WIDE)])
        first, second = chunks[k]
        first[2].wait_recv()
        first[3].wait_recv()
        second[0].wait_recv()
        second[1].wait_recv()
        mlp_low = pacc[k, 0, :, low] + rs_left[k, 0].astype(F32) + rs_right[k, 0].astype(F32)
        mlp_high = pacc[k, 0, :, high] + rs_left[k, 1].astype(F32) + rs_right[k, 1].astype(F32)
        term = (term + jnp.concatenate([mlp_low, mlp_high], axis=1)).astype(BF16)
        if k < 3:
            z_out[k] = term
            made = links.copy(z_out.at[k], z_in.at[k], (t_far, t_right, t_left)[k])
            made.start()
            sends.append(made)
        else:
            branch = term.astype(F32)
    gate = look_up(2, t * WIDE)
    for k, made in enumerate(sends):
        made.wait_recv()
        branch += z_in[k].astype(F32)
    own_out[...] = (hid[0].astype(F32) + gate * branch).astype(BF16)
    kept_cols = pl.ds(pl.multiple_of(g * GROUP, GROUP), GROUP)
    handed_cols = pl.ds(pl.multiple_of((1 - g) * GROUP, GROUP), GROUP)
    swap = links.copy(own_out.at[:, handed_cols], other_out, partner)
    swap.start()
    kept = own_out[:, kept_cols].astype(F32)
    swap.wait_recv()
    other = other_out[...].astype(F32)
    cond = jnp.where(g == 0, kept, other)
    uncond = jnp.where(g == 0, other, kept)
    result[...] = (uncond + GUIDANCE * (cond - uncond)).astype(BF16)
    links.drain()


def on_device(hidden, seg_ids, modulation, qk_gain, w_qkv, w_mlp_in, w_out, w_mlp_back):
    anywhere = pl.BlockSpec(memory_space=pl.ANY)
    guided = pl.pallas_call(
        body,
        out_shape=jax.ShapeDtypeStruct((ROWS, GROUP), BF16),
        in_specs=[anywhere] * 8,
        out_specs=pl.BlockSpec(memory_space=pltpu.VMEM),
        scratch_shapes=[
            pltpu.VMEM((4, ROWS, WIDE), BF16),
            pltpu.VMEM((4, ROWS, D), BF16),
            pltpu.VMEM((4, 4, 2, SLAB, GROUP), BF16),
            pltpu.VMEM((4, 4, 2, SLAB, GROUP), BF16),
            pltpu.VMEM((2, 2, SLAB // 2, GROUP), BF16),
            pltpu.VMEM((4, 4, 2, ROWS, KV), BF16),
            pltpu.VMEM((3, D, GROUP), BF16),
            pltpu.VMEM((GROUP, D), BF16),
            pltpu.VMEM((3, REQUESTS, D), BF16),
            pltpu.VMEM((2, HEAD), F32),
            pltpu.VMEM((1, ROWS), jnp.int32),
            pltpu.VMEM((ROWS, GROUP), BF16),
            pltpu.VMEM((4 * ROWS, GROUP), BF16),
            pltpu.VMEM((4, 4, ROWS, WIDE), F32),
            pltpu.VMEM((4, 6, ROWS, GROUP), BF16),
            pltpu.VMEM((4, 2, ROWS, GROUP), BF16),
            pltpu.VMEM((4, 2, ROWS, GROUP), BF16),
            pltpu.VMEM((4, 2, ROWS, GROUP), BF16),
            pltpu.VMEM((3, ROWS, WIDE), BF16),
            pltpu.VMEM((3, ROWS, WIDE), BF16),
            pltpu.VMEM((ROWS, WIDE), BF16),
            pltpu.VMEM((ROWS, GROUP), BF16),
            pltpu.SemaphoreType.DMA((COPIES,)),
            pltpu.SemaphoreType.DMA((COPIES,)),
            pltpu.SemaphoreType.DMA((LOCALS,)),
        ],
        compiler_params=pltpu.CompilerParams(
            collective_id=0, has_side_effects=True, vmem_limit_bytes=60 * 1024 * 1024
        ),
        name="layer",
    )(
        hidden,
        seg_ids.reshape(1, ROWS),
        jnp.transpose(modulation[0], (1, 0, 2)),
        qk_gain,
        jnp.transpose(w_qkv, (1, 0, 2)),
        w_mlp_in,
        w_out,
        w_mlp_back,
    )
    return guided.reshape(ROWS, 1, 1, GROUP)


def solution(mesh):
    in_specs = (
        P("seq", "tp"),
        P("seq"),
        P("guide", None, None, None),
        P(),
        P(None, None, "tp"),
        P("seq", "tp"),
        P("tp", None),
        P("seq", "tp"),
    )
    out_specs = P("seq", "tp", "guide", None)
    return jax.shard_map(
        on_device, mesh=mesh, in_specs=in_specs, out_specs=out_specs, check_vma=False
    )
```

```python
import jax
import jax.numpy as jnp
from jax import lax
from jax.experimental import pallas as pl
from jax.experimental.pallas import tpu as pltpu
from jax.sharding import PartitionSpec as P

D = 3072
HEAD = 128
ROWS = 64
WIDE = 768
GROUP = 384
SLAB = 96
HEADS_HERE = 3
REQUESTS = 4
KV = 2 * GROUP + HEAD
GUIDANCE = 3.5
COPIES = 96
LOCALS = 10

F32 = jnp.float32
BF16 = jnp.bfloat16


def dot(a, b):
    return jnp.dot(a, b, preferred_element_type=F32)


def dot_t(a, b):
    return lax.dot_general(a, b, (((1,), (1,)), ((), ())), preferred_element_type=F32)


class Links:
    def __init__(self, send_sems, recv_sems):
        self.send_sems, self.recv_sems = send_sems, recv_sems
        self.used = 0
        self.sent = []

    def copy(self, src, dst, device):
        i = self.used
        self.used += 1
        made = pltpu.make_async_remote_copy(
            src_ref=src,
            dst_ref=dst,
            send_sem=self.send_sems.at[i],
            recv_sem=self.recv_sems.at[i],
            device_id=device,
            device_id_type=pl.DeviceIdType.MESH,
        )
        self.sent.append(made)
        return made

    def drain(self):
        for made in self.sent:
            made.wait_send()


class RingGather:
    def __init__(self, links, right, left, own, at_right, at_left, from_left, from_right, on_right, on_left):
        self.first = [
            links.copy(own(0), at_right(0), right),
            links.copy(own(1), at_left(1), left),
            links.copy(own(1), at_right(1), right),
            links.copy(own(0), at_left(0), left),
        ]
        self.onward = [
            links.copy(from_left(0), on_right(0), right),
            links.copy(from_right(1), on_left(1), left),
        ]

    def start(self):
        for made in self.first:
            made.start()

    def forward(self):
        self.first[0].wait_recv()
        self.onward[0].start()
        self.first[1].wait_recv()
        self.onward[1].start()

    def near(self):
        self.first[2].wait_recv()
        self.first[3].wait_recv()

    def far(self):
        self.onward[0].wait_recv()
        self.onward[1].wait_recv()

    def finish(self):
        self.near()
        self.far()


def body(
    hidden, seg, modulation, qk_gain, w_qkv, w_in, w_out, w_back,
    result,
    raw, xm, win, wback, kv, wqkv_v, wout_v, mod_v, gain_v, seg_x, qx, peak_v, part_out, part_in,
    act, mlp_out, mlp_in, z_out, z_in, own_out, other_out,
    send_sems, recv_sems, local_sems,
):
    g = lax.axis_index("guide")
    s = lax.axis_index("seq")
    t = lax.axis_index("tp")
    x, y, c = s // 8, (s % 8) // 2, s % 2
    yr, yl = (y + 1) % 4, (y + 3) % 4

    def at_seq(xx, yy, cc):
        return {"seq": xx * 8 + yy * 2 + cc}

    x_right, x_left, x_far = at_seq((x + 1) % 4, y, c), at_seq((x + 3) % 4, y, c), at_seq((x + 2) % 4, y, c)
    y_right, y_left = at_seq(x, yr, c), at_seq(x, yl, c)
    mate = at_seq(x, y, 1 - c)
    t_right, t_left, t_far = {"tp": (t + 1) % 4}, {"tp": (t + 3) % 4}, {"tp": (t + 2) % 4}
    partner = {"guide": 1 - g}

    barrier = pltpu.get_barrier_semaphore()
    everyone = (x_right, x_left, x_far, y_right, y_left, mate, t_right, t_left, t_far, partner)
    for device in everyone:
        pl.semaphore_signal(barrier, inc=1, device_id=device, device_id_type=pl.DeviceIdType.MESH)

    def columns(weight, dx, h=None):
        cols = pl.ds(pl.multiple_of(((x + dx) % 4) * GROUP, GROUP), GROUP)
        return weight.at[:, cols] if h is None else weight.at[pl.ds(h * 48, 48), cols]

    pairs = [
        (hidden, raw.at[0, 0]),
        (seg, seg_x.at[0]),
        (modulation, mod_v),
        (qk_gain, gain_v),
        (w_qkv.at[1], wqkv_v.at[1]),
        (w_qkv.at[2], wqkv_v.at[2]),
        (w_qkv.at[0], wqkv_v.at[0]),
        (columns(w_in, 0), win.at[0, y, c]),
        (w_back, wback.at[y, c]),
        (w_out, wout_v),
    ]
    local = [pltpu.make_async_copy(a, b, local_sems.at[i]) for i, (a, b) in enumerate(pairs)]
    for made in local:
        made.start()
    pl.semaphore_wait(barrier, len(everyone))

    links = Links(send_sems, recv_sems)
    half32 = lambda h: pl.ds(h * 32, 32)
    half48 = lambda h: pl.ds(h * 48, 48)
    two = lambda h: pl.ds(h * 2, 2)

    def relative(right, left, spot, own=None):
        spots = [(lambda d: (lambda h: spot(d, h)))(d) for d in (3, 1, 3, 1, 2, 2)]
        return RingGather(links, right, left, own or (lambda h: spot(0, h)), *spots)

    def absolute(spot, own=None):
        spots = [(lambda yy: (lambda h: spot(yy, h)))(yy) for yy in (y, y, yl, yr, yl, yr)]
        return RingGather(links, y_right, y_left, own or (lambda h: spot(y, h)), *spots)

    over_tp = relative(t_right, t_left, lambda d, h: raw.at[0, d, half32(h)], lambda h: hidden.at[half32(h)])
    over_x = [
        relative(
            x_right, x_left, (lambda k: (lambda d, h: raw.at[d, k, half32(h)]))(k),
            (lambda h: hidden.at[half32(h)]) if k == 0 else None,
        )
        for k in range(4)
    ]
    seg_sent = [
        links.copy(seg, seg_x.at[3], x_right),
        links.copy(seg, seg_x.at[1], x_left),
        links.copy(seg, seg_x.at[2], x_far),
    ]
    win_sent = [
        links.copy(columns(w_in, 2), win.at[2, y, c], x_far),
        links.copy(columns(w_in, 1), win.at[3, y, c], x_right),
        links.copy(columns(w_in, 3), win.at[1, y, c], x_left),
    ]
    win_near = absolute(lambda yy, h: win.at[0, yy, c, half48(h)], lambda h: columns(w_in, 0, h))
    win_rest = absolute(lambda yy, h: win.at[1:4, yy, c, half48(h)])
    wback_all = absolute(lambda yy, h: wback.at[yy, c, half48(h)], lambda h: w_back.at[half48(h)])
    win_over = [
        links.copy(win.at[0:1, :, c], win.at[0:1, :, c], mate),
        links.copy(win.at[1:4, :, c], win.at[1:4, :, c], mate),
    ]
    wback_over = links.copy(wback.at[:, c], wback.at[:, c], mate)
    kv_all = absolute(lambda yy, h: kv.at[yy, c, half32(h)])
    kv_over = links.copy(kv.at[:, c], kv.at[:, c], mate)
    q_all = relative(x_right, x_left, lambda d, h: qx.at[d, half32(h)])
    act_all = relative(x_right, x_left, lambda d, h: act.at[d, two(h)])

    over_tp.start()
    over_x[0].start()
    for made in seg_sent + win_sent:
        made.start()
    win_near.start()
    wback_all.start()

    over_tp.forward()
    over_tp.near()
    over_x[3].start()
    over_x[1].start()
    over_x[0].forward()
    win_near.forward()
    for made in win_sent:
        made.wait_recv()
    win_rest.start()
    for made in local[:4]:
        made.wait()
    for made in seg_sent:
        made.wait_recv()
    over_tp.far()
    over_x[2].start()

    at_row = lax.broadcasted_iota(jnp.int32, (ROWS, ROWS), 0)
    at_col = lax.broadcasted_iota(jnp.int32, (ROWS, ROWS), 1)
    lane = lax.broadcasted_iota(jnp.int32, (ROWS, HEAD), 1).astype(F32)

    def seg_column(d):
        row = jnp.broadcast_to(seg_x[d].astype(F32), (ROWS, ROWS))
        return jnp.sum(jnp.where(at_row == at_col, row, 0.0), axis=-1, keepdims=True)

    seg_cols = [seg_column(d) for d in range(4)]
    one_hots = [jnp.where(seg_cols[d] == lane, 1.0, 0.0).astype(BF16) for d in range(4)]

    def look_up(kind, offset, d):
        table = mod_v[kind, :, pl.ds(pl.multiple_of(offset, WIDE), WIDE)].astype(F32)
        found = jnp.broadcast_to(table[0:1], (ROWS, WIDE))
        for r in range(1, REQUESTS):
            found = jnp.where(seg_cols[d] == float(r), table[r : r + 1], found)
        return found

    def normalise(d):
        total = sum(jnp.sum(raw[d, k].astype(F32), axis=-1, keepdims=True) for k in range(4))
        mean = total * (1.0 / D)
        squares = jnp.zeros((ROWS, 1), F32)
        for k in range(4):
            centred = raw[d, k].astype(F32) - mean
            squares += jnp.sum(centred * centred, axis=-1, keepdims=True)
        scale_rows = lax.rsqrt(squares * (1.0 / D) + 1e-06)
        for k in range(4):
            offset = ((t + k) % 4) * WIDE
            normed = (raw[d, k].astype(F32) - mean) * scale_rows
            xm[d, :, pl.ds(pl.multiple_of(offset, WIDE), WIDE)] = (
                normed * (1.0 + look_up(1, offset, d)) + look_up(0, offset, d)
            ).astype(BF16)

    normalise(0)
    over_x[3].forward()
    over_x[1].forward()

    def head_norm(values, gain):
        return values * lax.rsqrt(jnp.mean(values * values, axis=-1, keepdims=True) + 1e-06) * gain

    rows_own = xm[0]
    local[4].wait()
    keys = dot(rows_own, wqkv_v[1])
    for h in range(HEADS_HERE):
        cols = slice(h * HEAD, (h + 1) * HEAD)
        kv[y, c, :, cols] = head_norm(keys[:, cols], gain_v[1:2, :]).astype(BF16)
    win_rest.forward()
    wback_all.forward()
    local[5].wait()
    kv[y, c, :, GROUP : 2 * GROUP] = dot(rows_own, wqkv_v[2]).astype(BF16)
    kv[y, c, :, 2 * GROUP :] = one_hots[0]
    kv_all.start()
    over_x[2].forward()
    local[6].wait()
    query = dot(rows_own, wqkv_v[0])
    for h in range(HEADS_HERE):
        cols = slice(h * HEAD, (h + 1) * HEAD)
        qx[0, :, cols] = head_norm(query[:, cols], gain_v[0:1, :]).astype(BF16)
    q_all.start()

    local[7].wait()
    win_near.finish()
    win_over[0].start()
    win_rest.finish()
    win_over[1].start()
    over_x[0].finish()
    over_x[1].finish()
    over_x[3].finish()
    over_x[2].finish()
    normalise(1)
    kv_all.forward()
    normalise(3)
    q_all.forward()
    normalise(2)
    for made in win_over:
        made.wait_recv()

    pre = jnp.zeros((4 * ROWS, GROUP), F32)
    for d in range(4):
        cols = pl.ds(pl.multiple_of(((x + d) % 4) * WIDE, WIDE), WIDE)
        pre += dot(xm[:, :, cols].reshape(4 * ROWS, WIDE), win[d].reshape(WIDE, GROUP))
    acted = jax.nn.gelu(pre, approximate=True).astype(BF16)
    for d in range(4):
        act[0, (x + d) % 4] = acted[d * ROWS : (d + 1) * ROWS]
    act_all.start()

    local[8].wait()
    wback_all.finish()
    wback_over.start()
    kv_all.finish()
    kv_over.start()
    q_all.finish()
    kv_over.wait_recv()

    seen = kv.reshape(8 * ROWS, KV)
    same = dot_t(jnp.concatenate(one_hots, axis=0), seen[:, 2 * GROUP :]) > 0.5
    lanes = lax.broadcasted_iota(jnp.int32, (4 * ROWS, HEAD), 1)
    stats = jnp.zeros((4 * ROWS, HEAD), F32)
    for h in range(HEADS_HERE):
        k_cols = slice(h * HEAD, (h + 1) * HEAD)
        v_cols = slice(GROUP + h * HEAD, GROUP + (h + 1) * HEAD)
        score = dot_t(qx[:, :, k_cols].reshape(4 * ROWS, HEAD), seen[:, k_cols]) * HEAD ** (-0.5)
        score = jnp.where(same, score, -1e30)
        peak_v[...] = jnp.broadcast_to(jnp.max(score, axis=-1, keepdims=True), (4 * ROWS, HEAD)).astype(BF16)
        peak = peak_v[:, 0:1].astype(F32)
        weight = jnp.where(same, jnp.exp(score - peak), 0.0)
        total = jnp.sum(weight, axis=-1, keepdims=True)
        summed = dot(weight.astype(BF16), seen[:, v_cols])
        part = (summed / jnp.where(total > 0.0, total, 1.0)).astype(BF16)
        part_out[:, :, k_cols] = part.reshape(4, ROWS, HEAD)
        upper = total.astype(BF16).astype(F32)
        stats = jnp.where(lanes == h, peak, stats)
        stats = jnp.where(lanes == 3 + h, upper, stats)
        stats = jnp.where(lanes == 6 + h, total - upper, stats)
        if h == 0:
            act_all.forward()
    part_out[:, :, GROUP:] = stats.astype(BF16).reshape(4, ROWS, HEAD)
    part_sent = [
        links.copy(part_out.at[2], part_in.at[2], x_far),
        links.copy(part_out.at[1], part_in.at[3], x_right),
        links.copy(part_out.at[3], part_in.at[1], x_left),
    ]
    for made in part_sent:
        made.start()
    wback_over.wait_recv()

    def back(d):
        cols = pl.ds(pl.multiple_of(((x + d) % 4) * GROUP, GROUP), GROUP)
        return dot_t(act[d].reshape(4 * ROWS, GROUP), wback[:, :, :, cols].reshape(WIDE, GROUP))

    fed = back(0)
    act_all.near()
    fed += back(1)
    fed += back(3)
    act_all.far()
    fed += back(2)
    for b in range(4):
        mlp_out[(b - x + 4) % 4] = fed[b * ROWS : (b + 1) * ROWS].astype(BF16)
    mlp_sent = {
        2: links.copy(mlp_out.at[2], mlp_in.at[2], x_far),
        3: links.copy(mlp_out.at[1], mlp_in.at[3], x_right),
        1: links.copy(mlp_out.at[3], mlp_in.at[1], x_left),
    }
    for made in mlp_sent.values():
        made.start()

    for made in part_sent:
        made.wait_recv()
    attended = []
    for h in range(HEADS_HERE):
        cols = slice(h * HEAD, (h + 1) * HEAD)
        parts = [part_out[0]] + [part_in[d] for d in (1, 2, 3)]
        stat = [p[:, GROUP:].astype(F32) for p in parts]
        top = stat[0][:, h : h + 1]
        for other in stat[1:]:
            top = jnp.maximum(top, other[:, h : h + 1])
        total = jnp.zeros((ROWS, 1), F32)
        summed = jnp.zeros((ROWS, HEAD), F32)
        for p, st in zip(parts, stat):
            share = jnp.exp(st[:, h : h + 1] - top) * (st[:, 3 + h : 4 + h] + st[:, 6 + h : 7 + h])
            total += share
            summed += share * p[:, cols].astype(F32)
        attended.append((summed / total).astype(BF16))
    attended = jnp.concatenate(attended, axis=1)
    local[9].wait()

    steps = [
        links.copy(z_out.at[0], z_in.at[step - 1], {"tp": (t + step) % 4}) for step in (1, 2, 3)
    ]
    first_sem = links.used - 3
    for d in (0, 1, 3, 2):
        e = (x + d) % 4
        term = dot(attended, wout_v[:, pl.ds(pl.multiple_of(e * WIDE, WIDE), WIDE)])
        if d == 0:
            term += mlp_out[0].astype(F32)
        else:
            mlp_sent[d].wait_recv()
            term += mlp_in[d].astype(F32)
        z_out[d] = term.astype(BF16)
        for step in (1, 2, 3):

            @pl.when((e - t + 4) % 4 == step)
            def _():
                pltpu.make_async_remote_copy(
                    src_ref=z_out.at[d],
                    dst_ref=z_in.at[step - 1],
                    send_sem=send_sems.at[first_sem + step - 1],
                    recv_sem=recv_sems.at[first_sem + step - 1],
                    device_id={"tp": (t + step) % 4},
                    device_id_type=pl.DeviceIdType.MESH,
                ).start()

    gate = look_up(2, t * WIDE, 0)
    branch = z_out[(t - x + 4) % 4].astype(F32)
    for k, made in enumerate(steps):
        made.wait_recv()
        branch += z_in[k].astype(F32)
    own_out[...] = (raw[0, 0].astype(F32) + gate * branch).astype(BF16)
    kept_cols = pl.ds(pl.multiple_of(g * GROUP, GROUP), GROUP)
    handed_cols = pl.ds(pl.multiple_of((1 - g) * GROUP, GROUP), GROUP)
    swap = links.copy(own_out.at[:, handed_cols], other_out, partner)
    swap.start()
    kept = own_out[:, kept_cols].astype(F32)
    swap.wait_recv()
    other = other_out[...].astype(F32)
    cond = jnp.where(g == 0, kept, other)
    uncond = jnp.where(g == 0, other, kept)
    result[...] = (uncond + GUIDANCE * (cond - uncond)).astype(BF16)
    links.drain()


def on_device(hidden, seg_ids, modulation, qk_gain, w_qkv, w_mlp_in, w_out, w_mlp_back):
    anywhere = pl.BlockSpec(memory_space=pl.ANY)
    guided = pl.pallas_call(
        body,
        out_shape=jax.ShapeDtypeStruct((ROWS, GROUP), BF16),
        in_specs=[anywhere] * 8,
        out_specs=pl.BlockSpec(memory_space=pltpu.VMEM),
        scratch_shapes=[
            pltpu.VMEM((4, 4, ROWS, WIDE), BF16),
            pltpu.VMEM((4, ROWS, D), BF16),
            pltpu.VMEM((4, 4, 2, SLAB, GROUP), BF16),
            pltpu.VMEM((4, 2, SLAB, 4 * GROUP), BF16),
            pltpu.VMEM((4, 2, ROWS, KV), BF16),
            pltpu.VMEM((3, D, GROUP), BF16),
            pltpu.VMEM((GROUP, D), BF16),
            pltpu.VMEM((3, REQUESTS, D), BF16),
            pltpu.VMEM((2, HEAD), F32),
            pltpu.VMEM((4, 1, ROWS), jnp.int32),
            pltpu.VMEM((4, ROWS, GROUP), BF16),
            pltpu.VMEM((4 * ROWS, HEAD), BF16),
            pltpu.VMEM((4, ROWS, GROUP + HEAD), BF16),
            pltpu.VMEM((4, ROWS, GROUP + HEAD), BF16),
            pltpu.VMEM((4, 4, ROWS, GROUP), BF16),
            pltpu.VMEM((4, ROWS, WIDE), BF16),
            pltpu.VMEM((4, ROWS, WIDE), BF16),
            pltpu.VMEM((4, ROWS, WIDE), BF16),
            pltpu.VMEM((3, ROWS, WIDE), BF16),
            pltpu.VMEM((ROWS, WIDE), BF16),
            pltpu.VMEM((ROWS, GROUP), BF16),
            pltpu.SemaphoreType.DMA((COPIES,)),
            pltpu.SemaphoreType.DMA((COPIES,)),
            pltpu.SemaphoreType.DMA((LOCALS,)),
        ],
        compiler_params=pltpu.CompilerParams(
            collective_id=0, has_side_effects=True, vmem_limit_bytes=60 * 1024 * 1024
        ),
        name="layer",
    )(
        hidden,
        seg_ids.reshape(1, ROWS),
        jnp.transpose(modulation[0], (1, 0, 2)),
        qk_gain,
        jnp.transpose(w_qkv, (1, 0, 2)),
        w_mlp_in,
        w_out,
        w_mlp_back,
    )
    return guided.reshape(ROWS, 1, 1, GROUP)


def solution(mesh):
    in_specs = (
        P("seq", "tp"),
        P("seq"),
        P("guide", None, None, None),
        P(),
        P(None, None, "tp"),
        P("seq", "tp"),
        P("tp", None),
        P("seq", "tp"),
    )
    out_specs = P("seq", "tp", "guide", None)
    return jax.shard_map(
        on_device, mesh=mesh, in_specs=in_specs, out_specs=out_specs, check_vma=False
    )
```

```python
import jax
import jax.numpy as jnp
from jax import lax
from jax.experimental import pallas as pl
from jax.experimental.pallas import tpu as pltpu
from jax.sharding import PartitionSpec as P

D = 3072
HEAD = 128
ROWS = 64
WIDE = 768
GROUP = 384
SLAB = 96
HEADS_HERE = 3
REQUESTS = 4
KV = 2 * GROUP + HEAD
GUIDANCE = 3.5
COPIES = 96
LOCALS = 10

F32 = jnp.float32
BF16 = jnp.bfloat16


def dot(a, b):
    return jnp.dot(a, b, preferred_element_type=F32)


def dot_t(a, b):
    return lax.dot_general(a, b, (((1,), (1,)), ((), ())), preferred_element_type=F32)


class Links:
    def __init__(self, send_sems, recv_sems):
        self.send_sems, self.recv_sems = send_sems, recv_sems
        self.used = 0
        self.sent = []

    def copy(self, src, dst, device):
        i = self.used
        self.used += 1
        made = pltpu.make_async_remote_copy(
            src_ref=src,
            dst_ref=dst,
            send_sem=self.send_sems.at[i],
            recv_sem=self.recv_sems.at[i],
            device_id=device,
            device_id_type=pl.DeviceIdType.MESH,
        )
        self.sent.append(made)
        return made

    def drain(self):
        for made in self.sent:
            made.wait_send()


class RingGather:
    def __init__(self, links, right, left, own, at_right, at_left, from_left, from_right, on_right, on_left):
        self.first = [
            links.copy(own(0), at_right(0), right),
            links.copy(own(1), at_left(1), left),
            links.copy(own(1), at_right(1), right),
            links.copy(own(0), at_left(0), left),
        ]
        self.onward = [
            links.copy(from_left(0), on_right(0), right),
            links.copy(from_right(1), on_left(1), left),
        ]

    def begin(self):
        self.first[0].start()
        self.first[1].start()

    def follow(self):
        self.first[2].start()
        self.first[3].start()

    def start(self):
        self.begin()
        self.follow()

    def forward(self):
        self.first[0].wait_recv()
        self.onward[0].start()
        self.first[1].wait_recv()
        self.onward[1].start()

    def near(self):
        self.first[2].wait_recv()
        self.first[3].wait_recv()

    def far(self):
        self.onward[0].wait_recv()
        self.onward[1].wait_recv()

    def finish(self):
        self.near()
        self.far()


def body(
    hidden, seg, modulation, qk_gain, w_qkv, w_in, w_out, w_back,
    result,
    raw, xm, win, wback, kv, wqkv_v, wout_v, mod_v, gain_v, seg_x, qx, peak_v, part_out, part_in,
    act, mlp_out, mlp_in, z_out, z_in, gate_in,
    send_sems, recv_sems, local_sems,
):
    g = lax.axis_index("guide")
    s = lax.axis_index("seq")
    t = lax.axis_index("tp")
    x, y, c = s // 8, (s % 8) // 2, s % 2
    yr, yl = (y + 1) % 4, (y + 3) % 4

    def at_seq(xx, yy, cc):
        return {"seq": xx * 8 + yy * 2 + cc}

    x_right, x_left, x_far = at_seq((x + 1) % 4, y, c), at_seq((x + 3) % 4, y, c), at_seq((x + 2) % 4, y, c)
    y_right, y_left = at_seq(x, yr, c), at_seq(x, yl, c)
    mate = at_seq(x, y, 1 - c)
    t_right, t_left, t_far = {"tp": (t + 1) % 4}, {"tp": (t + 3) % 4}, {"tp": (t + 2) % 4}
    partner = {"guide": 1 - g}
    across = [{"guide": 1 - g, "tp": (t + step) % 4} for step in (1, 2, 3)]

    barrier = pltpu.get_barrier_semaphore()
    everyone = (x_right, x_left, x_far, y_right, y_left, mate, t_right, t_left, t_far, partner, *across)
    for device in everyone:
        pl.semaphore_signal(barrier, inc=1, device_id=device, device_id_type=pl.DeviceIdType.MESH)

    def columns(weight, dx, h=None):
        cols = pl.ds(pl.multiple_of(((x + dx) % 4) * GROUP, GROUP), GROUP)
        return weight.at[:, cols] if h is None else weight.at[pl.ds(h * 48, 48), cols]

    pairs = [
        (hidden, raw.at[0, 0]),
        (seg, seg_x.at[0]),
        (modulation, mod_v),
        (qk_gain, gain_v),
        (w_qkv.at[1], wqkv_v.at[1]),
        (w_qkv.at[2], wqkv_v.at[2]),
        (w_qkv.at[0], wqkv_v.at[0]),
        (columns(w_in, 0), win.at[0, y, c]),
        (w_back, wback.at[y, c]),
        (w_out, wout_v),
    ]
    local = [pltpu.make_async_copy(a, b, local_sems.at[i]) for i, (a, b) in enumerate(pairs)]
    for made in local:
        made.start()
    pl.semaphore_wait(barrier, len(everyone))

    links = Links(send_sems, recv_sems)
    half32 = lambda h: pl.ds(h * 32, 32)
    half48 = lambda h: pl.ds(h * 48, 48)
    two = lambda h: pl.ds(h * 2, 2)

    def relative(right, left, spot, own=None):
        spots = [(lambda d: (lambda h: spot(d, h)))(d) for d in (3, 1, 3, 1, 2, 2)]
        return RingGather(links, right, left, own or (lambda h: spot(0, h)), *spots)

    def absolute(spot, own=None):
        spots = [(lambda yy: (lambda h: spot(yy, h)))(yy) for yy in (y, y, yl, yr, yl, yr)]
        return RingGather(links, y_right, y_left, own or (lambda h: spot(y, h)), *spots)

    over_tp = relative(t_right, t_left, lambda d, h: raw.at[0, d, half32(h)], lambda h: hidden.at[half32(h)])
    over_x = [
        relative(
            x_right, x_left, (lambda k: (lambda d, h: raw.at[d, k, half32(h)]))(k),
            (lambda h: hidden.at[half32(h)]) if k == 0 else None,
        )
        for k in range(4)
    ]
    seg_sent = [
        links.copy(seg, seg_x.at[3], x_right),
        links.copy(seg, seg_x.at[1], x_left),
        links.copy(seg, seg_x.at[2], x_far),
    ]
    win_sent = [
        links.copy(columns(w_in, 2), win.at[2, y, c], x_far),
        links.copy(columns(w_in, 1), win.at[3, y, c], x_right),
        links.copy(columns(w_in, 3), win.at[1, y, c], x_left),
    ]
    win_near = absolute(lambda yy, h: win.at[0, yy, c, half48(h)], lambda h: columns(w_in, 0, h))
    win_rest = absolute(lambda yy, h: win.at[1:4, yy, c, half48(h)])
    wback_all = absolute(lambda yy, h: wback.at[yy, c, half48(h)], lambda h: w_back.at[half48(h)])
    win_over = [
        links.copy(win.at[0:1, :, c], win.at[0:1, :, c], mate),
        links.copy(win.at[1:4, :, c], win.at[1:4, :, c], mate),
    ]
    wback_over = links.copy(wback.at[:, c], wback.at[:, c], mate)
    kv_all = absolute(lambda yy, h: kv.at[yy, c, half32(h)])
    kv_over = links.copy(kv.at[:, c], kv.at[:, c], mate)
    q_all = relative(x_right, x_left, lambda d, h: qx.at[d, half32(h)])
    act_all = relative(x_right, x_left, lambda d, h: act.at[d, two(h)])

    gate_sent = links.copy(
        modulation.at[2, :, pl.ds(pl.multiple_of(t * WIDE + (1 - g) * GROUP, GROUP), GROUP)], gate_in, partner
    )

    over_tp.start()
    over_x[0].start()
    for made in seg_sent + win_sent:
        made.start()
    win_near.start()
    wback_all.begin()
    gate_sent.start()

    win_near.forward()
    over_tp.forward()
    over_x[0].forward()
    over_tp.near()
    over_x[3].start()
    over_x[1].start()
    for made in win_sent:
        made.wait_recv()
    win_rest.start()
    for made in local[:4]:
        made.wait()
    for made in seg_sent:
        made.wait_recv()
    over_tp.far()
    over_x[2].start()

    at_row = lax.broadcasted_iota(jnp.int32, (ROWS, ROWS), 0)
    at_col = lax.broadcasted_iota(jnp.int32, (ROWS, ROWS), 1)
    lane = lax.broadcasted_iota(jnp.int32, (ROWS, HEAD), 1).astype(F32)

    def seg_column(d):
        row = jnp.broadcast_to(seg_x[d].astype(F32), (ROWS, ROWS))
        return jnp.sum(jnp.where(at_row == at_col, row, 0.0), axis=-1, keepdims=True)

    seg_cols = [seg_column(d) for d in range(4)]
    one_hots = [jnp.where(seg_cols[d] == lane, 1.0, 0.0).astype(BF16) for d in range(4)]

    def look_up(kind, offset, d):
        table = mod_v[kind, :, pl.ds(pl.multiple_of(offset, WIDE), WIDE)].astype(F32)
        found = jnp.broadcast_to(table[0:1], (ROWS, WIDE))
        for r in range(1, REQUESTS):
            found = jnp.where(seg_cols[d] == float(r), table[r : r + 1], found)
        return found

    def normalise(d):
        total = sum(jnp.sum(raw[d, k].astype(F32), axis=-1, keepdims=True) for k in range(4))
        mean = total * (1.0 / D)
        squares = jnp.zeros((ROWS, 1), F32)
        for k in range(4):
            centred = raw[d, k].astype(F32) - mean
            squares += jnp.sum(centred * centred, axis=-1, keepdims=True)
        scale_rows = lax.rsqrt(squares * (1.0 / D) + 1e-06)
        for k in range(4):
            offset = ((t + k) % 4) * WIDE
            normed = (raw[d, k].astype(F32) - mean) * scale_rows
            xm[d, :, pl.ds(pl.multiple_of(offset, WIDE), WIDE)] = (
                normed * (1.0 + look_up(1, offset, d)) + look_up(0, offset, d)
            ).astype(BF16)

    normalise(0)
    over_x[3].forward()
    over_x[1].forward()

    def head_norm(values, gain):
        return values * lax.rsqrt(jnp.mean(values * values, axis=-1, keepdims=True) + 1e-06) * gain

    rows_own = xm[0]
    local[4].wait()
    keys = dot(rows_own, wqkv_v[1])
    for h in range(HEADS_HERE):
        cols = slice(h * HEAD, (h + 1) * HEAD)
        kv[y, c, :, cols] = head_norm(keys[:, cols], gain_v[1:2, :]).astype(BF16)
    win_rest.forward()
    local[5].wait()
    kv[y, c, :, GROUP : 2 * GROUP] = dot(rows_own, wqkv_v[2]).astype(BF16)
    kv[y, c, :, 2 * GROUP :] = one_hots[0]
    kv_all.start()
    over_x[2].forward()
    wback_all.follow()
    local[6].wait()
    query = dot(rows_own, wqkv_v[0])
    for h in range(HEADS_HERE):
        cols = slice(h * HEAD, (h + 1) * HEAD)
        qx[0, :, cols] = head_norm(query[:, cols], gain_v[0:1, :]).astype(BF16)
    q_all.start()

    local[7].wait()
    win_near.finish()
    win_over[0].start()
    win_rest.finish()
    win_over[1].start()
    kv_all.forward()
    wback_all.forward()
    for k in (0, 1, 3, 2):
        over_x[k].finish()
    normalise(1)
    q_all.forward()
    normalise(3)
    kv_all.finish()
    kv_over.start()
    normalise(2)
    for made in win_over:
        made.wait_recv()

    pre = jnp.zeros((4 * ROWS, GROUP), F32)
    for d in range(4):
        cols = pl.ds(pl.multiple_of(((x + d) % 4) * WIDE, WIDE), WIDE)
        pre += dot(xm[:, :, cols].reshape(4 * ROWS, WIDE), win[d].reshape(WIDE, GROUP))
    acted = jax.nn.gelu(pre, approximate=True).astype(BF16)
    for d in range(4):
        act[0, (x + d) % 4] = acted[d * ROWS : (d + 1) * ROWS]
    act_all.start()

    q_all.finish()
    kv_over.wait_recv()

    seen = kv.reshape(8 * ROWS, KV)
    same = dot_t(jnp.concatenate(one_hots, axis=0), seen[:, 2 * GROUP :]) > 0.5
    lanes = lax.broadcasted_iota(jnp.int32, (4 * ROWS, HEAD), 1)
    stats = jnp.zeros((4 * ROWS, HEAD), F32)
    for h in range(HEADS_HERE):
        k_cols = slice(h * HEAD, (h + 1) * HEAD)
        v_cols = slice(GROUP + h * HEAD, GROUP + (h + 1) * HEAD)
        score = dot_t(qx[:, :, k_cols].reshape(4 * ROWS, HEAD), seen[:, k_cols]) * HEAD ** (-0.5)
        score = jnp.where(same, score, -1e30)
        peak_v[...] = jnp.broadcast_to(jnp.max(score, axis=-1, keepdims=True), (4 * ROWS, HEAD)).astype(BF16)
        peak = peak_v[:, 0:1].astype(F32)
        weight = jnp.where(same, jnp.exp(score - peak), 0.0)
        total = jnp.sum(weight, axis=-1, keepdims=True)
        summed = dot(weight.astype(BF16), seen[:, v_cols])
        part = (summed / jnp.where(total > 0.0, total, 1.0)).astype(BF16)
        part_out[:, :, k_cols] = part.reshape(4, ROWS, HEAD)
        upper = total.astype(BF16).astype(F32)
        stats = jnp.where(lanes == h, peak, stats)
        stats = jnp.where(lanes == 3 + h, upper, stats)
        stats = jnp.where(lanes == 6 + h, total - upper, stats)
        if h == 0:
            local[8].wait()
            wback_all.finish()
            wback_over.start()
        if h == 1:
            act_all.forward()
    part_out[:, :, GROUP:] = stats.astype(BF16).reshape(4, ROWS, HEAD)
    part_sent = [
        links.copy(part_out.at[2], part_in.at[2], x_far),
        links.copy(part_out.at[1], part_in.at[3], x_right),
        links.copy(part_out.at[3], part_in.at[1], x_left),
    ]
    for made in part_sent:
        made.start()
    wback_over.wait_recv()

    def back(d):
        cols = pl.ds(pl.multiple_of(((x + d) % 4) * GROUP, GROUP), GROUP)
        return dot_t(act[d].reshape(4 * ROWS, GROUP), wback[:, :, :, cols].reshape(WIDE, GROUP))

    fed = back(0)
    act_all.near()
    fed += back(1)
    fed += back(3)
    act_all.far()
    fed += back(2)
    for b in range(4):
        mlp_out[(b - x + 4) % 4] = fed[b * ROWS : (b + 1) * ROWS].astype(BF16)
    mlp_sent = {
        2: links.copy(mlp_out.at[2], mlp_in.at[2], x_far),
        3: links.copy(mlp_out.at[1], mlp_in.at[3], x_right),
        1: links.copy(mlp_out.at[3], mlp_in.at[1], x_left),
    }
    for made in mlp_sent.values():
        made.start()

    for made in part_sent:
        made.wait_recv()
    attended = []
    for h in range(HEADS_HERE):
        cols = slice(h * HEAD, (h + 1) * HEAD)
        parts = [part_out[0]] + [part_in[d] for d in (1, 2, 3)]
        stat = [p[:, GROUP:].astype(F32) for p in parts]
        top = stat[0][:, h : h + 1]
        for other in stat[1:]:
            top = jnp.maximum(top, other[:, h : h + 1])
        total = jnp.zeros((ROWS, 1), F32)
        summed = jnp.zeros((ROWS, HEAD), F32)
        for p, st in zip(parts, stat):
            share = jnp.exp(st[:, h : h + 1] - top) * (st[:, 3 + h : 4 + h] + st[:, 6 + h : 7 + h])
            total += share
            summed += share * p[:, cols].astype(F32)
        attended.append((summed / total).astype(BF16))
    attended = jnp.concatenate(attended, axis=1)
    local[9].wait()

    base = links.used
    own_cols = pl.ds(pl.multiple_of(g * GROUP, GROUP), GROUP)
    other_cols = pl.ds(pl.multiple_of((1 - g) * GROUP, GROUP), GROUP)

    def term_copy(d, kind, step):
        return pltpu.make_async_remote_copy(
            src_ref=z_out.at[d, :, (own_cols, other_cols)[kind]],
            dst_ref=z_in.at[kind, step],
            send_sem=send_sems.at[base + 4 * kind + step],
            recv_sem=recv_sems.at[base + 4 * kind + step],
            device_id={"guide": (g, 1 - g)[kind], "tp": (t + step) % 4},
            device_id_type=pl.DeviceIdType.MESH,
        )

    for d in (0, 1, 3, 2):
        e = (x + d) % 4
        step = (x + d - t + 4) % 4
        term = dot(attended, wout_v[:, pl.ds(pl.multiple_of(e * WIDE, WIDE), WIDE)])
        if d == 0:
            term += mlp_out[0].astype(F32)
        else:
            mlp_sent[d].wait_recv()
            term += mlp_in[d].astype(F32)
        z_out[d] = term.astype(BF16)
        term_copy(d, 1, step).start()

        @pl.when(step != 0)
        def _():
            term_copy(d, 0, step).start()

    gate_sent.wait_recv()
    own_table = mod_v[2, :, pl.ds(pl.multiple_of(t * WIDE + g * GROUP, GROUP), GROUP)].astype(F32)
    other_table = gate_in[...].astype(F32)

    def gate_of(table):
        found = jnp.broadcast_to(table[0:1], (ROWS, GROUP))
        for r in range(1, REQUESTS):
            found = jnp.where(seg_cols[0] == float(r), table[r : r + 1], found)
        return found

    own_gate, other_gate = gate_of(own_table), gate_of(other_table)
    residual = raw[0, 0, :, own_cols].astype(F32)
    own_branch = z_out[(t - x + 4) % 4, :, own_cols].astype(F32)
    arrived = [term_copy(0, 0, step) for step in (1, 2, 3)] + [term_copy(0, 1, step) for step in range(4)]
    for made in arrived:
        made.wait_recv()
    for step in (1, 2, 3):
        own_branch += z_in[0, step].astype(F32)
    other_branch = z_in[1, 0].astype(F32)
    for step in (1, 2, 3):
        other_branch += z_in[1, step].astype(F32)
    mine = (residual + own_gate * own_branch).astype(BF16).astype(F32)
    theirs = (residual + other_gate * other_branch).astype(BF16).astype(F32)
    cond = jnp.where(g == 0, mine, theirs)
    uncond = jnp.where(g == 0, theirs, mine)
    result[...] = (uncond + GUIDANCE * (cond - uncond)).astype(BF16)
    for made in arrived:
        made.wait_send()
    links.drain()


def on_device(hidden, seg_ids, modulation, qk_gain, w_qkv, w_mlp_in, w_out, w_mlp_back):
    anywhere = pl.BlockSpec(memory_space=pl.ANY)
    guided = pl.pallas_call(
        body,
        out_shape=jax.ShapeDtypeStruct((ROWS, GROUP), BF16),
        in_specs=[anywhere] * 8,
        out_specs=pl.BlockSpec(memory_space=pltpu.VMEM),
        scratch_shapes=[
            pltpu.VMEM((4, 4, ROWS, WIDE), BF16),
            pltpu.VMEM((4, ROWS, D), BF16),
            pltpu.VMEM((4, 4, 2, SLAB, GROUP), BF16),
            pltpu.VMEM((4, 2, SLAB, 4 * GROUP), BF16),
            pltpu.VMEM((4, 2, ROWS, KV), BF16),
            pltpu.VMEM((3, D, GROUP), BF16),
            pltpu.VMEM((GROUP, D), BF16),
            pltpu.VMEM((3, REQUESTS, D), BF16),
            pltpu.VMEM((2, HEAD), F32),
            pltpu.VMEM((4, 1, ROWS), jnp.int32),
            pltpu.VMEM((4, ROWS, GROUP), BF16),
            pltpu.VMEM((4 * ROWS, HEAD), BF16),
            pltpu.VMEM((4, ROWS, GROUP + HEAD), BF16),
            pltpu.VMEM((4, ROWS, GROUP + HEAD), BF16),
            pltpu.VMEM((4, 4, ROWS, GROUP), BF16),
            pltpu.VMEM((4, ROWS, WIDE), BF16),
            pltpu.VMEM((4, ROWS, WIDE), BF16),
            pltpu.VMEM((4, ROWS, WIDE), BF16),
            pltpu.VMEM((2, 4, ROWS, GROUP), BF16),
            pltpu.VMEM((REQUESTS, GROUP), BF16),
            pltpu.SemaphoreType.DMA((COPIES,)),
            pltpu.SemaphoreType.DMA((COPIES,)),
            pltpu.SemaphoreType.DMA((LOCALS,)),
        ],
        compiler_params=pltpu.CompilerParams(
            collective_id=0, has_side_effects=True, vmem_limit_bytes=60 * 1024 * 1024
        ),
        name="layer",
    )(
        hidden,
        seg_ids.reshape(1, ROWS),
        jnp.transpose(modulation[0], (1, 0, 2)),
        qk_gain,
        jnp.transpose(w_qkv, (1, 0, 2)),
        w_mlp_in,
        w_out,
        w_mlp_back,
    )
    return guided.reshape(ROWS, 1, 1, GROUP)


def solution(mesh):
    in_specs = (
        P("seq", "tp"),
        P("seq"),
        P("guide", None, None, None),
        P(),
        P(None, None, "tp"),
        P("seq", "tp"),
        P("tp", None),
        P("seq", "tp"),
    )
    out_specs = P("seq", "tp", "guide", None)
    return jax.shard_map(
        on_device, mesh=mesh, in_specs=in_specs, out_specs=out_specs, check_vma=False
    )
```

```python
import jax
import jax.numpy as jnp
from jax import lax
from jax.experimental import pallas as pl
from jax.experimental.pallas import tpu as pltpu
from jax.sharding import PartitionSpec as P

D = 3072
HEAD = 128
ROWS = 64
WIDE = 768
GROUP = 384
SLAB = 96
HEADS_HERE = 3
REQUESTS = 4
KV = 2 * GROUP + HEAD
GUIDANCE = 3.5
COPIES = 128
LOCALS = 10

F32 = jnp.float32
BF16 = jnp.bfloat16


def dot(a, b):
    return jnp.dot(a, b, preferred_element_type=F32)


def dot_t(a, b):
    return lax.dot_general(a, b, (((1,), (1,)), ((), ())), preferred_element_type=F32)


class Links:
    def __init__(self, send_sems, recv_sems):
        self.send_sems, self.recv_sems = send_sems, recv_sems
        self.used = 0
        self.sent = []

    def copy(self, src, dst, device):
        i = self.used
        self.used += 1
        made = pltpu.make_async_remote_copy(
            src_ref=src,
            dst_ref=dst,
            send_sem=self.send_sems.at[i],
            recv_sem=self.recv_sems.at[i],
            device_id=device,
            device_id_type=pl.DeviceIdType.MESH,
        )
        self.sent.append(made)
        return made

    def drain(self):
        for made in self.sent:
            made.wait_send()


class RingGather:
    def __init__(self, links, right, left, own, at_right, at_left, from_left, from_right, on_right, on_left):
        self.first = [
            links.copy(own(0), at_right(0), right),
            links.copy(own(1), at_left(1), left),
            links.copy(own(1), at_right(1), right),
            links.copy(own(0), at_left(0), left),
        ]
        self.onward = [
            links.copy(from_left(0), on_right(0), right),
            links.copy(from_right(1), on_left(1), left),
        ]

    def begin(self):
        self.first[0].start()
        self.first[1].start()

    def follow(self):
        self.first[2].start()
        self.first[3].start()

    def start(self):
        self.begin()
        self.follow()

    def forward(self):
        self.first[0].wait_recv()
        self.onward[0].start()
        self.first[1].wait_recv()
        self.onward[1].start()

    def near(self):
        self.first[2].wait_recv()
        self.first[3].wait_recv()

    def far(self):
        self.onward[0].wait_recv()
        self.onward[1].wait_recv()

    def finish(self):
        self.near()
        self.far()


def body(
    hidden, seg, modulation, qk_gain, w_qkv, w_in, w_out, w_back,
    result,
    raw, xm, win, wback, kv, wqkv_v, wout_v, mod_v, gain_v, seg_x, qx, peak_v, part_out, part_in,
    act, mlp_out, mlp_in, z_out, z_in, gate_in,
    send_sems, recv_sems, local_sems,
):
    g = lax.axis_index("guide")
    s = lax.axis_index("seq")
    t = lax.axis_index("tp")
    x, y, c = s // 8, (s % 8) // 2, s % 2
    yr, yl = (y + 1) % 4, (y + 3) % 4

    def at_seq(xx, yy, cc):
        return {"seq": xx * 8 + yy * 2 + cc}

    x_right, x_left, x_far = at_seq((x + 1) % 4, y, c), at_seq((x + 3) % 4, y, c), at_seq((x + 2) % 4, y, c)
    y_right, y_left = at_seq(x, yr, c), at_seq(x, yl, c)
    mate = at_seq(x, y, 1 - c)
    t_right, t_left, t_far = {"tp": (t + 1) % 4}, {"tp": (t + 3) % 4}, {"tp": (t + 2) % 4}
    partner = {"guide": 1 - g}
    across = [{"guide": 1 - g, "tp": (t + step) % 4} for step in (1, 2, 3)]

    barrier = pltpu.get_barrier_semaphore()
    everyone = (x_right, x_left, x_far, y_right, y_left, mate, t_right, t_left, t_far, partner, *across)
    for device in everyone:
        pl.semaphore_signal(barrier, inc=1, device_id=device, device_id_type=pl.DeviceIdType.MESH)

    def columns(weight, dx, h=None):
        cols = pl.ds(pl.multiple_of(((x + dx) % 4) * GROUP, GROUP), GROUP)
        return weight.at[:, cols] if h is None else weight.at[pl.ds(h * 48, 48), cols]

    pairs = [
        (hidden, raw.at[0, 0]),
        (seg, seg_x.at[0]),
        (modulation, mod_v),
        (qk_gain, gain_v),
        (w_qkv.at[1], wqkv_v.at[1]),
        (w_qkv.at[2], wqkv_v.at[2]),
        (w_qkv.at[0], wqkv_v.at[0]),
        (columns(w_in, 0), win.at[0, y, c]),
        (w_back, wback.at[y, c]),
        (w_out, wout_v),
    ]
    local = [pltpu.make_async_copy(a, b, local_sems.at[i]) for i, (a, b) in enumerate(pairs)]
    for made in local:
        made.start()
    pl.semaphore_wait(barrier, len(everyone))

    links = Links(send_sems, recv_sems)
    half32 = lambda h: pl.ds(h * 32, 32)
    half48 = lambda h: pl.ds(h * 48, 48)
    two = lambda h: pl.ds(h * 2, 2)

    def relative(right, left, spot, own=None):
        spots = [(lambda d: (lambda h: spot(d, h)))(d) for d in (3, 1, 3, 1, 2, 2)]
        return RingGather(links, right, left, own or (lambda h: spot(0, h)), *spots)

    def absolute(spot, own=None):
        spots = [(lambda yy: (lambda h: spot(yy, h)))(yy) for yy in (y, y, yl, yr, yl, yr)]
        return RingGather(links, y_right, y_left, own or (lambda h: spot(y, h)), *spots)

    over_tp = relative(t_right, t_left, lambda d, h: raw.at[0, d, half32(h)], lambda h: hidden.at[half32(h)])
    over_x = [
        relative(
            x_right, x_left, (lambda k: (lambda d, h: raw.at[d, k, half32(h)]))(k),
            (lambda h: hidden.at[half32(h)]) if k == 0 else None,
        )
        for k in range(4)
    ]
    seg_sent = [
        links.copy(seg, seg_x.at[3], x_right),
        links.copy(seg, seg_x.at[1], x_left),
        links.copy(seg, seg_x.at[2], x_far),
    ]
    win_sent = [
        links.copy(columns(w_in, 1), win.at[2, y, c], x_right),
        links.copy(columns(w_in, 3), win.at[1, y, c], x_left),
        links.copy(columns(w_in, 2), win.at[3, y, c], x_far),
    ]
    win_near = absolute(lambda yy, h: win.at[0, yy, c, half48(h)], lambda h: columns(w_in, 0, h))
    win_sides = absolute(lambda yy, h: win.at[1:3, yy, c, half48(h)])
    win_rest = absolute(lambda yy, h: win.at[3, yy, c, half48(h)])
    wback_all = absolute(lambda yy, h: wback.at[yy, c, half48(h)], lambda h: w_back.at[half48(h)])

    def to_mate(spot):
        return links.copy(spot, spot, mate)

    over_first = to_mate(win.at[0, :, c])
    over_sides = [to_mate(win.at[1:3, yy, c]) for yy in (y, yr, yl, (y + 2) % 4)]
    over_rest = [to_mate(win.at[3, yy, c]) for yy in (y, yr, yl, (y + 2) % 4)]
    over_back = [to_mate(wback.at[yy, c]) for yy in (y, yr, yl, (y + 2) % 4)]
    kv_all = absolute(lambda yy, h: kv.at[yy, c, half32(h)])
    kv_over = links.copy(kv.at[:, c], kv.at[:, c], mate)
    q_all = relative(x_right, x_left, lambda d, h: qx.at[d, half32(h)])
    act_all = relative(x_right, x_left, lambda d, h: act.at[d, two(h)])

    gate_sent = links.copy(
        modulation.at[2, :, pl.ds(pl.multiple_of(t * WIDE + (1 - g) * GROUP, GROUP), GROUP)], gate_in, partner
    )

    over_tp.start()
    for made in win_sent:
        made.start()
    win_near.start()
    over_x[0].start()
    for made in seg_sent:
        made.start()
    gate_sent.start()

    win_near.forward()
    win_sent[0].wait_recv()
    win_sent[1].wait_recv()
    win_sides.start()
    over_sides[0].start()
    over_tp.forward()
    over_x[0].forward()
    win_sent[2].wait_recv()
    win_rest.start()
    over_rest[0].start()
    over_tp.near()
    over_x[3].start()
    over_x[1].start()
    win_sides.forward()
    for made in local[:4]:
        made.wait()
    for made in seg_sent:
        made.wait_recv()
    win_rest.forward()
    wback_all.begin()
    local[7].wait()
    win_near.finish()
    over_first.start()
    over_tp.far()
    over_x[2].start()

    at_row = lax.broadcasted_iota(jnp.int32, (ROWS, ROWS), 0)
    at_col = lax.broadcasted_iota(jnp.int32, (ROWS, ROWS), 1)
    lane = lax.broadcasted_iota(jnp.int32, (ROWS, HEAD), 1).astype(F32)

    def seg_column(d):
        row = jnp.broadcast_to(seg_x[d].astype(F32), (ROWS, ROWS))
        return jnp.sum(jnp.where(at_row == at_col, row, 0.0), axis=-1, keepdims=True)

    seg_cols = [seg_column(d) for d in range(4)]
    one_hots = [jnp.where(seg_cols[d] == lane, 1.0, 0.0).astype(BF16) for d in range(4)]

    def look_up(kind, offset, d):
        table = mod_v[kind, :, pl.ds(pl.multiple_of(offset, WIDE), WIDE)].astype(F32)
        found = jnp.broadcast_to(table[0:1], (ROWS, WIDE))
        for r in range(1, REQUESTS):
            found = jnp.where(seg_cols[d] == float(r), table[r : r + 1], found)
        return found

    def normalise(d):
        total = sum(jnp.sum(raw[d, k].astype(F32), axis=-1, keepdims=True) for k in range(4))
        mean = total * (1.0 / D)
        squares = jnp.zeros((ROWS, 1), F32)
        for k in range(4):
            centred = raw[d, k].astype(F32) - mean
            squares += jnp.sum(centred * centred, axis=-1, keepdims=True)
        scale_rows = lax.rsqrt(squares * (1.0 / D) + 1e-06)
        for k in range(4):
            offset = ((t + k) % 4) * WIDE
            normed = (raw[d, k].astype(F32) - mean) * scale_rows
            xm[d, :, pl.ds(pl.multiple_of(offset, WIDE), WIDE)] = (
                normed * (1.0 + look_up(1, offset, d)) + look_up(0, offset, d)
            ).astype(BF16)

    normalise(0)
    over_x[3].forward()
    over_x[1].forward()

    def head_norm(values, gain):
        return values * lax.rsqrt(jnp.mean(values * values, axis=-1, keepdims=True) + 1e-06) * gain

    rows_own = xm[0]
    local[4].wait()
    keys = dot(rows_own, wqkv_v[1])
    for h in range(HEADS_HERE):
        cols = slice(h * HEAD, (h + 1) * HEAD)
        kv[y, c, :, cols] = head_norm(keys[:, cols], gain_v[1:2, :]).astype(BF16)
    win_sides.near()
    over_sides[1].start()
    over_sides[2].start()
    local[5].wait()
    kv[y, c, :, GROUP : 2 * GROUP] = dot(rows_own, wqkv_v[2]).astype(BF16)
    kv[y, c, :, 2 * GROUP :] = one_hots[0]
    kv_all.start()
    over_x[2].forward()
    win_rest.near()
    over_rest[1].start()
    over_rest[2].start()
    win_sides.far()
    over_sides[3].start()
    win_rest.far()
    over_rest[3].start()
    local[6].wait()
    query = dot(rows_own, wqkv_v[0])
    for h in range(HEADS_HERE):
        cols = slice(h * HEAD, (h + 1) * HEAD)
        qx[0, :, cols] = head_norm(query[:, cols], gain_v[0:1, :]).astype(BF16)
    q_all.start()

    kv_all.forward()
    wback_all.follow()
    local[8].wait()
    over_back[0].start()
    wback_all.forward()
    for k in (0, 1, 3, 2):
        over_x[k].finish()
    normalise(1)
    q_all.forward()
    normalise(3)
    kv_all.finish()
    kv_over.start()
    normalise(2)
    for made in [over_first, *over_sides, *over_rest]:
        made.wait_recv()

    pre = jnp.zeros((4 * ROWS, GROUP), F32)
    for slot, d in enumerate((0, 1, 3, 2)):
        cols = pl.ds(pl.multiple_of(((x + d) % 4) * WIDE, WIDE), WIDE)
        pre += dot(xm[:, :, cols].reshape(4 * ROWS, WIDE), win[slot].reshape(WIDE, GROUP))
    acted = jax.nn.gelu(pre, approximate=True).astype(BF16)
    for d in range(4):
        act[0, (x + d) % 4] = acted[d * ROWS : (d + 1) * ROWS]
    act_all.start()

    q_all.finish()
    kv_over.wait_recv()

    seen = kv.reshape(8 * ROWS, KV)
    same = dot_t(jnp.concatenate(one_hots, axis=0), seen[:, 2 * GROUP :]) > 0.5
    lanes = lax.broadcasted_iota(jnp.int32, (4 * ROWS, HEAD), 1)
    stats = jnp.zeros((4 * ROWS, HEAD), F32)
    for h in range(HEADS_HERE):
        k_cols = slice(h * HEAD, (h + 1) * HEAD)
        v_cols = slice(GROUP + h * HEAD, GROUP + (h + 1) * HEAD)
        score = dot_t(qx[:, :, k_cols].reshape(4 * ROWS, HEAD), seen[:, k_cols]) * HEAD ** (-0.5)
        score = jnp.where(same, score, -1e30)
        peak_v[...] = jnp.broadcast_to(jnp.max(score, axis=-1, keepdims=True), (4 * ROWS, HEAD)).astype(BF16)
        peak = peak_v[:, 0:1].astype(F32)
        weight = jnp.where(same, jnp.exp(score - peak), 0.0)
        total = jnp.sum(weight, axis=-1, keepdims=True)
        summed = dot(weight.astype(BF16), seen[:, v_cols])
        part = (summed / jnp.where(total > 0.0, total, 1.0)).astype(BF16)
        part_out[:, :, k_cols] = part.reshape(4, ROWS, HEAD)
        upper = total.astype(BF16).astype(F32)
        stats = jnp.where(lanes == h, peak, stats)
        stats = jnp.where(lanes == 3 + h, upper, stats)
        stats = jnp.where(lanes == 6 + h, total - upper, stats)
        if h == 0:
            wback_all.near()
            over_back[1].start()
            over_back[2].start()
        if h == 1:
            act_all.forward()
    part_out[:, :, GROUP:] = stats.astype(BF16).reshape(4, ROWS, HEAD)
    part_sent = [
        links.copy(part_out.at[2], part_in.at[2], x_far),
        links.copy(part_out.at[1], part_in.at[3], x_right),
        links.copy(part_out.at[3], part_in.at[1], x_left),
    ]
    for made in part_sent:
        made.start()
    wback_all.far()
    over_back[3].start()
    for made in over_back:
        made.wait_recv()

    def back(d):
        cols = pl.ds(pl.multiple_of(((x + d) % 4) * GROUP, GROUP), GROUP)
        return dot_t(act[d].reshape(4 * ROWS, GROUP), wback[:, :, :, cols].reshape(WIDE, GROUP))

    fed = back(0)
    act_all.near()
    fed += back(1)
    fed += back(3)
    act_all.far()
    fed += back(2)
    for b in range(4):
        mlp_out[(b - x + 4) % 4] = fed[b * ROWS : (b + 1) * ROWS].astype(BF16)
    mlp_sent = {
        3: links.copy(mlp_out.at[1], mlp_in.at[3], x_right),
        1: links.copy(mlp_out.at[3], mlp_in.at[1], x_left),
        2: links.copy(mlp_out.at[2], mlp_in.at[2], x_far),
    }
    for made in mlp_sent.values():
        made.start()

    for made in part_sent:
        made.wait_recv()
    attended = []
    for h in range(HEADS_HERE):
        cols = slice(h * HEAD, (h + 1) * HEAD)
        parts = [part_out[0]] + [part_in[d] for d in (1, 2, 3)]
        stat = [p[:, GROUP:].astype(F32) for p in parts]
        top = stat[0][:, h : h + 1]
        for other in stat[1:]:
            top = jnp.maximum(top, other[:, h : h + 1])
        total = jnp.zeros((ROWS, 1), F32)
        summed = jnp.zeros((ROWS, HEAD), F32)
        for p, st in zip(parts, stat):
            share = jnp.exp(st[:, h : h + 1] - top) * (st[:, 3 + h : 4 + h] + st[:, 6 + h : 7 + h])
            total += share
            summed += share * p[:, cols].astype(F32)
        attended.append((summed / total).astype(BF16))
    attended = jnp.concatenate(attended, axis=1)
    local[9].wait()

    base = links.used
    own_cols = pl.ds(pl.multiple_of(g * GROUP, GROUP), GROUP)
    other_cols = pl.ds(pl.multiple_of((1 - g) * GROUP, GROUP), GROUP)

    def term_copy(d, kind, step):
        return pltpu.make_async_remote_copy(
            src_ref=z_out.at[d, :, (own_cols, other_cols)[kind]],
            dst_ref=z_in.at[kind, step],
            send_sem=send_sems.at[base + 4 * kind + step],
            recv_sem=recv_sems.at[base + 4 * kind + step],
            device_id={"guide": (g, 1 - g)[kind], "tp": (t + step) % 4},
            device_id_type=pl.DeviceIdType.MESH,
        )

    for d in (0, 1, 3, 2):
        e = (x + d) % 4
        step = (x + d - t + 4) % 4
        term = dot(attended, wout_v[:, pl.ds(pl.multiple_of(e * WIDE, WIDE), WIDE)])
        if d == 0:
            term += mlp_out[0].astype(F32)
        else:
            mlp_sent[d].wait_recv()
            term += mlp_in[d].astype(F32)
        z_out[d] = term.astype(BF16)
        term_copy(d, 1, step).start()

        @pl.when(step != 0)
        def _():
            term_copy(d, 0, step).start()

    gate_sent.wait_recv()
    own_table = mod_v[2, :, pl.ds(pl.multiple_of(t * WIDE + g * GROUP, GROUP), GROUP)].astype(F32)
    other_table = gate_in[...].astype(F32)

    def gate_of(table):
        found = jnp.broadcast_to(table[0:1], (ROWS, GROUP))
        for r in range(1, REQUESTS):
            found = jnp.where(seg_cols[0] == float(r), table[r : r + 1], found)
        return found

    own_gate, other_gate = gate_of(own_table), gate_of(other_table)
    residual = raw[0, 0, :, own_cols].astype(F32)
    own_branch = z_out[(t - x + 4) % 4, :, own_cols].astype(F32)
    arrived = [term_copy(0, 0, step) for step in (1, 2, 3)] + [term_copy(0, 1, step) for step in range(4)]
    for made in arrived:
        made.wait_recv()
    for step in (1, 2, 3):
        own_branch += z_in[0, step].astype(F32)
    other_branch = z_in[1, 0].astype(F32)
    for step in (1, 2, 3):
        other_branch += z_in[1, step].astype(F32)
    mine = (residual + own_gate * own_branch).astype(BF16).astype(F32)
    theirs = (residual + other_gate * other_branch).astype(BF16).astype(F32)
    cond = jnp.where(g == 0, mine, theirs)
    uncond = jnp.where(g == 0, theirs, mine)
    result[...] = (uncond + GUIDANCE * (cond - uncond)).astype(BF16)
    for made in arrived:
        made.wait_send()
    links.drain()


def on_device(hidden, seg_ids, modulation, qk_gain, w_qkv, w_mlp_in, w_out, w_mlp_back):
    anywhere = pl.BlockSpec(memory_space=pl.ANY)
    guided = pl.pallas_call(
        body,
        out_shape=jax.ShapeDtypeStruct((ROWS, GROUP), BF16),
        in_specs=[anywhere] * 8,
        out_specs=pl.BlockSpec(memory_space=pltpu.VMEM),
        scratch_shapes=[
            pltpu.VMEM((4, 4, ROWS, WIDE), BF16),
            pltpu.VMEM((4, ROWS, D), BF16),
            pltpu.VMEM((4, 4, 2, SLAB, GROUP), BF16),
            pltpu.VMEM((4, 2, SLAB, 4 * GROUP), BF16),
            pltpu.VMEM((4, 2, ROWS, KV), BF16),
            pltpu.VMEM((3, D, GROUP), BF16),
            pltpu.VMEM((GROUP, D), BF16),
            pltpu.VMEM((3, REQUESTS, D), BF16),
            pltpu.VMEM((2, HEAD), F32),
            pltpu.VMEM((4, 1, ROWS), jnp.int32),
            pltpu.VMEM((4, ROWS, GROUP), BF16),
            pltpu.VMEM((4 * ROWS, HEAD), BF16),
            pltpu.VMEM((4, ROWS, GROUP + HEAD), BF16),
            pltpu.VMEM((4, ROWS, GROUP + HEAD), BF16),
            pltpu.VMEM((4, 4, ROWS, GROUP), BF16),
            pltpu.VMEM((4, ROWS, WIDE), BF16),
            pltpu.VMEM((4, ROWS, WIDE), BF16),
            pltpu.VMEM((4, ROWS, WIDE), BF16),
            pltpu.VMEM((2, 4, ROWS, GROUP), BF16),
            pltpu.VMEM((REQUESTS, GROUP), BF16),
            pltpu.SemaphoreType.DMA((COPIES,)),
            pltpu.SemaphoreType.DMA((COPIES,)),
            pltpu.SemaphoreType.DMA((LOCALS,)),
        ],
        compiler_params=pltpu.CompilerParams(
            collective_id=0, has_side_effects=True, vmem_limit_bytes=60 * 1024 * 1024
        ),
        name="layer",
    )(
        hidden,
        seg_ids.reshape(1, ROWS),
        jnp.transpose(modulation[0], (1, 0, 2)),
        qk_gain,
        jnp.transpose(w_qkv, (1, 0, 2)),
        w_mlp_in,
        w_out,
        w_mlp_back,
    )
    return guided.reshape(ROWS, 1, 1, GROUP)


def solution(mesh):
    in_specs = (
        P("seq", "tp"),
        P("seq"),
        P("guide", None, None, None),
        P(),
        P(None, None, "tp"),
        P("seq", "tp"),
        P("tp", None),
        P("seq", "tp"),
    )
    out_specs = P("seq", "tp", "guide", None)
    return jax.shard_map(
        on_device, mesh=mesh, in_specs=in_specs, out_specs=out_specs, check_vma=False
    )
```

```python
import jax
import jax.numpy as jnp
from jax import lax
from jax.experimental import pallas as pl
from jax.experimental.pallas import tpu as pltpu
from jax.sharding import PartitionSpec as P

D = 3072
HEAD = 128
ROWS = 64
PART = 32
WIDE = 768
GROUP = 384
SLAB = 96
HEADS_HERE = 3
REQUESTS = 4
KV = 2 * GROUP + HEAD
GUIDANCE = 3.5
COPIES = 160
LOCALS = 10

F32 = jnp.float32
BF16 = jnp.bfloat16


def dot(a, b):
    return jnp.dot(a, b, preferred_element_type=F32)


def dot_t(a, b):
    return lax.dot_general(a, b, (((1,), (1,)), ((), ())), preferred_element_type=F32)


class Links:
    def __init__(self, send_sems, recv_sems):
        self.send_sems, self.recv_sems = send_sems, recv_sems
        self.used = 0
        self.sent = []

    def copy(self, src, dst, device):
        i = self.used
        self.used += 1
        made = pltpu.make_async_remote_copy(
            src_ref=src,
            dst_ref=dst,
            send_sem=self.send_sems.at[i],
            recv_sem=self.recv_sems.at[i],
            device_id=device,
            device_id_type=pl.DeviceIdType.MESH,
        )
        self.sent.append(made)
        return made

    def drain(self):
        for made in self.sent:
            made.wait_send()


class RingGather:
    def __init__(self, links, right, left, own, at_right, at_left, from_left, from_right, on_right, on_left):
        self.first = [
            links.copy(own(0), at_right(0), right),
            links.copy(own(1), at_left(1), left),
            links.copy(own(1), at_right(1), right),
            links.copy(own(0), at_left(0), left),
        ]
        self.onward = [
            links.copy(from_left(0), on_right(0), right),
            links.copy(from_right(1), on_left(1), left),
        ]

    def begin(self):
        self.first[0].start()
        self.first[1].start()

    def follow(self):
        self.first[2].start()
        self.first[3].start()

    def start(self):
        self.begin()
        self.follow()

    def forward(self):
        self.first[0].wait_recv()
        self.onward[0].start()
        self.first[1].wait_recv()
        self.onward[1].start()

    def near(self):
        self.first[2].wait_recv()
        self.first[3].wait_recv()

    def far(self):
        self.onward[0].wait_recv()
        self.onward[1].wait_recv()

    def finish(self):
        self.near()
        self.far()


def body(
    hidden, seg, modulation, qk_gain, w_qkv, w_in, w_out, w_back,
    result,
    raw, xm, win, wback, kv, wqkv_v, wout_v, mod_v, gain_v, seg_x, qx, peak_v, part_out, part_in,
    act, mlp_out, mlp_in, heads_term, z_out, z_in, gate_in,
    send_sems, recv_sems, local_sems,
):
    g = lax.axis_index("guide")
    s = lax.axis_index("seq")
    t = lax.axis_index("tp")
    x, y, c = s // 8, (s % 8) // 2, s % 2
    yr, yl = (y + 1) % 4, (y + 3) % 4

    def at_seq(xx, yy, cc):
        return {"seq": xx * 8 + yy * 2 + cc}

    x_right, x_left, x_far = at_seq((x + 1) % 4, y, c), at_seq((x + 3) % 4, y, c), at_seq((x + 2) % 4, y, c)
    y_right, y_left = at_seq(x, yr, c), at_seq(x, yl, c)
    mate = at_seq(x, y, 1 - c)
    t_right, t_left, t_far = {"tp": (t + 1) % 4}, {"tp": (t + 3) % 4}, {"tp": (t + 2) % 4}
    partner = {"guide": 1 - g}
    across = [{"guide": 1 - g, "tp": (t + step) % 4} for step in (1, 2, 3)]

    barrier = pltpu.get_barrier_semaphore()
    everyone = (x_right, x_left, x_far, y_right, y_left, mate, t_right, t_left, t_far, partner, *across)
    for device in everyone:
        pl.semaphore_signal(barrier, inc=1, device_id=device, device_id_type=pl.DeviceIdType.MESH)

    def columns(weight, dx, h=None):
        cols = pl.ds(pl.multiple_of(((x + dx) % 4) * GROUP, GROUP), GROUP)
        return weight.at[:, cols] if h is None else weight.at[pl.ds(h * 48, 48), cols]

    pairs = [
        (hidden, raw.at[0, 0]),
        (seg, seg_x.at[0]),
        (modulation, mod_v),
        (qk_gain, gain_v),
        (w_qkv.at[1], wqkv_v.at[1]),
        (w_qkv.at[2], wqkv_v.at[2]),
        (w_qkv.at[0], wqkv_v.at[0]),
        (columns(w_in, 0), win.at[0, y, c]),
        (w_back, wback.at[y, c]),
        (w_out, wout_v),
    ]
    local = [pltpu.make_async_copy(a, b, local_sems.at[i]) for i, (a, b) in enumerate(pairs)]
    for made in local:
        made.start()
    pl.semaphore_wait(barrier, len(everyone))

    links = Links(send_sems, recv_sems)
    half32 = lambda h: pl.ds(h * 32, 32)
    half48 = lambda h: pl.ds(h * 48, 48)
    two = lambda h: pl.ds(h * 2, 2)

    def relative(right, left, spot, own=None):
        spots = [(lambda d: (lambda h: spot(d, h)))(d) for d in (3, 1, 3, 1, 2, 2)]
        return RingGather(links, right, left, own or (lambda h: spot(0, h)), *spots)

    def absolute(spot, own=None):
        spots = [(lambda yy: (lambda h: spot(yy, h)))(yy) for yy in (y, y, yl, yr, yl, yr)]
        return RingGather(links, y_right, y_left, own or (lambda h: spot(y, h)), *spots)

    over_tp = relative(t_right, t_left, lambda d, h: raw.at[0, d, half32(h)], lambda h: hidden.at[half32(h)])
    over_x = [
        relative(
            x_right, x_left, (lambda k: (lambda d, h: raw.at[d, k, half32(h)]))(k),
            (lambda h: hidden.at[half32(h)]) if k == 0 else None,
        )
        for k in range(4)
    ]
    seg_sent = [
        links.copy(seg, seg_x.at[3], x_right),
        links.copy(seg, seg_x.at[1], x_left),
        links.copy(seg, seg_x.at[2], x_far),
    ]
    win_sent = [
        links.copy(columns(w_in, 1), win.at[2, y, c], x_right),
        links.copy(columns(w_in, 3), win.at[1, y, c], x_left),
        links.copy(columns(w_in, 2), win.at[3, y, c], x_far),
    ]
    win_near = absolute(lambda yy, h: win.at[0, yy, c, half48(h)], lambda h: columns(w_in, 0, h))
    win_sides = absolute(lambda yy, h: win.at[1:3, yy, c, half48(h)])
    win_rest = absolute(lambda yy, h: win.at[3, yy, c, half48(h)])
    wback_all = absolute(lambda yy, h: wback.at[yy, c, half48(h)], lambda h: w_back.at[half48(h)])

    def to_mate(spot):
        return links.copy(spot, spot, mate)

    over_first = to_mate(win.at[0, :, c])
    over_sides = [to_mate(win.at[1:3, yy, c]) for yy in (y, yr, yl, (y + 2) % 4)]
    over_rest = [to_mate(win.at[3, yy, c]) for yy in (y, yr, yl, (y + 2) % 4)]
    over_back = [to_mate(wback.at[yy, c]) for yy in (y, yr, yl, (y + 2) % 4)]
    kv_all = absolute(lambda yy, h: kv.at[yy, c, half32(h)])
    kv_over = links.copy(kv.at[:, c], kv.at[:, c], mate)
    q_all = relative(x_right, x_left, lambda d, h: qx.at[d, half32(h)])
    act_all = [
        relative(x_right, x_left, (lambda r: (lambda d, h: act.at[d, r, two(h)]))(r)) for r in range(2)
    ]

    gate_sent = links.copy(
        modulation.at[2, :, pl.ds(pl.multiple_of(t * WIDE + (1 - g) * GROUP, GROUP), GROUP)], gate_in, partner
    )

    over_tp.start()
    for made in win_sent:
        made.start()
    win_near.start()
    over_x[0].start()
    for made in seg_sent:
        made.start()
    gate_sent.start()

    win_near.forward()
    win_sent[0].wait_recv()
    win_sent[1].wait_recv()
    win_sides.start()
    over_sides[0].start()
    over_tp.forward()
    over_x[0].forward()
    win_sent[2].wait_recv()
    win_rest.start()
    over_rest[0].start()
    over_tp.near()
    over_x[3].start()
    over_x[1].start()
    win_sides.forward()
    for made in local[:4]:
        made.wait()
    for made in seg_sent:
        made.wait_recv()
    win_rest.forward()
    wback_all.begin()
    local[7].wait()
    win_near.finish()
    over_first.start()
    over_tp.far()
    over_x[2].start()

    at_row = lax.broadcasted_iota(jnp.int32, (ROWS, ROWS), 0)
    at_col = lax.broadcasted_iota(jnp.int32, (ROWS, ROWS), 1)
    lane = lax.broadcasted_iota(jnp.int32, (ROWS, HEAD), 1).astype(F32)

    def seg_column(d):
        row = jnp.broadcast_to(seg_x[d].astype(F32), (ROWS, ROWS))
        return jnp.sum(jnp.where(at_row == at_col, row, 0.0), axis=-1, keepdims=True)

    seg_cols = [seg_column(d) for d in range(4)]
    one_hots = [jnp.where(seg_cols[d] == lane, 1.0, 0.0).astype(BF16) for d in range(4)]

    def look_up(kind, offset, d):
        table = mod_v[kind, :, pl.ds(pl.multiple_of(offset, WIDE), WIDE)].astype(F32)
        found = jnp.broadcast_to(table[0:1], (ROWS, WIDE))
        for r in range(1, REQUESTS):
            found = jnp.where(seg_cols[d] == float(r), table[r : r + 1], found)
        return found

    def normalise(d):
        total = sum(jnp.sum(raw[d, k].astype(F32), axis=-1, keepdims=True) for k in range(4))
        mean = total * (1.0 / D)
        squares = jnp.zeros((ROWS, 1), F32)
        for k in range(4):
            centred = raw[d, k].astype(F32) - mean
            squares += jnp.sum(centred * centred, axis=-1, keepdims=True)
        scale_rows = lax.rsqrt(squares * (1.0 / D) + 1e-06)
        for k in range(4):
            offset = ((t + k) % 4) * WIDE
            normed = (raw[d, k].astype(F32) - mean) * scale_rows
            xm[d, :, pl.ds(pl.multiple_of(offset, WIDE), WIDE)] = (
                normed * (1.0 + look_up(1, offset, d)) + look_up(0, offset, d)
            ).astype(BF16)

    normalise(0)
    over_x[3].forward()
    over_x[1].forward()

    def head_norm(values, gain):
        return values * lax.rsqrt(jnp.mean(values * values, axis=-1, keepdims=True) + 1e-06) * gain

    rows_own = xm[0]
    local[4].wait()
    keys = dot(rows_own, wqkv_v[1])
    for h in range(HEADS_HERE):
        cols = slice(h * HEAD, (h + 1) * HEAD)
        kv[y, c, :, cols] = head_norm(keys[:, cols], gain_v[1:2, :]).astype(BF16)
    win_sides.near()
    over_sides[1].start()
    over_sides[2].start()
    local[5].wait()
    kv[y, c, :, GROUP : 2 * GROUP] = dot(rows_own, wqkv_v[2]).astype(BF16)
    kv[y, c, :, 2 * GROUP :] = one_hots[0]
    kv_all.start()
    over_x[2].forward()
    win_rest.near()
    over_rest[1].start()
    over_rest[2].start()
    win_sides.far()
    over_sides[3].start()
    win_rest.far()
    over_rest[3].start()
    local[6].wait()
    query = dot(rows_own, wqkv_v[0])
    for h in range(HEADS_HERE):
        cols = slice(h * HEAD, (h + 1) * HEAD)
        qx[0, :, cols] = head_norm(query[:, cols], gain_v[0:1, :]).astype(BF16)
    q_all.start()

    kv_all.forward()
    wback_all.follow()
    local[8].wait()
    over_back[0].start()
    wback_all.forward()
    for k in (0, 1, 3, 2):
        over_x[k].finish()
    normalise(1)
    q_all.forward()
    normalise(3)
    kv_all.finish()
    kv_over.start()
    normalise(2)
    for made in [over_first, *over_sides, *over_rest]:
        made.wait_recv()

    pre = jnp.zeros((4 * ROWS, GROUP), F32)
    for slot, d in enumerate((0, 1, 3, 2)):
        cols = pl.ds(pl.multiple_of(((x + d) % 4) * WIDE, WIDE), WIDE)
        pre += dot(xm[:, :, cols].reshape(4 * ROWS, WIDE), win[slot].reshape(WIDE, GROUP))
    acted = jax.nn.gelu(pre, approximate=True).astype(BF16)
    for d in range(4):
        for r in range(2):
            act[0, r, (x + d) % 4] = acted[d * ROWS + r * PART : d * ROWS + (r + 1) * PART]
    act_all[0].start()
    act_all[1].start()

    q_all.finish()
    kv_over.wait_recv()

    seen = kv.reshape(8 * ROWS, KV)
    same = dot_t(jnp.concatenate(one_hots, axis=0), seen[:, 2 * GROUP :]) > 0.5
    lanes = lax.broadcasted_iota(jnp.int32, (4 * ROWS, HEAD), 1)
    stats = jnp.zeros((4 * ROWS, HEAD), F32)
    for h in range(HEADS_HERE):
        k_cols = slice(h * HEAD, (h + 1) * HEAD)
        v_cols = slice(GROUP + h * HEAD, GROUP + (h + 1) * HEAD)
        score = dot_t(qx[:, :, k_cols].reshape(4 * ROWS, HEAD), seen[:, k_cols]) * HEAD ** (-0.5)
        score = jnp.where(same, score, -1e30)
        peak_v[...] = jnp.broadcast_to(jnp.max(score, axis=-1, keepdims=True), (4 * ROWS, HEAD)).astype(BF16)
        peak = peak_v[:, 0:1].astype(F32)
        weight = jnp.where(same, jnp.exp(score - peak), 0.0)
        total = jnp.sum(weight, axis=-1, keepdims=True)
        summed = dot(weight.astype(BF16), seen[:, v_cols])
        part = (summed / jnp.where(total > 0.0, total, 1.0)).astype(BF16)
        part_out[:, :, k_cols] = part.reshape(4, ROWS, HEAD)
        upper = total.astype(BF16).astype(F32)
        stats = jnp.where(lanes == h, peak, stats)
        stats = jnp.where(lanes == 3 + h, upper, stats)
        stats = jnp.where(lanes == 6 + h, total - upper, stats)
        if h == 0:
            wback_all.near()
            over_back[1].start()
            over_back[2].start()
        if h == 1:
            act_all[0].forward()
    part_out[:, :, GROUP:] = stats.astype(BF16).reshape(4, ROWS, HEAD)
    part_sent = [
        links.copy(part_out.at[2], part_in.at[2], x_far),
        links.copy(part_out.at[1], part_in.at[3], x_right),
        links.copy(part_out.at[3], part_in.at[1], x_left),
    ]
    for made in part_sent:
        made.start()
    act_all[1].forward()
    wback_all.far()
    over_back[3].start()
    for made in over_back:
        made.wait_recv()

    def back(d, r):
        cols = pl.ds(pl.multiple_of(((x + d) % 4) * GROUP, GROUP), GROUP)
        return dot_t(act[d, r].reshape(4 * PART, GROUP), wback[:, :, :, cols].reshape(WIDE, GROUP))

    def output_product(r):
        fed = back(0, r)
        act_all[r].near()
        fed += back(1, r)
        fed += back(3, r)
        act_all[r].far()
        fed += back(2, r)
        for b in range(4):
            mlp_out[r, (b - x + 4) % 4] = fed[b * PART : (b + 1) * PART].astype(BF16)
        sent = {
            3: links.copy(mlp_out.at[r, 1], mlp_in.at[r, 3], x_right),
            1: links.copy(mlp_out.at[r, 3], mlp_in.at[r, 1], x_left),
            2: links.copy(mlp_out.at[r, 2], mlp_in.at[r, 2], x_far),
        }
        for made in sent.values():
            made.start()
        return sent

    mlp_sent = [output_product(0)]

    for made in part_sent:
        made.wait_recv()
    attended = []
    for h in range(HEADS_HERE):
        cols = slice(h * HEAD, (h + 1) * HEAD)
        parts = [part_out[0]] + [part_in[d] for d in (1, 2, 3)]
        stat = [p[:, GROUP:].astype(F32) for p in parts]
        top = stat[0][:, h : h + 1]
        for other in stat[1:]:
            top = jnp.maximum(top, other[:, h : h + 1])
        total = jnp.zeros((ROWS, 1), F32)
        summed = jnp.zeros((ROWS, HEAD), F32)
        for p, st in zip(parts, stat):
            share = jnp.exp(st[:, h : h + 1] - top) * (st[:, 3 + h : 4 + h] + st[:, 6 + h : 7 + h])
            total += share
            summed += share * p[:, cols].astype(F32)
        attended.append((summed / total).astype(BF16))
    attended = jnp.concatenate(attended, axis=1)
    local[9].wait()

    base = COPIES - 16
    own_cols = pl.ds(pl.multiple_of(g * GROUP, GROUP), GROUP)
    other_cols = pl.ds(pl.multiple_of((1 - g) * GROUP, GROUP), GROUP)

    def term_copy(r, d, kind, step):
        return pltpu.make_async_remote_copy(
            src_ref=z_out.at[r, d, :, (own_cols, other_cols)[kind]],
            dst_ref=z_in.at[r, kind, step],
            send_sem=send_sems.at[base + 8 * r + 4 * kind + step],
            recv_sem=recv_sems.at[base + 8 * r + 4 * kind + step],
            device_id={"guide": (g, 1 - g)[kind], "tp": (t + step) % 4},
            device_id_type=pl.DeviceIdType.MESH,
        )

    for d in range(4):
        e = (x + d) % 4
        heads_term[d] = dot(attended, wout_v[:, pl.ds(pl.multiple_of(e * WIDE, WIDE), WIDE)])

    def send_term(r, d):
        step = (x + d - t + 4) % 4
        term = heads_term[d, r * PART : (r + 1) * PART]
        if d == 0:
            term += mlp_out[r, 0].astype(F32)
        else:
            mlp_sent[r][d].wait_recv()
            term += mlp_in[r, d].astype(F32)
        z_out[r, d] = term.astype(BF16)
        term_copy(r, d, 1, step).start()

        @pl.when(step != 0)
        def _():
            term_copy(r, d, 0, step).start()

    send_term(0, 0)
    mlp_sent.append(output_product(1))
    for d in (1, 3, 2):
        send_term(0, d)
    for d in (0, 1, 3, 2):
        send_term(1, d)

    gate_sent.wait_recv()
    own_table = mod_v[2, :, pl.ds(pl.multiple_of(t * WIDE + g * GROUP, GROUP), GROUP)].astype(F32)
    other_table = gate_in[...].astype(F32)

    def gate_of(table):
        found = jnp.broadcast_to(table[0:1], (ROWS, GROUP))
        for r in range(1, REQUESTS):
            found = jnp.where(seg_cols[0] == float(r), table[r : r + 1], found)
        return found

    own_gate, other_gate = gate_of(own_table), gate_of(other_table)
    arrived = []
    for r in range(2):
        rows = slice(r * PART, (r + 1) * PART)
        residual = raw[0, 0, rows, own_cols].astype(F32)
        own_branch = z_out[r, (t - x + 4) % 4, :, own_cols].astype(F32)
        here = [term_copy(r, 0, 0, step) for step in (1, 2, 3)] + [term_copy(r, 0, 1, step) for step in range(4)]
        for made in here:
            made.wait_recv()
        arrived += here
        for step in (1, 2, 3):
            own_branch += z_in[r, 0, step].astype(F32)
        other_branch = z_in[r, 1, 0].astype(F32)
        for step in (1, 2, 3):
            other_branch += z_in[r, 1, step].astype(F32)
        mine = (residual + own_gate[rows] * own_branch).astype(BF16).astype(F32)
        theirs = (residual + other_gate[rows] * other_branch).astype(BF16).astype(F32)
        cond = jnp.where(g == 0, mine, theirs)
        uncond = jnp.where(g == 0, theirs, mine)
        result[rows] = (uncond + GUIDANCE * (cond - uncond)).astype(BF16)
    for made in arrived:
        made.wait_send()
    links.drain()


def on_device(hidden, seg_ids, modulation, qk_gain, w_qkv, w_mlp_in, w_out, w_mlp_back):
    anywhere = pl.BlockSpec(memory_space=pl.ANY)
    guided = pl.pallas_call(
        body,
        out_shape=jax.ShapeDtypeStruct((ROWS, GROUP), BF16),
        in_specs=[anywhere] * 8,
        out_specs=pl.BlockSpec(memory_space=pltpu.VMEM),
        scratch_shapes=[
            pltpu.VMEM((4, 4, ROWS, WIDE), BF16),
            pltpu.VMEM((4, ROWS, D), BF16),
            pltpu.VMEM((4, 4, 2, SLAB, GROUP), BF16),
            pltpu.VMEM((4, 2, SLAB, 4 * GROUP), BF16),
            pltpu.VMEM((4, 2, ROWS, KV), BF16),
            pltpu.VMEM((3, D, GROUP), BF16),
            pltpu.VMEM((GROUP, D), BF16),
            pltpu.VMEM((3, REQUESTS, D), BF16),
            pltpu.VMEM((2, HEAD), F32),
            pltpu.VMEM((4, 1, ROWS), jnp.int32),
            pltpu.VMEM((4, ROWS, GROUP), BF16),
            pltpu.VMEM((4 * ROWS, HEAD), BF16),
            pltpu.VMEM((4, ROWS, GROUP + HEAD), BF16),
            pltpu.VMEM((4, ROWS, GROUP + HEAD), BF16),
            pltpu.VMEM((4, 2, 4, PART, GROUP), BF16),
            pltpu.VMEM((2, 4, PART, WIDE), BF16),
            pltpu.VMEM((2, 4, PART, WIDE), BF16),
            pltpu.VMEM((4, ROWS, WIDE), F32),
            pltpu.VMEM((2, 4, PART, WIDE), BF16),
            pltpu.VMEM((2, 2, 4, PART, GROUP), BF16),
            pltpu.VMEM((REQUESTS, GROUP), BF16),
            pltpu.SemaphoreType.DMA((COPIES,)),
            pltpu.SemaphoreType.DMA((COPIES,)),
            pltpu.SemaphoreType.DMA((LOCALS,)),
        ],
        compiler_params=pltpu.CompilerParams(
            collective_id=0, has_side_effects=True, vmem_limit_bytes=60 * 1024 * 1024
        ),
        name="layer",
    )(
        hidden,
        seg_ids.reshape(1, ROWS),
        jnp.transpose(modulation[0], (1, 0, 2)),
        qk_gain,
        jnp.transpose(w_qkv, (1, 0, 2)),
        w_mlp_in,
        w_out,
        w_mlp_back,
    )
    return guided.reshape(ROWS, 1, 1, GROUP)


def solution(mesh):
    in_specs = (
        P("seq", "tp"),
        P("seq"),
        P("guide", None, None, None),
        P(),
        P(None, None, "tp"),
        P("seq", "tp"),
        P("tp", None),
        P("seq", "tp"),
    )
    out_specs = P("seq", "tp", "guide", None)
    return jax.shard_map(
        on_device, mesh=mesh, in_specs=in_specs, out_specs=out_specs, check_vma=False
    )
```

```python
import jax
import jax.numpy as jnp
from jax import lax
from jax.experimental import pallas as pl
from jax.experimental.pallas import tpu as pltpu
from jax.sharding import PartitionSpec as P

D = 3072
HEAD = 128
ROWS = 64
WIDE = 768
GROUP = 384
SLAB = 96
HEADS_HERE = 3
REQUESTS = 4
KV = 2 * GROUP + HEAD
GUIDANCE = 3.5
COPIES = 128
LOCALS = 10

F32 = jnp.float32
BF16 = jnp.bfloat16


def dot(a, b):
    return jnp.dot(a, b, preferred_element_type=F32)


def dot_t(a, b):
    return lax.dot_general(a, b, (((1,), (1,)), ((), ())), preferred_element_type=F32)


class Links:
    def __init__(self, send_sems, recv_sems):
        self.send_sems, self.recv_sems = send_sems, recv_sems
        self.used = 0
        self.sent = []

    def copy(self, src, dst, device):
        i = self.used
        self.used += 1
        made = pltpu.make_async_remote_copy(
            src_ref=src,
            dst_ref=dst,
            send_sem=self.send_sems.at[i],
            recv_sem=self.recv_sems.at[i],
            device_id=device,
            device_id_type=pl.DeviceIdType.MESH,
        )
        self.sent.append(made)
        return made

    def drain(self):
        for made in self.sent:
            made.wait_send()


class RingGather:
    def __init__(self, links, right, left, own, at_right, at_left, from_left, from_right, on_right, on_left):
        self.first = [
            links.copy(own(0), at_right(0), right),
            links.copy(own(1), at_left(1), left),
            links.copy(own(1), at_right(1), right),
            links.copy(own(0), at_left(0), left),
        ]
        self.onward = [
            links.copy(from_left(0), on_right(0), right),
            links.copy(from_right(1), on_left(1), left),
        ]

    def begin(self):
        self.first[0].start()
        self.first[1].start()

    def follow(self):
        self.first[2].start()
        self.first[3].start()

    def start(self):
        self.begin()
        self.follow()

    def forward(self):
        self.first[0].wait_recv()
        self.onward[0].start()
        self.first[1].wait_recv()
        self.onward[1].start()

    def near(self):
        self.first[2].wait_recv()
        self.first[3].wait_recv()

    def far(self):
        self.onward[0].wait_recv()
        self.onward[1].wait_recv()

    def finish(self):
        self.near()
        self.far()


def body(
    hidden, seg, modulation, qk_gain, w_qkv, w_in, w_out, w_back,
    result,
    raw, xm, win, wback, kv, wqkv_v, wout_v, mod_v, gain_v, seg_x, qx, peak_v, part_out, part_in,
    act, mlp_out, mlp_in, z_out, z_in, gate_in,
    send_sems, recv_sems, local_sems,
):
    g = lax.axis_index("guide")
    s = lax.axis_index("seq")
    t = lax.axis_index("tp")
    x, y, c = s // 8, (s % 8) // 2, s % 2
    yr, yl = (y + 1) % 4, (y + 3) % 4

    def at_seq(xx, yy, cc):
        return {"seq": xx * 8 + yy * 2 + cc}

    x_right, x_left, x_far = at_seq((x + 1) % 4, y, c), at_seq((x + 3) % 4, y, c), at_seq((x + 2) % 4, y, c)
    y_right, y_left = at_seq(x, yr, c), at_seq(x, yl, c)
    mate = at_seq(x, y, 1 - c)
    t_right, t_left, t_far = {"tp": (t + 1) % 4}, {"tp": (t + 3) % 4}, {"tp": (t + 2) % 4}
    partner = {"guide": 1 - g}
    across = [{"guide": 1 - g, "tp": (t + step) % 4} for step in (1, 2, 3)]

    barrier = pltpu.get_barrier_semaphore()
    everyone = (x_right, x_left, x_far, y_right, y_left, mate, t_right, t_left, t_far, partner, *across)
    for device in everyone:
        pl.semaphore_signal(barrier, inc=1, device_id=device, device_id_type=pl.DeviceIdType.MESH)

    def columns(weight, dx, h=None):
        cols = pl.ds(pl.multiple_of(((x + dx) % 4) * GROUP, GROUP), GROUP)
        return weight.at[:, cols] if h is None else weight.at[pl.ds(h * 48, 48), cols]

    pairs = [
        (hidden, raw.at[0, 0]),
        (seg, seg_x.at[0]),
        (modulation, mod_v),
        (qk_gain, gain_v),
        (w_qkv.at[1], wqkv_v.at[1]),
        (w_qkv.at[2], wqkv_v.at[2]),
        (w_qkv.at[0], wqkv_v.at[0]),
        (columns(w_in, 0), win.at[0, y, c]),
        (w_back, wback.at[y, c]),
        (w_out, wout_v),
    ]
    local = [pltpu.make_async_copy(a, b, local_sems.at[i]) for i, (a, b) in enumerate(pairs)]
    for made in local:
        made.start()
    pl.semaphore_wait(barrier, len(everyone))

    links = Links(send_sems, recv_sems)
    half32 = lambda h: pl.ds(h * 32, 32)
    half48 = lambda h: pl.ds(h * 48, 48)
    two = lambda h: pl.ds(h * 2, 2)

    def relative(right, left, spot, own=None):
        spots = [(lambda d: (lambda h: spot(d, h)))(d) for d in (3, 1, 3, 1, 2, 2)]
        return RingGather(links, right, left, own or (lambda h: spot(0, h)), *spots)

    def absolute(spot, own=None):
        spots = [(lambda yy: (lambda h: spot(yy, h)))(yy) for yy in (y, y, yl, yr, yl, yr)]
        return RingGather(links, y_right, y_left, own or (lambda h: spot(y, h)), *spots)

    over_tp = relative(t_right, t_left, lambda d, h: raw.at[0, d, half32(h)], lambda h: hidden.at[half32(h)])
    over_x = [
        relative(
            x_right, x_left, (lambda k: (lambda d, h: raw.at[d, k, half32(h)]))(k),
            (lambda h: hidden.at[half32(h)]) if k == 0 else None,
        )
        for k in range(4)
    ]
    seg_sent = [
        links.copy(seg, seg_x.at[3], x_right),
        links.copy(seg, seg_x.at[1], x_left),
        links.copy(seg, seg_x.at[2], x_far),
    ]
    win_sent = [
        links.copy(columns(w_in, 1), win.at[2, y, c], x_right),
        links.copy(columns(w_in, 3), win.at[1, y, c], x_left),
        links.copy(columns(w_in, 2), win.at[3, y, c], x_far),
    ]
    win_near = absolute(lambda yy, h: win.at[0, yy, c, half48(h)], lambda h: columns(w_in, 0, h))
    win_sides = absolute(lambda yy, h: win.at[1:3, yy, c, half48(h)])
    win_rest = absolute(lambda yy, h: win.at[3, yy, c, half48(h)])
    wback_all = absolute(lambda yy, h: wback.at[yy, c, half48(h)], lambda h: w_back.at[half48(h)])

    def to_mate(spot):
        return links.copy(spot, spot, mate)

    over_first = to_mate(win.at[0, :, c])
    over_sides = [to_mate(win.at[1:3, yy, c]) for yy in (y, yr, yl, (y + 2) % 4)]
    over_rest = [to_mate(win.at[3, yy, c]) for yy in (y, yr, yl, (y + 2) % 4)]
    over_back = [to_mate(wback.at[yy, c]) for yy in (y, yr, yl, (y + 2) % 4)]
    kv_all = absolute(lambda yy, h: kv.at[yy, c, half32(h)])
    kv_over = links.copy(kv.at[:, c], kv.at[:, c], mate)
    q_all = relative(x_right, x_left, lambda d, h: qx.at[d, half32(h)])
    act_all = relative(x_right, x_left, lambda d, h: act.at[d, two(h)])

    gate_sent = links.copy(
        modulation.at[2, :, pl.ds(pl.multiple_of(t * WIDE + (1 - g) * GROUP, GROUP), GROUP)], gate_in, partner
    )

    over_tp.start()
    for made in win_sent:
        made.start()
    win_near.start()
    wback_all.begin()
    over_x[0].start()
    for made in seg_sent:
        made.start()
    gate_sent.start()

    win_near.forward()
    win_sent[0].wait_recv()
    win_sent[1].wait_recv()
    win_sides.start()
    over_sides[0].start()
    over_tp.forward()
    over_x[0].forward()
    win_sent[2].wait_recv()
    win_rest.start()
    over_rest[0].start()
    over_tp.near()
    over_x[3].start()
    over_x[1].start()
    win_sides.forward()
    for made in local[:4]:
        made.wait()
    for made in seg_sent:
        made.wait_recv()
    win_rest.forward()
    over_x[3].forward()
    over_x[1].forward()
    over_tp.far()
    over_x[2].start()

    at_row = lax.broadcasted_iota(jnp.int32, (ROWS, ROWS), 0)
    at_col = lax.broadcasted_iota(jnp.int32, (ROWS, ROWS), 1)
    lane = lax.broadcasted_iota(jnp.int32, (ROWS, HEAD), 1).astype(F32)

    def seg_column(d):
        row = jnp.broadcast_to(seg_x[d].astype(F32), (ROWS, ROWS))
        return jnp.sum(jnp.where(at_row == at_col, row, 0.0), axis=-1, keepdims=True)

    seg_cols = [seg_column(d) for d in range(4)]
    one_hots = [jnp.where(seg_cols[d] == lane, 1.0, 0.0).astype(BF16) for d in range(4)]

    def look_up(kind, offset, d):
        table = mod_v[kind, :, pl.ds(pl.multiple_of(offset, WIDE), WIDE)].astype(F32)
        found = jnp.broadcast_to(table[0:1], (ROWS, WIDE))
        for r in range(1, REQUESTS):
            found = jnp.where(seg_cols[d] == float(r), table[r : r + 1], found)
        return found

    def normalise(d):
        total = sum(jnp.sum(raw[d, k].astype(F32), axis=-1, keepdims=True) for k in range(4))
        mean = total * (1.0 / D)
        squares = jnp.zeros((ROWS, 1), F32)
        for k in range(4):
            centred = raw[d, k].astype(F32) - mean
            squares += jnp.sum(centred * centred, axis=-1, keepdims=True)
        scale_rows = lax.rsqrt(squares * (1.0 / D) + 1e-06)
        for k in range(4):
            offset = ((t + k) % 4) * WIDE
            normed = (raw[d, k].astype(F32) - mean) * scale_rows
            xm[d, :, pl.ds(pl.multiple_of(offset, WIDE), WIDE)] = (
                normed * (1.0 + look_up(1, offset, d)) + look_up(0, offset, d)
            ).astype(BF16)

    normalise(0)

    def head_norm(values, gain):
        return values * lax.rsqrt(jnp.mean(values * values, axis=-1, keepdims=True) + 1e-06) * gain

    rows_own = xm[0]
    local[4].wait()
    keys = dot(rows_own, wqkv_v[1])
    for h in range(HEADS_HERE):
        cols = slice(h * HEAD, (h + 1) * HEAD)
        kv[y, c, :, cols] = head_norm(keys[:, cols], gain_v[1:2, :]).astype(BF16)
    local[5].wait()
    kv[y, c, :, GROUP : 2 * GROUP] = dot(rows_own, wqkv_v[2]).astype(BF16)
    kv[y, c, :, 2 * GROUP :] = one_hots[0]
    kv_all.start()
    local[6].wait()
    query = dot(rows_own, wqkv_v[0])
    for h in range(HEADS_HERE):
        cols = slice(h * HEAD, (h + 1) * HEAD)
        qx[0, :, cols] = head_norm(query[:, cols], gain_v[0:1, :]).astype(BF16)
    q_all.start()

    over_x[2].forward()
    local[7].wait()
    win_near.finish()
    over_first.start()
    win_sides.near()
    over_sides[1].start()
    over_sides[2].start()
    win_rest.near()
    over_rest[1].start()
    over_rest[2].start()
    kv_all.forward()
    local[8].wait()
    over_back[0].start()
    wback_all.forward()
    wback_all.follow()
    win_sides.far()
    over_sides[3].start()
    win_rest.far()
    over_rest[3].start()
    q_all.forward()
    for k in (0, 1, 3, 2):
        over_x[k].finish()
    normalise(1)
    kv_all.finish()
    kv_over.start()
    normalise(3)
    normalise(2)
    for made in [over_first, *over_sides, *over_rest]:
        made.wait_recv()

    pre = jnp.zeros((4 * ROWS, GROUP), F32)
    for slot, d in enumerate((0, 1, 3, 2)):
        cols = pl.ds(pl.multiple_of(((x + d) % 4) * WIDE, WIDE), WIDE)
        pre += dot(xm[:, :, cols].reshape(4 * ROWS, WIDE), win[slot].reshape(WIDE, GROUP))
    acted = jax.nn.gelu(pre, approximate=True).astype(BF16)
    for d in range(4):
        act[0, (x + d) % 4] = acted[d * ROWS : (d + 1) * ROWS]
    act_all.start()

    q_all.finish()
    kv_over.wait_recv()

    seen = kv.reshape(8 * ROWS, KV)
    same = dot_t(jnp.concatenate(one_hots, axis=0), seen[:, 2 * GROUP :]) > 0.5
    lanes = lax.broadcasted_iota(jnp.int32, (4 * ROWS, HEAD), 1)
    stats = jnp.zeros((4 * ROWS, HEAD), F32)
    for h in range(HEADS_HERE):
        k_cols = slice(h * HEAD, (h + 1) * HEAD)
        v_cols = slice(GROUP + h * HEAD, GROUP + (h + 1) * HEAD)
        score = dot_t(qx[:, :, k_cols].reshape(4 * ROWS, HEAD), seen[:, k_cols]) * HEAD ** (-0.5)
        score = jnp.where(same, score, -1e30)
        peak_v[...] = jnp.broadcast_to(jnp.max(score, axis=-1, keepdims=True), (4 * ROWS, HEAD)).astype(BF16)
        peak = peak_v[:, 0:1].astype(F32)
        weight = jnp.where(same, jnp.exp(score - peak), 0.0)
        total = jnp.sum(weight, axis=-1, keepdims=True)
        summed = dot(weight.astype(BF16), seen[:, v_cols])
        part = (summed / jnp.where(total > 0.0, total, 1.0)).astype(BF16)
        part_out[:, :, k_cols] = part.reshape(4, ROWS, HEAD)
        upper = total.astype(BF16).astype(F32)
        stats = jnp.where(lanes == h, peak, stats)
        stats = jnp.where(lanes == 3 + h, upper, stats)
        stats = jnp.where(lanes == 6 + h, total - upper, stats)
        if h == 0:
            wback_all.near()
            over_back[1].start()
            over_back[2].start()
        if h == 1:
            act_all.forward()
    part_out[:, :, GROUP:] = stats.astype(BF16).reshape(4, ROWS, HEAD)
    part_sent = [
        links.copy(part_out.at[2], part_in.at[2], x_far),
        links.copy(part_out.at[1], part_in.at[3], x_right),
        links.copy(part_out.at[3], part_in.at[1], x_left),
    ]
    for made in part_sent:
        made.start()
    wback_all.far()
    over_back[3].start()
    for made in over_back:
        made.wait_recv()

    def back(d):
        cols = pl.ds(pl.multiple_of(((x + d) % 4) * GROUP, GROUP), GROUP)
        return dot_t(act[d].reshape(4 * ROWS, GROUP), wback[:, :, :, cols].reshape(WIDE, GROUP))

    fed = back(0)
    act_all.near()
    fed += back(1)
    fed += back(3)
    act_all.far()
    fed += back(2)
    for b in range(4):
        mlp_out[(b - x + 4) % 4] = fed[b * ROWS : (b + 1) * ROWS].astype(BF16)
    mlp_sent = {
        3: links.copy(mlp_out.at[1], mlp_in.at[3], x_right),
        1: links.copy(mlp_out.at[3], mlp_in.at[1], x_left),
        2: links.copy(mlp_out.at[2], mlp_in.at[2], x_far),
    }
    for made in mlp_sent.values():
        made.start()

    for made in part_sent:
        made.wait_recv()
    attended = []
    for h in range(HEADS_HERE):
        cols = slice(h * HEAD, (h + 1) * HEAD)
        parts = [part_out[0]] + [part_in[d] for d in (1, 2, 3)]
        stat = [p[:, GROUP:].astype(F32) for p in parts]
        top = stat[0][:, h : h + 1]
        for other in stat[1:]:
            top = jnp.maximum(top, other[:, h : h + 1])
        total = jnp.zeros((ROWS, 1), F32)
        summed = jnp.zeros((ROWS, HEAD), F32)
        for p, st in zip(parts, stat):
            share = jnp.exp(st[:, h : h + 1] - top) * (st[:, 3 + h : 4 + h] + st[:, 6 + h : 7 + h])
            total += share
            summed += share * p[:, cols].astype(F32)
        attended.append((summed / total).astype(BF16))
    attended = jnp.concatenate(attended, axis=1)
    local[9].wait()

    base = links.used
    own_cols = pl.ds(pl.multiple_of(g * GROUP, GROUP), GROUP)
    other_cols = pl.ds(pl.multiple_of((1 - g) * GROUP, GROUP), GROUP)

    def term_copy(d, kind, step):
        return pltpu.make_async_remote_copy(
            src_ref=z_out.at[d, :, (own_cols, other_cols)[kind]],
            dst_ref=z_in.at[kind, step],
            send_sem=send_sems.at[base + 4 * kind + step],
            recv_sem=recv_sems.at[base + 4 * kind + step],
            device_id={"guide": (g, 1 - g)[kind], "tp": (t + step) % 4},
            device_id_type=pl.DeviceIdType.MESH,
        )

    for d in (0, 1, 3, 2):
        e = (x + d) % 4
        step = (x + d - t + 4) % 4
        term = dot(attended, wout_v[:, pl.ds(pl.multiple_of(e * WIDE, WIDE), WIDE)])
        if d == 0:
            term += mlp_out[0].astype(F32)
        else:
            mlp_sent[d].wait_recv()
            term += mlp_in[d].astype(F32)
        z_out[d] = term.astype(BF16)
        term_copy(d, 1, step).start()

        @pl.when(step != 0)
        def _():
            term_copy(d, 0, step).start()

    gate_sent.wait_recv()
    own_table = mod_v[2, :, pl.ds(pl.multiple_of(t * WIDE + g * GROUP, GROUP), GROUP)].astype(F32)
    other_table = gate_in[...].astype(F32)

    def gate_of(table):
        found = jnp.broadcast_to(table[0:1], (ROWS, GROUP))
        for r in range(1, REQUESTS):
            found = jnp.where(seg_cols[0] == float(r), table[r : r + 1], found)
        return found

    own_gate, other_gate = gate_of(own_table), gate_of(other_table)
    residual = raw[0, 0, :, own_cols].astype(F32)
    own_branch = z_out[(t - x + 4) % 4, :, own_cols].astype(F32)
    arrived = [term_copy(0, 0, step) for step in (1, 2, 3)] + [term_copy(0, 1, step) for step in range(4)]
    for made in arrived:
        made.wait_recv()
    for step in (1, 2, 3):
        own_branch += z_in[0, step].astype(F32)
    other_branch = z_in[1, 0].astype(F32)
    for step in (1, 2, 3):
        other_branch += z_in[1, step].astype(F32)
    mine = (residual + own_gate * own_branch).astype(BF16).astype(F32)
    theirs = (residual + other_gate * other_branch).astype(BF16).astype(F32)
    cond = jnp.where(g == 0, mine, theirs)
    uncond = jnp.where(g == 0, theirs, mine)
    result[...] = (uncond + GUIDANCE * (cond - uncond)).astype(BF16)
    for made in arrived:
        made.wait_send()
    links.drain()


def on_device(hidden, seg_ids, modulation, qk_gain, w_qkv, w_mlp_in, w_out, w_mlp_back):
    anywhere = pl.BlockSpec(memory_space=pl.ANY)
    guided = pl.pallas_call(
        body,
        out_shape=jax.ShapeDtypeStruct((ROWS, GROUP), BF16),
        in_specs=[anywhere] * 8,
        out_specs=pl.BlockSpec(memory_space=pltpu.VMEM),
        scratch_shapes=[
            pltpu.VMEM((4, 4, ROWS, WIDE), BF16),
            pltpu.VMEM((4, ROWS, D), BF16),
            pltpu.VMEM((4, 4, 2, SLAB, GROUP), BF16),
            pltpu.VMEM((4, 2, SLAB, 4 * GROUP), BF16),
            pltpu.VMEM((4, 2, ROWS, KV), BF16),
            pltpu.VMEM((3, D, GROUP), BF16),
            pltpu.VMEM((GROUP, D), BF16),
            pltpu.VMEM((3, REQUESTS, D), BF16),
            pltpu.VMEM((2, HEAD), F32),
            pltpu.VMEM((4, 1, ROWS), jnp.int32),
            pltpu.VMEM((4, ROWS, GROUP), BF16),
            pltpu.VMEM((4 * ROWS, HEAD), BF16),
            pltpu.VMEM((4, ROWS, GROUP + HEAD), BF16),
            pltpu.VMEM((4, ROWS, GROUP + HEAD), BF16),
            pltpu.VMEM((4, 4, ROWS, GROUP), BF16),
            pltpu.VMEM((4, ROWS, WIDE), BF16),
            pltpu.VMEM((4, ROWS, WIDE), BF16),
            pltpu.VMEM((4, ROWS, WIDE), BF16),
            pltpu.VMEM((2, 4, ROWS, GROUP), BF16),
            pltpu.VMEM((REQUESTS, GROUP), BF16),
            pltpu.SemaphoreType.DMA((COPIES,)),
            pltpu.SemaphoreType.DMA((COPIES,)),
            pltpu.SemaphoreType.DMA((LOCALS,)),
        ],
        compiler_params=pltpu.CompilerParams(
            collective_id=0, has_side_effects=True, vmem_limit_bytes=60 * 1024 * 1024
        ),
        name="layer",
    )(
        hidden,
        seg_ids.reshape(1, ROWS),
        jnp.transpose(modulation[0], (1, 0, 2)),
        qk_gain,
        jnp.transpose(w_qkv, (1, 0, 2)),
        w_mlp_in,
        w_out,
        w_mlp_back,
    )
    return guided.reshape(ROWS, 1, 1, GROUP)


def solution(mesh):
    in_specs = (
        P("seq", "tp"),
        P("seq"),
        P("guide", None, None, None),
        P(),
        P(None, None, "tp"),
        P("seq", "tp"),
        P("tp", None),
        P("seq", "tp"),
    )
    out_specs = P("seq", "tp", "guide", None)
    return jax.shard_map(
        on_device, mesh=mesh, in_specs=in_specs, out_specs=out_specs, check_vma=False
    )
```

```python
import jax
import jax.numpy as jnp
from jax import lax
from jax.experimental import pallas as pl
from jax.experimental.pallas import tpu as pltpu
from jax.sharding import PartitionSpec as P

D = 3072
HEAD = 128
ROWS = 64
WIDE = 768
GROUP = 384
SLAB = 96
HEADS_HERE = 3
REQUESTS = 4
KV = 2 * GROUP + HEAD
GUIDANCE = 3.5
COPIES = 128
LOCALS = 10

F32 = jnp.float32
BF16 = jnp.bfloat16


def dot(a, b):
    return jnp.dot(a, b, preferred_element_type=F32)


def dot_t(a, b):
    return lax.dot_general(a, b, (((1,), (1,)), ((), ())), preferred_element_type=F32)


class Links:
    def __init__(self, send_sems, recv_sems):
        self.send_sems, self.recv_sems = send_sems, recv_sems
        self.used = 0
        self.sent = []

    def copy(self, src, dst, device):
        i = self.used
        self.used += 1
        made = pltpu.make_async_remote_copy(
            src_ref=src,
            dst_ref=dst,
            send_sem=self.send_sems.at[i],
            recv_sem=self.recv_sems.at[i],
            device_id=device,
            device_id_type=pl.DeviceIdType.MESH,
        )
        self.sent.append(made)
        return made

    def drain(self):
        for made in self.sent:
            made.wait_send()


class RingGather:
    def __init__(self, links, right, left, own, at_right, at_left, from_left, from_right, on_right, on_left):
        self.first = [
            links.copy(own(0), at_right(0), right),
            links.copy(own(1), at_left(1), left),
            links.copy(own(1), at_right(1), right),
            links.copy(own(0), at_left(0), left),
        ]
        self.onward = [
            links.copy(from_left(0), on_right(0), right),
            links.copy(from_right(1), on_left(1), left),
        ]

    def begin(self):
        self.first[0].start()
        self.first[1].start()

    def follow(self):
        self.first[2].start()
        self.first[3].start()

    def start(self):
        self.begin()
        self.follow()

    def forward(self):
        self.first[0].wait_recv()
        self.onward[0].start()
        self.first[1].wait_recv()
        self.onward[1].start()

    def near(self):
        self.first[2].wait_recv()
        self.first[3].wait_recv()

    def far(self):
        self.onward[0].wait_recv()
        self.onward[1].wait_recv()

    def finish(self):
        self.near()
        self.far()


def body(
    hidden, seg, modulation, qk_gain, w_qkv, w_in, w_out, w_back,
    result,
    raw, xm, win, wback, kv, wqkv_v, wout_v, mod_v, gain_v, seg_x, qx, peak_v, part_out, part_in,
    act, mlp_out, mlp_in, z_out, z_in, gate_in,
    send_sems, recv_sems, local_sems,
):
    g = lax.axis_index("guide")
    s = lax.axis_index("seq")
    t = lax.axis_index("tp")
    x, y, c = s // 8, (s % 8) // 2, s % 2
    yr, yl = (y + 1) % 4, (y + 3) % 4

    def at_seq(xx, yy, cc):
        return {"seq": xx * 8 + yy * 2 + cc}

    x_right, x_left, x_far = at_seq((x + 1) % 4, y, c), at_seq((x + 3) % 4, y, c), at_seq((x + 2) % 4, y, c)
    y_right, y_left = at_seq(x, yr, c), at_seq(x, yl, c)
    mate = at_seq(x, y, 1 - c)
    t_right, t_left, t_far = {"tp": (t + 1) % 4}, {"tp": (t + 3) % 4}, {"tp": (t + 2) % 4}
    partner = {"guide": 1 - g}
    across = [{"guide": 1 - g, "tp": (t + step) % 4} for step in (1, 2, 3)]

    barrier = pltpu.get_barrier_semaphore()
    everyone = (x_right, x_left, x_far, y_right, y_left, mate, t_right, t_left, t_far, partner, *across)
    for device in everyone:
        pl.semaphore_signal(barrier, inc=1, device_id=device, device_id_type=pl.DeviceIdType.MESH)

    def columns(weight, dx, h=None):
        cols = pl.ds(pl.multiple_of(((x + dx) % 4) * GROUP, GROUP), GROUP)
        return weight.at[:, cols] if h is None else weight.at[pl.ds(h * 48, 48), cols]

    pairs = [
        (hidden, raw.at[0, 0]),
        (seg, seg_x.at[0]),
        (modulation, mod_v),
        (qk_gain, gain_v),
        (w_qkv.at[1], wqkv_v.at[1]),
        (w_qkv.at[2], wqkv_v.at[2]),
        (w_qkv.at[0], wqkv_v.at[0]),
        (columns(w_in, 0), win.at[0, y, c]),
        (w_back, wback.at[y, c]),
        (w_out, wout_v),
    ]
    local = [pltpu.make_async_copy(a, b, local_sems.at[i]) for i, (a, b) in enumerate(pairs)]
    for made in local:
        made.start()
    pl.semaphore_wait(barrier, len(everyone))

    links = Links(send_sems, recv_sems)
    half32 = lambda h: pl.ds(h * 32, 32)
    half48 = lambda h: pl.ds(h * 48, 48)
    two = lambda h: pl.ds(h * 2, 2)

    def relative(right, left, spot, own=None):
        spots = [(lambda d: (lambda h: spot(d, h)))(d) for d in (3, 1, 3, 1, 2, 2)]
        return RingGather(links, right, left, own or (lambda h: spot(0, h)), *spots)

    def absolute(spot, own=None):
        spots = [(lambda yy: (lambda h: spot(yy, h)))(yy) for yy in (y, y, yl, yr, yl, yr)]
        return RingGather(links, y_right, y_left, own or (lambda h: spot(y, h)), *spots)

    over_tp = relative(t_right, t_left, lambda d, h: raw.at[0, d, half32(h)], lambda h: hidden.at[half32(h)])
    over_x = [
        relative(
            x_right, x_left, (lambda k: (lambda d, h: raw.at[d, k, half32(h)]))(k),
            (lambda h: hidden.at[half32(h)]) if k == 0 else None,
        )
        for k in range(4)
    ]
    seg_sent = [
        links.copy(seg, seg_x.at[3], x_right),
        links.copy(seg, seg_x.at[1], x_left),
        links.copy(seg, seg_x.at[2], x_far),
    ]
    win_sent = [
        links.copy(columns(w_in, 1), win.at[2, y, c], x_right),
        links.copy(columns(w_in, 3), win.at[1, y, c], x_left),
        links.copy(columns(w_in, 2), win.at[3, y, c], x_far),
    ]
    win_near = absolute(lambda yy, h: win.at[0, yy, c, half48(h)], lambda h: columns(w_in, 0, h))
    win_sides = absolute(lambda yy, h: win.at[1:3, yy, c, half48(h)])
    win_rest = absolute(lambda yy, h: win.at[3, yy, c, half48(h)])
    wback_all = absolute(lambda yy, h: wback.at[yy, c, half48(h)], lambda h: w_back.at[half48(h)])

    def to_mate(spot):
        return links.copy(spot, spot, mate)

    over_first = to_mate(win.at[0, :, c])
    over_sides = [to_mate(win.at[1:3, yy, c]) for yy in (y, yr, yl, (y + 2) % 4)]
    over_rest = [to_mate(win.at[3, yy, c]) for yy in (y, yr, yl, (y + 2) % 4)]
    over_back = [to_mate(wback.at[yy, c]) for yy in (y, yr, yl, (y + 2) % 4)]
    kv_all = absolute(lambda yy, h: kv.at[yy, c, half32(h)])
    over_kv = [to_mate(kv.at[yy, c]) for yy in (y, yr, yl, (y + 2) % 4)]
    q_all = relative(x_right, x_left, lambda d, h: qx.at[d, half32(h)])
    act_all = relative(x_right, x_left, lambda d, h: act.at[d, two(h)])

    gate_sent = links.copy(
        modulation.at[2, :, pl.ds(pl.multiple_of(t * WIDE + (1 - g) * GROUP, GROUP), GROUP)], gate_in, partner
    )

    over_tp.start()
    for made in win_sent:
        made.start()
    win_near.start()
    over_x[0].start()
    for made in seg_sent:
        made.start()
    gate_sent.start()

    win_near.forward()
    win_sent[0].wait_recv()
    win_sent[1].wait_recv()
    win_sides.start()
    over_sides[0].start()
    over_tp.forward()
    over_x[0].forward()
    win_sent[2].wait_recv()
    win_rest.start()
    over_rest[0].start()
    over_tp.near()
    over_x[3].start()
    over_x[1].start()
    win_sides.forward()
    for made in local[:4]:
        made.wait()
    for made in seg_sent:
        made.wait_recv()
    win_rest.forward()
    wback_all.begin()
    local[7].wait()
    win_near.finish()
    over_first.start()
    over_tp.far()
    over_x[2].start()

    at_row = lax.broadcasted_iota(jnp.int32, (ROWS, ROWS), 0)
    at_col = lax.broadcasted_iota(jnp.int32, (ROWS, ROWS), 1)
    lane = lax.broadcasted_iota(jnp.int32, (ROWS, HEAD), 1).astype(F32)

    def seg_column(d):
        row = jnp.broadcast_to(seg_x[d].astype(F32), (ROWS, ROWS))
        return jnp.sum(jnp.where(at_row == at_col, row, 0.0), axis=-1, keepdims=True)

    seg_cols = [seg_column(d) for d in range(4)]
    one_hots = [jnp.where(seg_cols[d] == lane, 1.0, 0.0).astype(BF16) for d in range(4)]

    def look_up(kind, offset, d):
        table = mod_v[kind, :, pl.ds(pl.multiple_of(offset, WIDE), WIDE)].astype(F32)
        found = jnp.broadcast_to(table[0:1], (ROWS, WIDE))
        for r in range(1, REQUESTS):
            found = jnp.where(seg_cols[d] == float(r), table[r : r + 1], found)
        return found

    def normalise(d):
        total = sum(jnp.sum(raw[d, k].astype(F32), axis=-1, keepdims=True) for k in range(4))
        mean = total * (1.0 / D)
        squares = jnp.zeros((ROWS, 1), F32)
        for k in range(4):
            centred = raw[d, k].astype(F32) - mean
            squares += jnp.sum(centred * centred, axis=-1, keepdims=True)
        scale_rows = lax.rsqrt(squares * (1.0 / D) + 1e-06)
        for k in range(4):
            offset = ((t + k) % 4) * WIDE
            normed = (raw[d, k].astype(F32) - mean) * scale_rows
            xm[d, :, pl.ds(pl.multiple_of(offset, WIDE), WIDE)] = (
                normed * (1.0 + look_up(1, offset, d)) + look_up(0, offset, d)
            ).astype(BF16)

    normalise(0)
    over_x[3].forward()
    over_x[1].forward()

    def head_norm(values, gain):
        return values * lax.rsqrt(jnp.mean(values * values, axis=-1, keepdims=True) + 1e-06) * gain

    rows_own = xm[0]
    local[4].wait()
    keys = dot(rows_own, wqkv_v[1])
    for h in range(HEADS_HERE):
        cols = slice(h * HEAD, (h + 1) * HEAD)
        kv[y, c, :, cols] = head_norm(keys[:, cols], gain_v[1:2, :]).astype(BF16)
    win_sides.near()
    over_sides[1].start()
    over_sides[2].start()
    local[5].wait()
    kv[y, c, :, GROUP : 2 * GROUP] = dot(rows_own, wqkv_v[2]).astype(BF16)
    kv[y, c, :, 2 * GROUP :] = one_hots[0]
    kv_all.start()
    over_kv[0].start()
    over_x[2].forward()
    win_rest.near()
    over_rest[1].start()
    over_rest[2].start()
    win_sides.far()
    over_sides[3].start()
    win_rest.far()
    over_rest[3].start()
    local[6].wait()
    query = dot(rows_own, wqkv_v[0])
    for h in range(HEADS_HERE):
        cols = slice(h * HEAD, (h + 1) * HEAD)
        qx[0, :, cols] = head_norm(query[:, cols], gain_v[0:1, :]).astype(BF16)
    q_all.start()

    kv_all.forward()
    wback_all.follow()
    local[8].wait()
    over_back[0].start()
    wback_all.forward()
    for k in (0, 1, 3, 2):
        over_x[k].finish()
    kv_all.near()
    over_kv[1].start()
    over_kv[2].start()
    normalise(1)
    q_all.forward()
    normalise(3)
    kv_all.far()
    over_kv[3].start()
    normalise(2)
    for made in [over_first, *over_sides, *over_rest]:
        made.wait_recv()

    pre = jnp.zeros((4 * ROWS, GROUP), F32)
    for slot, d in enumerate((0, 1, 3, 2)):
        cols = pl.ds(pl.multiple_of(((x + d) % 4) * WIDE, WIDE), WIDE)
        pre += dot(xm[:, :, cols].reshape(4 * ROWS, WIDE), win[slot].reshape(WIDE, GROUP))
    acted = jax.nn.gelu(pre, approximate=True).astype(BF16)
    for d in range(4):
        act[0, (x + d) % 4] = acted[d * ROWS : (d + 1) * ROWS]
    act_all.start()

    q_all.finish()
    for made in over_kv:
        made.wait_recv()

    seen = kv.reshape(8 * ROWS, KV)
    same = dot_t(jnp.concatenate(one_hots, axis=0), seen[:, 2 * GROUP :]) > 0.5
    lanes = lax.broadcasted_iota(jnp.int32, (4 * ROWS, HEAD), 1)
    stats = jnp.zeros((4 * ROWS, HEAD), F32)
    for h in range(HEADS_HERE):
        k_cols = slice(h * HEAD, (h + 1) * HEAD)
        v_cols = slice(GROUP + h * HEAD, GROUP + (h + 1) * HEAD)
        score = dot_t(qx[:, :, k_cols].reshape(4 * ROWS, HEAD), seen[:, k_cols]) * HEAD ** (-0.5)
        score = jnp.where(same, score, -1e30)
        peak_v[...] = jnp.broadcast_to(jnp.max(score, axis=-1, keepdims=True), (4 * ROWS, HEAD)).astype(BF16)
        peak = peak_v[:, 0:1].astype(F32)
        weight = jnp.where(same, jnp.exp(score - peak), 0.0)
        total = jnp.sum(weight, axis=-1, keepdims=True)
        summed = dot(weight.astype(BF16), seen[:, v_cols])
        part = (summed / jnp.where(total > 0.0, total, 1.0)).astype(BF16)
        part_out[:, :, k_cols] = part.reshape(4, ROWS, HEAD)
        upper = total.astype(BF16).astype(F32)
        stats = jnp.where(lanes == h, peak, stats)
        stats = jnp.where(lanes == 3 + h, upper, stats)
        stats = jnp.where(lanes == 6 + h, total - upper, stats)
        if h == 0:
            wback_all.near()
            over_back[1].start()
            over_back[2].start()
        if h == 1:
            act_all.forward()
    part_out[:, :, GROUP:] = stats.astype(BF16).reshape(4, ROWS, HEAD)
    part_sent = [
        links.copy(part_out.at[2], part_in.at[2], x_far),
        links.copy(part_out.at[1], part_in.at[3], x_right),
        links.copy(part_out.at[3], part_in.at[1], x_left),
    ]
    for made in part_sent:
        made.start()
    wback_all.far()
    over_back[3].start()
    for made in over_back:
        made.wait_recv()

    def back(d):
        cols = pl.ds(pl.multiple_of(((x + d) % 4) * GROUP, GROUP), GROUP)
        return dot_t(act[d].reshape(4 * ROWS, GROUP), wback[:, :, :, cols].reshape(WIDE, GROUP))

    fed = back(0)
    act_all.near()
    fed += back(1)
    fed += back(3)
    act_all.far()
    fed += back(2)
    for b in range(4):
        mlp_out[(b - x + 4) % 4] = fed[b * ROWS : (b + 1) * ROWS].astype(BF16)
    mlp_sent = {
        3: links.copy(mlp_out.at[1], mlp_in.at[3], x_right),
        1: links.copy(mlp_out.at[3], mlp_in.at[1], x_left),
        2: links.copy(mlp_out.at[2], mlp_in.at[2], x_far),
    }
    for made in mlp_sent.values():
        made.start()

    for made in part_sent:
        made.wait_recv()
    attended = []
    for h in range(HEADS_HERE):
        cols = slice(h * HEAD, (h + 1) * HEAD)
        parts = [part_out[0]] + [part_in[d] for d in (1, 2, 3)]
        stat = [p[:, GROUP:].astype(F32) for p in parts]
        top = stat[0][:, h : h + 1]
        for other in stat[1:]:
            top = jnp.maximum(top, other[:, h : h + 1])
        total = jnp.zeros((ROWS, 1), F32)
        summed = jnp.zeros((ROWS, HEAD), F32)
        for p, st in zip(parts, stat):
            share = jnp.exp(st[:, h : h + 1] - top) * (st[:, 3 + h : 4 + h] + st[:, 6 + h : 7 + h])
            total += share
            summed += share * p[:, cols].astype(F32)
        attended.append((summed / total).astype(BF16))
    attended = jnp.concatenate(attended, axis=1)
    local[9].wait()

    base = links.used
    own_cols = pl.ds(pl.multiple_of(g * GROUP, GROUP), GROUP)
    other_cols = pl.ds(pl.multiple_of((1 - g) * GROUP, GROUP), GROUP)

    def term_copy(d, kind, step):
        return pltpu.make_async_remote_copy(
            src_ref=z_out.at[d, :, (own_cols, other_cols)[kind]],
            dst_ref=z_in.at[kind, step],
            send_sem=send_sems.at[base + 4 * kind + step],
            recv_sem=recv_sems.at[base + 4 * kind + step],
            device_id={"guide": (g, 1 - g)[kind], "tp": (t + step) % 4},
            device_id_type=pl.DeviceIdType.MESH,
        )

    for d in (0, 1, 3, 2):
        e = (x + d) % 4
        step = (x + d - t + 4) % 4
        term = dot(attended, wout_v[:, pl.ds(pl.multiple_of(e * WIDE, WIDE), WIDE)])
        if d == 0:
            term += mlp_out[0].astype(F32)
        else:
            mlp_sent[d].wait_recv()
            term += mlp_in[d].astype(F32)
        z_out[d] = term.astype(BF16)
        term_copy(d, 1, step).start()

        @pl.when(step != 0)
        def _():
            term_copy(d, 0, step).start()

    gate_sent.wait_recv()
    own_table = mod_v[2, :, pl.ds(pl.multiple_of(t * WIDE + g * GROUP, GROUP), GROUP)].astype(F32)
    other_table = gate_in[...].astype(F32)

    def gate_of(table):
        found = jnp.broadcast_to(table[0:1], (ROWS, GROUP))
        for r in range(1, REQUESTS):
            found = jnp.where(seg_cols[0] == float(r), table[r : r + 1], found)
        return found

    own_gate, other_gate = gate_of(own_table), gate_of(other_table)
    residual = raw[0, 0, :, own_cols].astype(F32)
    own_branch = z_out[(t - x + 4) % 4, :, own_cols].astype(F32)
    arrived = [term_copy(0, 0, step) for step in (1, 2, 3)] + [term_copy(0, 1, step) for step in range(4)]
    for made in arrived:
        made.wait_recv()
    for step in (1, 2, 3):
        own_branch += z_in[0, step].astype(F32)
    other_branch = z_in[1, 0].astype(F32)
    for step in (1, 2, 3):
        other_branch += z_in[1, step].astype(F32)
    mine = (residual + own_gate * own_branch).astype(BF16).astype(F32)
    theirs = (residual + other_gate * other_branch).astype(BF16).astype(F32)
    cond = jnp.where(g == 0, mine, theirs)
    uncond = jnp.where(g == 0, theirs, mine)
    result[...] = (uncond + GUIDANCE * (cond - uncond)).astype(BF16)
    for made in arrived:
        made.wait_send()
    links.drain()


def on_device(hidden, seg_ids, modulation, qk_gain, w_qkv, w_mlp_in, w_out, w_mlp_back):
    anywhere = pl.BlockSpec(memory_space=pl.ANY)
    guided = pl.pallas_call(
        body,
        out_shape=jax.ShapeDtypeStruct((ROWS, GROUP), BF16),
        in_specs=[anywhere] * 8,
        out_specs=pl.BlockSpec(memory_space=pltpu.VMEM),
        scratch_shapes=[
            pltpu.VMEM((4, 4, ROWS, WIDE), BF16),
            pltpu.VMEM((4, ROWS, D), BF16),
            pltpu.VMEM((4, 4, 2, SLAB, GROUP), BF16),
            pltpu.VMEM((4, 2, SLAB, 4 * GROUP), BF16),
            pltpu.VMEM((4, 2, ROWS, KV), BF16),
            pltpu.VMEM((3, D, GROUP), BF16),
            pltpu.VMEM((GROUP, D), BF16),
            pltpu.VMEM((3, REQUESTS, D), BF16),
            pltpu.VMEM((2, HEAD), F32),
            pltpu.VMEM((4, 1, ROWS), jnp.int32),
            pltpu.VMEM((4, ROWS, GROUP), BF16),
            pltpu.VMEM((4 * ROWS, HEAD), BF16),
            pltpu.VMEM((4, ROWS, GROUP + HEAD), BF16),
            pltpu.VMEM((4, ROWS, GROUP + HEAD), BF16),
            pltpu.VMEM((4, 4, ROWS, GROUP), BF16),
            pltpu.VMEM((4, ROWS, WIDE), BF16),
            pltpu.VMEM((4, ROWS, WIDE), BF16),
            pltpu.VMEM((4, ROWS, WIDE), BF16),
            pltpu.VMEM((2, 4, ROWS, GROUP), BF16),
            pltpu.VMEM((REQUESTS, GROUP), BF16),
            pltpu.SemaphoreType.DMA((COPIES,)),
            pltpu.SemaphoreType.DMA((COPIES,)),
            pltpu.SemaphoreType.DMA((LOCALS,)),
        ],
        compiler_params=pltpu.CompilerParams(
            collective_id=0, has_side_effects=True, vmem_limit_bytes=60 * 1024 * 1024
        ),
        name="layer",
    )(
        hidden,
        seg_ids.reshape(1, ROWS),
        jnp.transpose(modulation[0], (1, 0, 2)),
        qk_gain,
        jnp.transpose(w_qkv, (1, 0, 2)),
        w_mlp_in,
        w_out,
        w_mlp_back,
    )
    return guided.reshape(ROWS, 1, 1, GROUP)


def solution(mesh):
    in_specs = (
        P("seq", "tp"),
        P("seq"),
        P("guide", None, None, None),
        P(),
        P(None, None, "tp"),
        P("seq", "tp"),
        P("tp", None),
        P("seq", "tp"),
    )
    out_specs = P("seq", "tp", "guide", None)
    return jax.shard_map(
        on_device, mesh=mesh, in_specs=in_specs, out_specs=out_specs, check_vma=False
    )
```

```python
import jax
import jax.numpy as jnp
from jax import lax
from jax.experimental import pallas as pl
from jax.experimental.pallas import tpu as pltpu
from jax.sharding import PartitionSpec as P

D = 3072
HEAD = 128
ROWS = 64
WIDE = 768
GROUP = 384
SLAB = 96
HEADS_HERE = 3
REQUESTS = 4
KV = 2 * GROUP + HEAD
GUIDANCE = 3.5
COPIES = 128
LOCALS = 10

F32 = jnp.float32
BF16 = jnp.bfloat16


def dot(a, b):
    return jnp.dot(a, b, preferred_element_type=F32)


def dot_t(a, b):
    return lax.dot_general(a, b, (((1,), (1,)), ((), ())), preferred_element_type=F32)


class Links:
    def __init__(self, send_sems, recv_sems):
        self.send_sems, self.recv_sems = send_sems, recv_sems
        self.used = 0
        self.sent = []

    def copy(self, src, dst, device):
        i = self.used
        self.used += 1
        made = pltpu.make_async_remote_copy(
            src_ref=src,
            dst_ref=dst,
            send_sem=self.send_sems.at[i],
            recv_sem=self.recv_sems.at[i],
            device_id=device,
            device_id_type=pl.DeviceIdType.MESH,
        )
        self.sent.append(made)
        return made

    def drain(self):
        for made in self.sent:
            made.wait_send()


class RingGather:
    def __init__(self, links, right, left, own, at_right, at_left, from_left, from_right, on_right, on_left):
        self.first = [
            links.copy(own(0), at_right(0), right),
            links.copy(own(1), at_left(1), left),
            links.copy(own(1), at_right(1), right),
            links.copy(own(0), at_left(0), left),
        ]
        self.onward = [
            links.copy(from_left(0), on_right(0), right),
            links.copy(from_right(1), on_left(1), left),
        ]

    def begin(self):
        self.first[0].start()
        self.first[1].start()

    def follow(self):
        self.first[2].start()
        self.first[3].start()

    def start(self):
        self.begin()
        self.follow()

    def forward(self):
        self.first[0].wait_recv()
        self.onward[0].start()
        self.first[1].wait_recv()
        self.onward[1].start()

    def near(self):
        self.first[2].wait_recv()
        self.first[3].wait_recv()

    def far(self):
        self.onward[0].wait_recv()
        self.onward[1].wait_recv()

    def finish(self):
        self.near()
        self.far()


def body(
    hidden, seg, modulation, qk_gain, w_qkv, w_in, w_out, w_back,
    result,
    raw, xm, win, wback, kv, wqkv_v, wout_v, mod_v, gain_v, seg_x, qx, peak_v, part_out, part_in,
    act, mlp_out, mlp_in, z_out, z_in, gate_in,
    send_sems, recv_sems, local_sems,
):
    g = lax.axis_index("guide")
    s = lax.axis_index("seq")
    t = lax.axis_index("tp")
    x, y, c = s // 8, (s % 8) // 2, s % 2
    yr, yl = (y + 1) % 4, (y + 3) % 4

    def at_seq(xx, yy, cc):
        return {"seq": xx * 8 + yy * 2 + cc}

    x_right, x_left, x_far = at_seq((x + 1) % 4, y, c), at_seq((x + 3) % 4, y, c), at_seq((x + 2) % 4, y, c)
    y_right, y_left = at_seq(x, yr, c), at_seq(x, yl, c)
    mate = at_seq(x, y, 1 - c)
    t_right, t_left, t_far = {"tp": (t + 1) % 4}, {"tp": (t + 3) % 4}, {"tp": (t + 2) % 4}
    partner = {"guide": 1 - g}
    across = [{"guide": 1 - g, "tp": (t + step) % 4} for step in (1, 2, 3)]

    barrier = pltpu.get_barrier_semaphore()
    everyone = (x_right, x_left, x_far, y_right, y_left, mate, t_right, t_left, t_far, partner, *across)
    for device in everyone:
        pl.semaphore_signal(barrier, inc=1, device_id=device, device_id_type=pl.DeviceIdType.MESH)

    def columns(weight, dx, h=None):
        cols = pl.ds(pl.multiple_of(((x + dx) % 4) * GROUP, GROUP), GROUP)
        return weight.at[:, cols] if h is None else weight.at[pl.ds(h * 48, 48), cols]

    pairs = [
        (hidden, raw.at[0, 0]),
        (seg, seg_x.at[0]),
        (modulation, mod_v),
        (qk_gain, gain_v),
        (w_qkv.at[1], wqkv_v.at[1]),
        (w_qkv.at[2], wqkv_v.at[2]),
        (w_qkv.at[0], wqkv_v.at[0]),
        (columns(w_in, 0), win.at[0, y, c]),
        (w_back, wback.at[y, c]),
        (w_out, wout_v),
    ]
    local = [pltpu.make_async_copy(a, b, local_sems.at[i]) for i, (a, b) in enumerate(pairs)]
    for made in local:
        made.start()
    pl.semaphore_wait(barrier, len(everyone))

    links = Links(send_sems, recv_sems)
    half32 = lambda h: pl.ds(h * 32, 32)
    half48 = lambda h: pl.ds(h * 48, 48)
    two = lambda h: pl.ds(h * 2, 2)

    def relative(right, left, spot, own=None):
        spots = [(lambda d: (lambda h: spot(d, h)))(d) for d in (3, 1, 3, 1, 2, 2)]
        return RingGather(links, right, left, own or (lambda h: spot(0, h)), *spots)

    def absolute(spot, own=None):
        spots = [(lambda yy: (lambda h: spot(yy, h)))(yy) for yy in (y, y, yl, yr, yl, yr)]
        return RingGather(links, y_right, y_left, own or (lambda h: spot(y, h)), *spots)

    over_tp = relative(t_right, t_left, lambda d, h: raw.at[0, d, half32(h)], lambda h: hidden.at[half32(h)])
    over_x = [
        relative(
            x_right, x_left, (lambda k: (lambda d, h: raw.at[d, k, half32(h)]))(k),
            (lambda h: hidden.at[half32(h)]) if k == 0 else None,
        )
        for k in range(4)
    ]
    seg_sent = [
        links.copy(seg, seg_x.at[3], x_right),
        links.copy(seg, seg_x.at[1], x_left),
        links.copy(seg, seg_x.at[2], x_far),
    ]
    win_sent = [
        links.copy(columns(w_in, 1), win.at[2, y, c], x_right),
        links.copy(columns(w_in, 3), win.at[1, y, c], x_left),
        links.copy(columns(w_in, 2), win.at[3, y, c], x_far),
    ]
    win_near = absolute(lambda yy, h: win.at[0, yy, c, half48(h)], lambda h: columns(w_in, 0, h))
    win_sides = absolute(lambda yy, h: win.at[1:3, yy, c, half48(h)])
    win_rest = absolute(lambda yy, h: win.at[3, yy, c, half48(h)])
    wback_all = absolute(lambda yy, h: wback.at[yy, c, half48(h)], lambda h: w_back.at[half48(h)])

    def to_mate(spot):
        return links.copy(spot, spot, mate)

    over_first = to_mate(win.at[0, :, c])
    over_sides = [to_mate(win.at[1:3, yy, c]) for yy in (y, yr, yl, (y + 2) % 4)]
    over_rest = [to_mate(win.at[3, yy, c]) for yy in (y, yr, yl, (y + 2) % 4)]
    over_back = [to_mate(wback.at[yy, c]) for yy in (y, yr, yl, (y + 2) % 4)]
    kv_all = absolute(lambda yy, h: kv.at[yy, c, half32(h)])
    kv_over = links.copy(kv.at[:, c], kv.at[:, c], mate)
    q_all = relative(x_right, x_left, lambda d, h: qx.at[d, half32(h)])
    act_all = relative(x_right, x_left, lambda d, h: act.at[d, two(h)])

    gate_sent = links.copy(
        modulation.at[2, :, pl.ds(pl.multiple_of(t * WIDE + (1 - g) * GROUP, GROUP), GROUP)], gate_in, partner
    )

    over_tp.start()
    for made in win_sent:
        made.start()
    win_near.start()
    over_x[0].start()
    for made in seg_sent:
        made.start()
    gate_sent.start()

    win_near.forward()
    win_sent[0].wait_recv()
    win_sent[1].wait_recv()
    win_sides.start()
    over_sides[0].start()
    over_tp.forward()
    over_x[0].forward()
    win_sent[2].wait_recv()
    win_rest.start()
    over_rest[0].start()
    over_tp.near()
    over_x[3].start()
    over_x[1].start()
    win_sides.forward()
    for made in local[:4]:
        made.wait()
    for made in seg_sent:
        made.wait_recv()
    win_rest.forward()
    local[7].wait()
    win_near.finish()
    over_first.start()
    over_tp.far()
    over_x[2].start()

    at_row = lax.broadcasted_iota(jnp.int32, (ROWS, ROWS), 0)
    at_col = lax.broadcasted_iota(jnp.int32, (ROWS, ROWS), 1)
    lane = lax.broadcasted_iota(jnp.int32, (ROWS, HEAD), 1).astype(F32)

    def seg_column(d):
        row = jnp.broadcast_to(seg_x[d].astype(F32), (ROWS, ROWS))
        return jnp.sum(jnp.where(at_row == at_col, row, 0.0), axis=-1, keepdims=True)

    seg_cols = [seg_column(d) for d in range(4)]
    one_hots = [jnp.where(seg_cols[d] == lane, 1.0, 0.0).astype(BF16) for d in range(4)]

    def look_up(kind, offset, d):
        table = mod_v[kind, :, pl.ds(pl.multiple_of(offset, WIDE), WIDE)].astype(F32)
        found = jnp.broadcast_to(table[0:1], (ROWS, WIDE))
        for r in range(1, REQUESTS):
            found = jnp.where(seg_cols[d] == float(r), table[r : r + 1], found)
        return found

    def normalise(d):
        total = sum(jnp.sum(raw[d, k].astype(F32), axis=-1, keepdims=True) for k in range(4))
        mean = total * (1.0 / D)
        squares = jnp.zeros((ROWS, 1), F32)
        for k in range(4):
            centred = raw[d, k].astype(F32) - mean
            squares += jnp.sum(centred * centred, axis=-1, keepdims=True)
        scale_rows = lax.rsqrt(squares * (1.0 / D) + 1e-06)
        for k in range(4):
            offset = ((t + k) % 4) * WIDE
            normed = (raw[d, k].astype(F32) - mean) * scale_rows
            xm[d, :, pl.ds(pl.multiple_of(offset, WIDE), WIDE)] = (
                normed * (1.0 + look_up(1, offset, d)) + look_up(0, offset, d)
            ).astype(BF16)

    normalise(0)
    over_x[3].forward()
    over_x[1].forward()

    def head_norm(values, gain):
        return values * lax.rsqrt(jnp.mean(values * values, axis=-1, keepdims=True) + 1e-06) * gain

    rows_own = xm[0]
    local[4].wait()
    keys = dot(rows_own, wqkv_v[1])
    for h in range(HEADS_HERE):
        cols = slice(h * HEAD, (h + 1) * HEAD)
        kv[y, c, :, cols] = head_norm(keys[:, cols], gain_v[1:2, :]).astype(BF16)
    win_sides.near()
    over_sides[1].start()
    over_sides[2].start()
    local[5].wait()
    kv[y, c, :, GROUP : 2 * GROUP] = dot(rows_own, wqkv_v[2]).astype(BF16)
    kv[y, c, :, 2 * GROUP :] = one_hots[0]
    kv_all.start()
    wback_all.begin()
    over_x[2].forward()
    win_rest.near()
    over_rest[1].start()
    over_rest[2].start()
    win_sides.far()
    over_sides[3].start()
    win_rest.far()
    over_rest[3].start()
    local[6].wait()
    query = dot(rows_own, wqkv_v[0])
    for h in range(HEADS_HERE):
        cols = slice(h * HEAD, (h + 1) * HEAD)
        qx[0, :, cols] = head_norm(query[:, cols], gain_v[0:1, :]).astype(BF16)
    q_all.start()

    kv_all.forward()
    wback_all.follow()
    local[8].wait()
    over_back[0].start()
    wback_all.forward()
    for k in (0, 1, 3, 2):
        over_x[k].finish()
    normalise(1)
    q_all.forward()
    normalise(3)
    kv_all.finish()
    kv_over.start()
    normalise(2)
    for made in [over_first, *over_sides, *over_rest]:
        made.wait_recv()

    pre = jnp.zeros((4 * ROWS, GROUP), F32)
    for slot, d in enumerate((0, 1, 3, 2)):
        cols = pl.ds(pl.multiple_of(((x + d) % 4) * WIDE, WIDE), WIDE)
        pre += dot(xm[:, :, cols].reshape(4 * ROWS, WIDE), win[slot].reshape(WIDE, GROUP))
    acted = jax.nn.gelu(pre, approximate=True).astype(BF16)
    for d in range(4):
        act[0, (x + d) % 4] = acted[d * ROWS : (d + 1) * ROWS]
    act_all.start()

    q_all.finish()
    kv_over.wait_recv()

    seen = kv.reshape(8 * ROWS, KV)
    same = dot_t(jnp.concatenate(one_hots, axis=0), seen[:, 2 * GROUP :]) > 0.5
    lanes = lax.broadcasted_iota(jnp.int32, (4 * ROWS, HEAD), 1)
    stats = jnp.zeros((4 * ROWS, HEAD), F32)
    for h in range(HEADS_HERE):
        k_cols = slice(h * HEAD, (h + 1) * HEAD)
        v_cols = slice(GROUP + h * HEAD, GROUP + (h + 1) * HEAD)
        score = dot_t(qx[:, :, k_cols].reshape(4 * ROWS, HEAD), seen[:, k_cols]) * HEAD ** (-0.5)
        score = jnp.where(same, score, -1e30)
        peak_v[...] = jnp.broadcast_to(jnp.max(score, axis=-1, keepdims=True), (4 * ROWS, HEAD)).astype(BF16)
        peak = peak_v[:, 0:1].astype(F32)
        weight = jnp.where(same, jnp.exp(score - peak), 0.0)
        total = jnp.sum(weight, axis=-1, keepdims=True)
        summed = dot(weight.astype(BF16), seen[:, v_cols])
        part = (summed / jnp.where(total > 0.0, total, 1.0)).astype(BF16)
        part_out[:, :, k_cols] = part.reshape(4, ROWS, HEAD)
        upper = total.astype(BF16).astype(F32)
        stats = jnp.where(lanes == h, peak, stats)
        stats = jnp.where(lanes == 3 + h, upper, stats)
        stats = jnp.where(lanes == 6 + h, total - upper, stats)
        if h == 0:
            wback_all.near()
            over_back[1].start()
            over_back[2].start()
        if h == 1:
            act_all.forward()
    part_out[:, :, GROUP:] = stats.astype(BF16).reshape(4, ROWS, HEAD)
    part_sent = [
        links.copy(part_out.at[2], part_in.at[2], x_far),
        links.copy(part_out.at[1], part_in.at[3], x_right),
        links.copy(part_out.at[3], part_in.at[1], x_left),
    ]
    for made in part_sent:
        made.start()
    wback_all.far()
    over_back[3].start()
    for made in over_back:
        made.wait_recv()

    def back(d):
        cols = pl.ds(pl.multiple_of(((x + d) % 4) * GROUP, GROUP), GROUP)
        return dot_t(act[d].reshape(4 * ROWS, GROUP), wback[:, :, :, cols].reshape(WIDE, GROUP))

    fed = back(0)
    act_all.near()
    fed += back(1)
    fed += back(3)
    act_all.far()
    fed += back(2)
    for b in range(4):
        mlp_out[(b - x + 4) % 4] = fed[b * ROWS : (b + 1) * ROWS].astype(BF16)
    mlp_sent = {
        3: links.copy(mlp_out.at[1], mlp_in.at[3], x_right),
        1: links.copy(mlp_out.at[3], mlp_in.at[1], x_left),
        2: links.copy(mlp_out.at[2], mlp_in.at[2], x_far),
    }
    for made in mlp_sent.values():
        made.start()

    for made in part_sent:
        made.wait_recv()
    attended = []
    for h in range(HEADS_HERE):
        cols = slice(h * HEAD, (h + 1) * HEAD)
        parts = [part_out[0]] + [part_in[d] for d in (1, 2, 3)]
        stat = [p[:, GROUP:].astype(F32) for p in parts]
        top = stat[0][:, h : h + 1]
        for other in stat[1:]:
            top = jnp.maximum(top, other[:, h : h + 1])
        total = jnp.zeros((ROWS, 1), F32)
        summed = jnp.zeros((ROWS, HEAD), F32)
        for p, st in zip(parts, stat):
            share = jnp.exp(st[:, h : h + 1] - top) * (st[:, 3 + h : 4 + h] + st[:, 6 + h : 7 + h])
            total += share
            summed += share * p[:, cols].astype(F32)
        attended.append((summed / total).astype(BF16))
    attended = jnp.concatenate(attended, axis=1)
    local[9].wait()

    base = links.used
    own_cols = pl.ds(pl.multiple_of(g * GROUP, GROUP), GROUP)
    other_cols = pl.ds(pl.multiple_of((1 - g) * GROUP, GROUP), GROUP)

    def term_copy(d, kind, step):
        return pltpu.make_async_remote_copy(
            src_ref=z_out.at[d, :, (own_cols, other_cols)[kind]],
            dst_ref=z_in.at[kind, step],
            send_sem=send_sems.at[base + 4 * kind + step],
            recv_sem=recv_sems.at[base + 4 * kind + step],
            device_id={"guide": (g, 1 - g)[kind], "tp": (t + step) % 4},
            device_id_type=pl.DeviceIdType.MESH,
        )

    for d in (0, 1, 3, 2):
        e = (x + d) % 4
        step = (x + d - t + 4) % 4
        term = dot(attended, wout_v[:, pl.ds(pl.multiple_of(e * WIDE, WIDE), WIDE)])
        if d == 0:
            term += mlp_out[0].astype(F32)
        else:
            mlp_sent[d].wait_recv()
            term += mlp_in[d].astype(F32)
        z_out[d] = term.astype(BF16)
        term_copy(d, 1, step).start()

        @pl.when(step != 0)
        def _():
            term_copy(d, 0, step).start()

    gate_sent.wait_recv()
    own_table = mod_v[2, :, pl.ds(pl.multiple_of(t * WIDE + g * GROUP, GROUP), GROUP)].astype(F32)
    other_table = gate_in[...].astype(F32)

    def gate_of(table):
        found = jnp.broadcast_to(table[0:1], (ROWS, GROUP))
        for r in range(1, REQUESTS):
            found = jnp.where(seg_cols[0] == float(r), table[r : r + 1], found)
        return found

    own_gate, other_gate = gate_of(own_table), gate_of(other_table)
    residual = raw[0, 0, :, own_cols].astype(F32)
    own_branch = z_out[(t - x + 4) % 4, :, own_cols].astype(F32)
    arrived = [term_copy(0, 0, step) for step in (1, 2, 3)] + [term_copy(0, 1, step) for step in range(4)]
    for made in arrived:
        made.wait_recv()
    for step in (1, 2, 3):
        own_branch += z_in[0, step].astype(F32)
    other_branch = z_in[1, 0].astype(F32)
    for step in (1, 2, 3):
        other_branch += z_in[1, step].astype(F32)
    mine = (residual + own_gate * own_branch).astype(BF16).astype(F32)
    theirs = (residual + other_gate * other_branch).astype(BF16).astype(F32)
    cond = jnp.where(g == 0, mine, theirs)
    uncond = jnp.where(g == 0, theirs, mine)
    result[...] = (uncond + GUIDANCE * (cond - uncond)).astype(BF16)
    for made in arrived:
        made.wait_send()
    links.drain()


def on_device(hidden, seg_ids, modulation, qk_gain, w_qkv, w_mlp_in, w_out, w_mlp_back):
    anywhere = pl.BlockSpec(memory_space=pl.ANY)
    guided = pl.pallas_call(
        body,
        out_shape=jax.ShapeDtypeStruct((ROWS, GROUP), BF16),
        in_specs=[anywhere] * 8,
        out_specs=pl.BlockSpec(memory_space=pltpu.VMEM),
        scratch_shapes=[
            pltpu.VMEM((4, 4, ROWS, WIDE), BF16),
            pltpu.VMEM((4, ROWS, D), BF16),
            pltpu.VMEM((4, 4, 2, SLAB, GROUP), BF16),
            pltpu.VMEM((4, 2, SLAB, 4 * GROUP), BF16),
            pltpu.VMEM((4, 2, ROWS, KV), BF16),
            pltpu.VMEM((3, D, GROUP), BF16),
            pltpu.VMEM((GROUP, D), BF16),
            pltpu.VMEM((3, REQUESTS, D), BF16),
            pltpu.VMEM((2, HEAD), F32),
            pltpu.VMEM((4, 1, ROWS), jnp.int32),
            pltpu.VMEM((4, ROWS, GROUP), BF16),
            pltpu.VMEM((4 * ROWS, HEAD), BF16),
            pltpu.VMEM((4, ROWS, GROUP + HEAD), BF16),
            pltpu.VMEM((4, ROWS, GROUP + HEAD), BF16),
            pltpu.VMEM((4, 4, ROWS, GROUP), BF16),
            pltpu.VMEM((4, ROWS, WIDE), BF16),
            pltpu.VMEM((4, ROWS, WIDE), BF16),
            pltpu.VMEM((4, ROWS, WIDE), BF16),
            pltpu.VMEM((2, 4, ROWS, GROUP), BF16),
            pltpu.VMEM((REQUESTS, GROUP), BF16),
            pltpu.SemaphoreType.DMA((COPIES,)),
            pltpu.SemaphoreType.DMA((COPIES,)),
            pltpu.SemaphoreType.DMA((LOCALS,)),
        ],
        compiler_params=pltpu.CompilerParams(
            collective_id=0, has_side_effects=True, vmem_limit_bytes=60 * 1024 * 1024
        ),
        name="layer",
    )(
        hidden,
        seg_ids.reshape(1, ROWS),
        jnp.transpose(modulation[0], (1, 0, 2)),
        qk_gain,
        jnp.transpose(w_qkv, (1, 0, 2)),
        w_mlp_in,
        w_out,
        w_mlp_back,
    )
    return guided.reshape(ROWS, 1, 1, GROUP)


def solution(mesh):
    in_specs = (
        P("seq", "tp"),
        P("seq"),
        P("guide", None, None, None),
        P(),
        P(None, None, "tp"),
        P("seq", "tp"),
        P("tp", None),
        P("seq", "tp"),
    )
    out_specs = P("seq", "tp", "guide", None)
    return jax.shard_map(
        on_device, mesh=mesh, in_specs=in_specs, out_specs=out_specs, check_vma=False
    )
```

```python
import jax
import jax.numpy as jnp
from jax import lax
from jax.experimental import pallas as pl
from jax.experimental.pallas import tpu as pltpu
from jax.sharding import PartitionSpec as P

D = 3072
HEAD = 128
ROWS = 64
WIDE = 768
GROUP = 384
SLAB = 96
HEADS_HERE = 3
REQUESTS = 4
KV = 2 * GROUP + HEAD
GUIDANCE = 3.5
COPIES = 128
LOCALS = 10

F32 = jnp.float32
BF16 = jnp.bfloat16


def dot(a, b):
    return jnp.dot(a, b, preferred_element_type=F32)


def dot_t(a, b):
    return lax.dot_general(a, b, (((1,), (1,)), ((), ())), preferred_element_type=F32)


class Links:
    def __init__(self, send_sems, recv_sems):
        self.send_sems, self.recv_sems = send_sems, recv_sems
        self.used = 0
        self.sent = []

    def copy(self, src, dst, device):
        i = self.used
        self.used += 1
        made = pltpu.make_async_remote_copy(
            src_ref=src,
            dst_ref=dst,
            send_sem=self.send_sems.at[i],
            recv_sem=self.recv_sems.at[i],
            device_id=device,
            device_id_type=pl.DeviceIdType.MESH,
        )
        self.sent.append(made)
        return made

    def drain(self):
        for made in self.sent:
            made.wait_send()


class RingGather:
    def __init__(self, links, right, left, own, at_right, at_left, from_left, from_right, on_right, on_left):
        self.first = [
            links.copy(own(0), at_right(0), right),
            links.copy(own(1), at_left(1), left),
            links.copy(own(1), at_right(1), right),
            links.copy(own(0), at_left(0), left),
        ]
        self.onward = [
            links.copy(from_left(0), on_right(0), right),
            links.copy(from_right(1), on_left(1), left),
        ]

    def begin(self):
        self.first[0].start()
        self.first[1].start()

    def follow(self):
        self.first[2].start()
        self.first[3].start()

    def start(self):
        self.begin()
        self.follow()

    def forward(self):
        self.first[0].wait_recv()
        self.onward[0].start()
        self.first[1].wait_recv()
        self.onward[1].start()

    def near(self):
        self.first[2].wait_recv()
        self.first[3].wait_recv()

    def far(self):
        self.onward[0].wait_recv()
        self.onward[1].wait_recv()

    def finish(self):
        self.near()
        self.far()


def body(
    hidden, seg, modulation, qk_gain, w_qkv, w_in, w_out, w_back,
    result,
    raw, xm, win, wback, kv, wqkv_v, wout_v, mod_v, gain_v, seg_x, qx, peak_v, part_out, part_in,
    act, mlp_out, mlp_in, z_out, z_in, gate_in,
    send_sems, recv_sems, local_sems,
):
    g = lax.axis_index("guide")
    s = lax.axis_index("seq")
    t = lax.axis_index("tp")
    x, y, c = s // 8, (s % 8) // 2, s % 2
    yr, yl = (y + 1) % 4, (y + 3) % 4

    def at_seq(xx, yy, cc):
        return {"seq": xx * 8 + yy * 2 + cc}

    x_right, x_left, x_far = at_seq((x + 1) % 4, y, c), at_seq((x + 3) % 4, y, c), at_seq((x + 2) % 4, y, c)
    y_right, y_left = at_seq(x, yr, c), at_seq(x, yl, c)
    mate = at_seq(x, y, 1 - c)
    t_right, t_left, t_far = {"tp": (t + 1) % 4}, {"tp": (t + 3) % 4}, {"tp": (t + 2) % 4}
    partner = {"guide": 1 - g}
    across = [{"guide": 1 - g, "tp": (t + step) % 4} for step in (1, 2, 3)]

    barrier = pltpu.get_barrier_semaphore()
    everyone = (x_right, x_left, x_far, y_right, y_left, mate, t_right, t_left, t_far, partner, *across)
    for device in everyone:
        pl.semaphore_signal(barrier, inc=1, device_id=device, device_id_type=pl.DeviceIdType.MESH)

    def columns(weight, dx, h=None):
        cols = pl.ds(pl.multiple_of(((x + dx) % 4) * GROUP, GROUP), GROUP)
        return weight.at[:, cols] if h is None else weight.at[pl.ds(h * 48, 48), cols]

    pairs = [
        (hidden, raw.at[0, 0]),
        (seg, seg_x.at[0]),
        (modulation, mod_v),
        (qk_gain, gain_v),
        (w_qkv.at[1], wqkv_v.at[1]),
        (w_qkv.at[2], wqkv_v.at[2]),
        (w_qkv.at[0], wqkv_v.at[0]),
        (columns(w_in, 0), win.at[0, y, c]),
        (w_back, wback.at[y, c]),
        (w_out, wout_v),
    ]
    local = [pltpu.make_async_copy(a, b, local_sems.at[i]) for i, (a, b) in enumerate(pairs)]
    for made in local:
        made.start()
    pl.semaphore_wait(barrier, len(everyone))

    links = Links(send_sems, recv_sems)
    half32 = lambda h: pl.ds(h * 32, 32)
    half48 = lambda h: pl.ds(h * 48, 48)
    two = lambda h: pl.ds(h * 2, 2)

    def relative(right, left, spot, own=None):
        spots = [(lambda d: (lambda h: spot(d, h)))(d) for d in (3, 1, 3, 1, 2, 2)]
        return RingGather(links, right, left, own or (lambda h: spot(0, h)), *spots)

    def absolute(spot, own=None):
        spots = [(lambda yy: (lambda h: spot(yy, h)))(yy) for yy in (y, y, yl, yr, yl, yr)]
        return RingGather(links, y_right, y_left, own or (lambda h: spot(y, h)), *spots)

    over_tp = relative(t_right, t_left, lambda d, h: raw.at[0, d, half32(h)], lambda h: hidden.at[half32(h)])
    over_x = [
        relative(
            x_right, x_left, (lambda k: (lambda d, h: raw.at[d, k, half32(h)]))(k),
            (lambda h: hidden.at[half32(h)]) if k == 0 else None,
        )
        for k in range(4)
    ]
    seg_sent = [
        links.copy(seg, seg_x.at[3], x_right),
        links.copy(seg, seg_x.at[1], x_left),
        links.copy(seg, seg_x.at[2], x_far),
    ]
    win_sent = [
        links.copy(columns(w_in, 1), win.at[2, y, c], x_right),
        links.copy(columns(w_in, 3), win.at[1, y, c], x_left),
        links.copy(columns(w_in, 2), win.at[3, y, c], x_far),
    ]
    win_near = absolute(lambda yy, h: win.at[0, yy, c, half48(h)], lambda h: columns(w_in, 0, h))
    win_sides = absolute(lambda yy, h: win.at[1:3, yy, c, half48(h)])
    win_rest = absolute(lambda yy, h: win.at[3, yy, c, half48(h)])
    wback_all = absolute(lambda yy, h: wback.at[yy, c, half48(h)], lambda h: w_back.at[half48(h)])

    def to_mate(spot):
        return links.copy(spot, spot, mate)

    over_first = to_mate(win.at[0, :, c])
    over_sides = [to_mate(win.at[1:3, yy, c]) for yy in (y, yr, yl, (y + 2) % 4)]
    over_rest = [to_mate(win.at[3, yy, c]) for yy in (y, yr, yl, (y + 2) % 4)]
    over_back = [to_mate(wback.at[yy, c]) for yy in (y, yr, yl, (y + 2) % 4)]
    kv_all = absolute(lambda yy, h: kv.at[yy, c, half32(h)])
    kv_over = links.copy(kv.at[:, c], kv.at[:, c], mate)
    q_all = relative(x_right, x_left, lambda d, h: qx.at[d, half32(h)])
    act_all = relative(x_right, x_left, lambda d, h: act.at[d, two(h)])

    gate_sent = links.copy(
        modulation.at[2, :, pl.ds(pl.multiple_of(t * WIDE + (1 - g) * GROUP, GROUP), GROUP)], gate_in, partner
    )

    over_tp.start()
    for made in win_sent:
        made.start()
    win_near.start()
    over_x[0].start()
    for made in seg_sent:
        made.start()
    gate_sent.start()

    win_near.forward()
    win_sent[0].wait_recv()
    win_sent[1].wait_recv()
    win_sides.start()
    over_sides[0].start()
    over_tp.forward()
    over_x[0].forward()
    win_sent[2].wait_recv()
    win_rest.start()
    over_rest[0].start()
    over_tp.near()
    over_x[3].start()
    over_x[1].start()
    win_sides.forward()
    for made in local[:4]:
        made.wait()
    for made in seg_sent:
        made.wait_recv()
    win_rest.forward()
    wback_all.begin()
    local[7].wait()
    win_near.finish()
    over_first.start()
    over_tp.far()
    over_x[2].start()

    at_row = lax.broadcasted_iota(jnp.int32, (ROWS, ROWS), 0)
    at_col = lax.broadcasted_iota(jnp.int32, (ROWS, ROWS), 1)
    lane = lax.broadcasted_iota(jnp.int32, (ROWS, HEAD), 1).astype(F32)

    def seg_column(d):
        row = jnp.broadcast_to(seg_x[d].astype(F32), (ROWS, ROWS))
        return jnp.sum(jnp.where(at_row == at_col, row, 0.0), axis=-1, keepdims=True)

    seg_cols = [seg_column(d) for d in range(4)]
    one_hots = [jnp.where(seg_cols[d] == lane, 1.0, 0.0).astype(BF16) for d in range(4)]

    def look_up(kind, offset, d):
        table = mod_v[kind, :, pl.ds(pl.multiple_of(offset, WIDE), WIDE)].astype(F32)
        found = jnp.broadcast_to(table[0:1], (ROWS, WIDE))
        for r in range(1, REQUESTS):
            found = jnp.where(seg_cols[d] == float(r), table[r : r + 1], found)
        return found

    def normalise(d):
        total = sum(jnp.sum(raw[d, k].astype(F32), axis=-1, keepdims=True) for k in range(4))
        mean = total * (1.0 / D)
        squares = jnp.zeros((ROWS, 1), F32)
        for k in range(4):
            centred = raw[d, k].astype(F32) - mean
            squares += jnp.sum(centred * centred, axis=-1, keepdims=True)
        scale_rows = lax.rsqrt(squares * (1.0 / D) + 1e-06)
        for k in range(4):
            offset = ((t + k) % 4) * WIDE
            normed = (raw[d, k].astype(F32) - mean) * scale_rows
            xm[d, :, pl.ds(pl.multiple_of(offset, WIDE), WIDE)] = (
                normed * (1.0 + look_up(1, offset, d)) + look_up(0, offset, d)
            ).astype(BF16)

    normalise(0)
    over_x[3].forward()
    over_x[1].forward()

    def head_norm(values, gain):
        return values * lax.rsqrt(jnp.mean(values * values, axis=-1, keepdims=True) + 1e-06) * gain

    rows_own = xm[0]
    local[4].wait()
    keys = dot(rows_own, wqkv_v[1])
    for h in range(HEADS_HERE):
        cols = slice(h * HEAD, (h + 1) * HEAD)
        kv[y, c, :, cols] = head_norm(keys[:, cols], gain_v[1:2, :]).astype(BF16)
    win_sides.near()
    over_sides[1].start()
    over_sides[2].start()
    local[5].wait()
    kv[y, c, :, GROUP : 2 * GROUP] = dot(rows_own, wqkv_v[2]).astype(BF16)
    kv[y, c, :, 2 * GROUP :] = one_hots[0]
    kv_all.start()
    over_x[2].forward()
    win_rest.near()
    over_rest[1].start()
    over_rest[2].start()
    win_sides.far()
    over_sides[3].start()
    win_rest.far()
    over_rest[3].start()
    local[6].wait()
    query = dot(rows_own, wqkv_v[0])
    for h in range(HEADS_HERE):
        cols = slice(h * HEAD, (h + 1) * HEAD)
        qx[0, :, cols] = head_norm(query[:, cols], gain_v[0:1, :]).astype(BF16)
    q_all.start()

    kv_all.forward()
    wback_all.follow()
    local[8].wait()
    over_back[0].start()
    wback_all.forward()
    for k in (0, 1, 3, 2):
        over_x[k].finish()
    normalise(1)
    q_all.forward()
    normalise(3)
    kv_all.finish()
    kv_over.start()
    normalise(2)
    for made in [over_first, *over_sides, *over_rest]:
        made.wait_recv()

    pre = jnp.zeros((4 * ROWS, GROUP), F32)
    for slot, d in enumerate((0, 1, 3, 2)):
        cols = pl.ds(pl.multiple_of(((x + d) % 4) * WIDE, WIDE), WIDE)
        pre += dot(xm[:, :, cols].reshape(4 * ROWS, WIDE), win[slot].reshape(WIDE, GROUP))
    acted = jax.nn.gelu(pre, approximate=True).astype(BF16)
    for d in range(4):
        act[0, (x + d) % 4] = acted[d * ROWS : (d + 1) * ROWS]
    act_all.start()

    q_all.finish()
    kv_over.wait_recv()

    seen = kv.reshape(8 * ROWS, KV)
    same = dot_t(jnp.concatenate(one_hots, axis=0), seen[:, 2 * GROUP :]) > 0.5
    lanes = lax.broadcasted_iota(jnp.int32, (4 * ROWS, HEAD), 1)
    stats = jnp.zeros((4 * ROWS, HEAD), F32)
    for h in range(HEADS_HERE):
        k_cols = slice(h * HEAD, (h + 1) * HEAD)
        v_cols = slice(GROUP + h * HEAD, GROUP + (h + 1) * HEAD)
        score = dot_t(qx[:, :, k_cols].reshape(4 * ROWS, HEAD), seen[:, k_cols]) * HEAD ** (-0.5)
        score = jnp.where(same, score, -1e30)
        peak_v[...] = jnp.broadcast_to(jnp.max(score, axis=-1, keepdims=True), (4 * ROWS, HEAD)).astype(BF16)
        peak = peak_v[:, 0:1].astype(F32)
        weight = jnp.where(same, jnp.exp(score - peak), 0.0)
        total = jnp.sum(weight, axis=-1, keepdims=True)
        summed = dot(weight.astype(BF16), seen[:, v_cols])
        part = (summed / jnp.where(total > 0.0, total, 1.0)).astype(BF16)
        part_out[:, :, k_cols] = part.reshape(4, ROWS, HEAD)
        upper = total.astype(BF16).astype(F32)
        stats = jnp.where(lanes == h, peak, stats)
        stats = jnp.where(lanes == 3 + h, upper, stats)
        stats = jnp.where(lanes == 6 + h, total - upper, stats)
        if h == 0:
            wback_all.near()
            over_back[1].start()
            over_back[2].start()
    part_out[:, :, GROUP:] = stats.astype(BF16).reshape(4, ROWS, HEAD)
    part_sent = [
        links.copy(part_out.at[2], part_in.at[2], x_far),
        links.copy(part_out.at[1], part_in.at[3], x_right),
        links.copy(part_out.at[3], part_in.at[1], x_left),
    ]
    for made in part_sent:
        made.start()
    act_all.forward()
    wback_all.far()
    over_back[3].start()
    for made in over_back:
        made.wait_recv()

    def back(d):
        cols = pl.ds(pl.multiple_of(((x + d) % 4) * GROUP, GROUP), GROUP)
        return dot_t(act[d].reshape(4 * ROWS, GROUP), wback[:, :, :, cols].reshape(WIDE, GROUP))

    fed = back(0)
    act_all.near()
    fed += back(1)
    fed += back(3)
    act_all.far()
    fed += back(2)
    for b in range(4):
        mlp_out[(b - x + 4) % 4] = fed[b * ROWS : (b + 1) * ROWS].astype(BF16)
    mlp_sent = {
        3: links.copy(mlp_out.at[1], mlp_in.at[3], x_right),
        1: links.copy(mlp_out.at[3], mlp_in.at[1], x_left),
        2: links.copy(mlp_out.at[2], mlp_in.at[2], x_far),
    }
    for made in mlp_sent.values():
        made.start()

    for made in part_sent:
        made.wait_recv()
    attended = []
    for h in range(HEADS_HERE):
        cols = slice(h * HEAD, (h + 1) * HEAD)
        parts = [part_out[0]] + [part_in[d] for d in (1, 2, 3)]
        stat = [p[:, GROUP:].astype(F32) for p in parts]
        top = stat[0][:, h : h + 1]
        for other in stat[1:]:
            top = jnp.maximum(top, other[:, h : h + 1])
        total = jnp.zeros((ROWS, 1), F32)
        summed = jnp.zeros((ROWS, HEAD), F32)
        for p, st in zip(parts, stat):
            share = jnp.exp(st[:, h : h + 1] - top) * (st[:, 3 + h : 4 + h] + st[:, 6 + h : 7 + h])
            total += share
            summed += share * p[:, cols].astype(F32)
        attended.append((summed / total).astype(BF16))
    attended = jnp.concatenate(attended, axis=1)
    local[9].wait()

    base = links.used
    own_cols = pl.ds(pl.multiple_of(g * GROUP, GROUP), GROUP)
    other_cols = pl.ds(pl.multiple_of((1 - g) * GROUP, GROUP), GROUP)

    def term_copy(d, kind, step):
        return pltpu.make_async_remote_copy(
            src_ref=z_out.at[d, :, (own_cols, other_cols)[kind]],
            dst_ref=z_in.at[kind, step],
            send_sem=send_sems.at[base + 4 * kind + step],
            recv_sem=recv_sems.at[base + 4 * kind + step],
            device_id={"guide": (g, 1 - g)[kind], "tp": (t + step) % 4},
            device_id_type=pl.DeviceIdType.MESH,
        )

    for d in (0, 1, 3, 2):
        e = (x + d) % 4
        step = (x + d - t + 4) % 4
        term = dot(attended, wout_v[:, pl.ds(pl.multiple_of(e * WIDE, WIDE), WIDE)])
        if d == 0:
            term += mlp_out[0].astype(F32)
        else:
            mlp_sent[d].wait_recv()
            term += mlp_in[d].astype(F32)
        z_out[d] = term.astype(BF16)
        term_copy(d, 1, step).start()

        @pl.when(step != 0)
        def _():
            term_copy(d, 0, step).start()

    gate_sent.wait_recv()
    own_table = mod_v[2, :, pl.ds(pl.multiple_of(t * WIDE + g * GROUP, GROUP), GROUP)].astype(F32)
    other_table = gate_in[...].astype(F32)

    def gate_of(table):
        found = jnp.broadcast_to(table[0:1], (ROWS, GROUP))
        for r in range(1, REQUESTS):
            found = jnp.where(seg_cols[0] == float(r), table[r : r + 1], found)
        return found

    own_gate, other_gate = gate_of(own_table), gate_of(other_table)
    residual = raw[0, 0, :, own_cols].astype(F32)
    own_branch = z_out[(t - x + 4) % 4, :, own_cols].astype(F32)
    arrived = [term_copy(0, 0, step) for step in (1, 2, 3)] + [term_copy(0, 1, step) for step in range(4)]
    for made in arrived:
        made.wait_recv()
    for step in (1, 2, 3):
        own_branch += z_in[0, step].astype(F32)
    other_branch = z_in[1, 0].astype(F32)
    for step in (1, 2, 3):
        other_branch += z_in[1, step].astype(F32)
    mine = (residual + own_gate * own_branch).astype(BF16).astype(F32)
    theirs = (residual + other_gate * other_branch).astype(BF16).astype(F32)
    cond = jnp.where(g == 0, mine, theirs)
    uncond = jnp.where(g == 0, theirs, mine)
    result[...] = (uncond + GUIDANCE * (cond - uncond)).astype(BF16)
    for made in arrived:
        made.wait_send()
    links.drain()


def on_device(hidden, seg_ids, modulation, qk_gain, w_qkv, w_mlp_in, w_out, w_mlp_back):
    anywhere = pl.BlockSpec(memory_space=pl.ANY)
    guided = pl.pallas_call(
        body,
        out_shape=jax.ShapeDtypeStruct((ROWS, GROUP), BF16),
        in_specs=[anywhere] * 8,
        out_specs=pl.BlockSpec(memory_space=pltpu.VMEM),
        scratch_shapes=[
            pltpu.VMEM((4, 4, ROWS, WIDE), BF16),
            pltpu.VMEM((4, ROWS, D), BF16),
            pltpu.VMEM((4, 4, 2, SLAB, GROUP), BF16),
            pltpu.VMEM((4, 2, SLAB, 4 * GROUP), BF16),
            pltpu.VMEM((4, 2, ROWS, KV), BF16),
            pltpu.VMEM((3, D, GROUP), BF16),
            pltpu.VMEM((GROUP, D), BF16),
            pltpu.VMEM((3, REQUESTS, D), BF16),
            pltpu.VMEM((2, HEAD), F32),
            pltpu.VMEM((4, 1, ROWS), jnp.int32),
            pltpu.VMEM((4, ROWS, GROUP), BF16),
            pltpu.VMEM((4 * ROWS, HEAD), BF16),
            pltpu.VMEM((4, ROWS, GROUP + HEAD), BF16),
            pltpu.VMEM((4, ROWS, GROUP + HEAD), BF16),
            pltpu.VMEM((4, 4, ROWS, GROUP), BF16),
            pltpu.VMEM((4, ROWS, WIDE), BF16),
            pltpu.VMEM((4, ROWS, WIDE), BF16),
            pltpu.VMEM((4, ROWS, WIDE), BF16),
            pltpu.VMEM((2, 4, ROWS, GROUP), BF16),
            pltpu.VMEM((REQUESTS, GROUP), BF16),
            pltpu.SemaphoreType.DMA((COPIES,)),
            pltpu.SemaphoreType.DMA((COPIES,)),
            pltpu.SemaphoreType.DMA((LOCALS,)),
        ],
        compiler_params=pltpu.CompilerParams(
            collective_id=0, has_side_effects=True, vmem_limit_bytes=60 * 1024 * 1024
        ),
        name="layer",
    )(
        hidden,
        seg_ids.reshape(1, ROWS),
        jnp.transpose(modulation[0], (1, 0, 2)),
        qk_gain,
        jnp.transpose(w_qkv, (1, 0, 2)),
        w_mlp_in,
        w_out,
        w_mlp_back,
    )
    return guided.reshape(ROWS, 1, 1, GROUP)


def solution(mesh):
    in_specs = (
        P("seq", "tp"),
        P("seq"),
        P("guide", None, None, None),
        P(),
        P(None, None, "tp"),
        P("seq", "tp"),
        P("tp", None),
        P("seq", "tp"),
    )
    out_specs = P("seq", "tp", "guide", None)
    return jax.shard_map(
        on_device, mesh=mesh, in_specs=in_specs, out_specs=out_specs, check_vma=False
    )
```

```python
import jax
import jax.numpy as jnp
from jax import lax
from jax.experimental import pallas as pl
from jax.experimental.pallas import tpu as pltpu
from jax.sharding import PartitionSpec as P

D = 3072
HEAD = 128
ROWS = 64
WIDE = 768
GROUP = 384
SLAB = 96
HEADS_HERE = 3
REQUESTS = 4
KV = 2 * GROUP + HEAD
GUIDANCE = 3.5
COPIES = 128
LOCALS = 10

F32 = jnp.float32
BF16 = jnp.bfloat16


def dot(a, b):
    return jnp.dot(a, b, preferred_element_type=F32)


def dot_t(a, b):
    return lax.dot_general(a, b, (((1,), (1,)), ((), ())), preferred_element_type=F32)


class Links:
    def __init__(self, send_sems, recv_sems):
        self.send_sems, self.recv_sems = send_sems, recv_sems
        self.used = 0
        self.sent = []

    def copy(self, src, dst, device):
        i = self.used
        self.used += 1
        made = pltpu.make_async_remote_copy(
            src_ref=src,
            dst_ref=dst,
            send_sem=self.send_sems.at[i],
            recv_sem=self.recv_sems.at[i],
            device_id=device,
            device_id_type=pl.DeviceIdType.MESH,
        )
        self.sent.append(made)
        return made

    def drain(self):
        for made in self.sent:
            made.wait_send()


class RingGather:
    def __init__(self, links, right, left, own, at_right, at_left, from_left, from_right, on_right, on_left):
        self.first = [
            links.copy(own(0), at_right(0), right),
            links.copy(own(1), at_left(1), left),
            links.copy(own(1), at_right(1), right),
            links.copy(own(0), at_left(0), left),
        ]
        self.onward = [
            links.copy(from_left(0), on_right(0), right),
            links.copy(from_right(1), on_left(1), left),
        ]

    def begin(self):
        self.first[0].start()
        self.first[1].start()

    def follow(self):
        self.first[2].start()
        self.first[3].start()

    def start(self):
        self.begin()
        self.follow()

    def forward(self):
        self.first[0].wait_recv()
        self.onward[0].start()
        self.first[1].wait_recv()
        self.onward[1].start()

    def near(self):
        self.first[2].wait_recv()
        self.first[3].wait_recv()

    def far(self):
        self.onward[0].wait_recv()
        self.onward[1].wait_recv()

    def finish(self):
        self.near()
        self.far()


def body(
    hidden, seg, modulation, qk_gain, w_qkv, w_in, w_out, w_back,
    result,
    raw, xm, win, wback, kv, wqkv_v, wout_v, mod_v, gain_v, seg_x, qx, peak_v, part_out, part_in,
    act, mlp_out, mlp_in, z_out, z_in, gate_in,
    send_sems, recv_sems, local_sems,
):
    g = lax.axis_index("guide")
    s = lax.axis_index("seq")
    t = lax.axis_index("tp")
    x, y, c = s // 8, (s % 8) // 2, s % 2
    yr, yl = (y + 1) % 4, (y + 3) % 4

    def at_seq(xx, yy, cc):
        return {"seq": xx * 8 + yy * 2 + cc}

    x_right, x_left, x_far = at_seq((x + 1) % 4, y, c), at_seq((x + 3) % 4, y, c), at_seq((x + 2) % 4, y, c)
    y_right, y_left = at_seq(x, yr, c), at_seq(x, yl, c)
    mate = at_seq(x, y, 1 - c)
    t_right, t_left, t_far = {"tp": (t + 1) % 4}, {"tp": (t + 3) % 4}, {"tp": (t + 2) % 4}
    partner = {"guide": 1 - g}
    across = [{"guide": 1 - g, "tp": (t + step) % 4} for step in (1, 2, 3)]

    barrier = pltpu.get_barrier_semaphore()
    everyone = (x_right, x_left, x_far, y_right, y_left, mate, t_right, t_left, t_far, partner, *across)
    for device in everyone:
        pl.semaphore_signal(barrier, inc=1, device_id=device, device_id_type=pl.DeviceIdType.MESH)

    def columns(weight, dx, h=None):
        cols = pl.ds(pl.multiple_of(((x + dx) % 4) * GROUP, GROUP), GROUP)
        return weight.at[:, cols] if h is None else weight.at[pl.ds(h * 48, 48), cols]

    pairs = [
        (hidden, raw.at[0, 0]),
        (seg, seg_x.at[0]),
        (modulation, mod_v),
        (qk_gain, gain_v),
        (w_qkv.at[1], wqkv_v.at[1]),
        (w_qkv.at[2], wqkv_v.at[2]),
        (w_qkv.at[0], wqkv_v.at[0]),
        (columns(w_in, 0), win.at[0, y, c]),
        (w_back, wback.at[y, c]),
        (w_out, wout_v),
    ]
    local = [pltpu.make_async_copy(a, b, local_sems.at[i]) for i, (a, b) in enumerate(pairs)]
    for made in local:
        made.start()
    pl.semaphore_wait(barrier, len(everyone))

    links = Links(send_sems, recv_sems)
    half32 = lambda h: pl.ds(h * 32, 32)
    half48 = lambda h: pl.ds(h * 48, 48)
    two = lambda h: pl.ds(h * 2, 2)

    def relative(right, left, spot, own=None):
        spots = [(lambda d: (lambda h: spot(d, h)))(d) for d in (3, 1, 3, 1, 2, 2)]
        return RingGather(links, right, left, own or (lambda h: spot(0, h)), *spots)

    def absolute(spot, own=None):
        spots = [(lambda yy: (lambda h: spot(yy, h)))(yy) for yy in (y, y, yl, yr, yl, yr)]
        return RingGather(links, y_right, y_left, own or (lambda h: spot(y, h)), *spots)

    over_tp = relative(t_right, t_left, lambda d, h: raw.at[0, d, half32(h)], lambda h: hidden.at[half32(h)])
    over_x = [
        relative(
            x_right, x_left, (lambda k: (lambda d, h: raw.at[d, k, half32(h)]))(k),
            (lambda h: hidden.at[half32(h)]) if k == 0 else None,
        )
        for k in range(4)
    ]
    seg_sent = [
        links.copy(seg, seg_x.at[3], x_right),
        links.copy(seg, seg_x.at[1], x_left),
        links.copy(seg, seg_x.at[2], x_far),
    ]
    win_sent = [
        links.copy(columns(w_in, 1), win.at[2, y, c], x_right),
        links.copy(columns(w_in, 3), win.at[1, y, c], x_left),
        links.copy(columns(w_in, 2), win.at[3, y, c], x_far),
    ]
    win_near = absolute(lambda yy, h: win.at[0, yy, c, half48(h)], lambda h: columns(w_in, 0, h))
    win_sides = absolute(lambda yy, h: win.at[1:3, yy, c, half48(h)])
    win_rest = absolute(lambda yy, h: win.at[3, yy, c, half48(h)])
    wback_all = absolute(lambda yy, h: wback.at[yy, c, half48(h)], lambda h: w_back.at[half48(h)])

    def to_mate(spot):
        return links.copy(spot, spot, mate)

    over_first = to_mate(win.at[0, :, c])
    over_sides = [to_mate(win.at[1:3, yy, c]) for yy in (y, yr, yl, (y + 2) % 4)]
    over_rest = [to_mate(win.at[3, yy, c]) for yy in (y, yr, yl, (y + 2) % 4)]
    over_back = [to_mate(wback.at[yy, c]) for yy in (y, yr, yl, (y + 2) % 4)]
    kv_all = absolute(lambda yy, h: kv.at[yy, c, half32(h)])
    kv_over = links.copy(kv.at[:, c], kv.at[:, c], mate)
    q_all = relative(x_right, x_left, lambda d, h: qx.at[d, half32(h)])
    act_all = relative(x_right, x_left, lambda d, h: act.at[d, two(h)])

    gate_sent = links.copy(
        modulation.at[2, :, pl.ds(pl.multiple_of(t * WIDE + (1 - g) * GROUP, GROUP), GROUP)], gate_in, partner
    )

    over_tp.start()
    for made in win_sent:
        made.start()
    win_near.start()
    over_x[0].start()
    for made in seg_sent:
        made.start()
    gate_sent.start()

    win_near.forward()
    win_sent[0].wait_recv()
    win_sent[1].wait_recv()
    win_sides.start()
    over_sides[0].start()
    over_tp.forward()
    over_x[0].forward()
    win_sent[2].wait_recv()
    win_rest.start()
    over_rest[0].start()
    over_tp.near()
    over_x[3].start()
    over_x[1].start()
    win_sides.forward()
    for made in local[:4]:
        made.wait()
    for made in seg_sent:
        made.wait_recv()
    win_rest.forward()
    wback_all.begin()
    local[7].wait()
    win_near.finish()
    over_first.start()
    over_x[3].forward()
    over_x[1].forward()
    over_tp.far()
    over_x[2].start()

    at_row = lax.broadcasted_iota(jnp.int32, (ROWS, ROWS), 0)
    at_col = lax.broadcasted_iota(jnp.int32, (ROWS, ROWS), 1)
    lane = lax.broadcasted_iota(jnp.int32, (ROWS, HEAD), 1).astype(F32)

    def seg_column(d):
        row = jnp.broadcast_to(seg_x[d].astype(F32), (ROWS, ROWS))
        return jnp.sum(jnp.where(at_row == at_col, row, 0.0), axis=-1, keepdims=True)

    seg_cols = [seg_column(d) for d in range(4)]
    one_hots = [jnp.where(seg_cols[d] == lane, 1.0, 0.0).astype(BF16) for d in range(4)]

    def look_up(kind, offset, d):
        table = mod_v[kind, :, pl.ds(pl.multiple_of(offset, WIDE), WIDE)].astype(F32)
        found = jnp.broadcast_to(table[0:1], (ROWS, WIDE))
        for r in range(1, REQUESTS):
            found = jnp.where(seg_cols[d] == float(r), table[r : r + 1], found)
        return found

    def normalise(d):
        total = sum(jnp.sum(raw[d, k].astype(F32), axis=-1, keepdims=True) for k in range(4))
        mean = total * (1.0 / D)
        squares = jnp.zeros((ROWS, 1), F32)
        for k in range(4):
            centred = raw[d, k].astype(F32) - mean
            squares += jnp.sum(centred * centred, axis=-1, keepdims=True)
        scale_rows = lax.rsqrt(squares * (1.0 / D) + 1e-06)
        for k in range(4):
            offset = ((t + k) % 4) * WIDE
            normed = (raw[d, k].astype(F32) - mean) * scale_rows
            xm[d, :, pl.ds(pl.multiple_of(offset, WIDE), WIDE)] = (
                normed * (1.0 + look_up(1, offset, d)) + look_up(0, offset, d)
            ).astype(BF16)

    normalise(0)

    def head_norm(values, gain):
        return values * lax.rsqrt(jnp.mean(values * values, axis=-1, keepdims=True) + 1e-06) * gain

    rows_own = xm[0]
    local[4].wait()
    keys = dot(rows_own, wqkv_v[1])
    for h in range(HEADS_HERE):
        cols = slice(h * HEAD, (h + 1) * HEAD)
        kv[y, c, :, cols] = head_norm(keys[:, cols], gain_v[1:2, :]).astype(BF16)
    win_sides.near()
    over_sides[1].start()
    over_sides[2].start()
    local[5].wait()
    kv[y, c, :, GROUP : 2 * GROUP] = dot(rows_own, wqkv_v[2]).astype(BF16)
    kv[y, c, :, 2 * GROUP :] = one_hots[0]
    kv_all.start()
    over_x[2].forward()
    win_rest.near()
    over_rest[1].start()
    over_rest[2].start()
    win_sides.far()
    over_sides[3].start()
    win_rest.far()
    over_rest[3].start()
    local[6].wait()
    query = dot(rows_own, wqkv_v[0])
    for h in range(HEADS_HERE):
        cols = slice(h * HEAD, (h + 1) * HEAD)
        qx[0, :, cols] = head_norm(query[:, cols], gain_v[0:1, :]).astype(BF16)
    q_all.start()

    kv_all.forward()
    wback_all.follow()
    local[8].wait()
    over_back[0].start()
    wback_all.forward()
    for k in (0, 1, 3, 2):
        over_x[k].finish()
    normalise(1)
    q_all.forward()
    normalise(3)
    kv_all.finish()
    kv_over.start()
    normalise(2)
    for made in [over_first, *over_sides, *over_rest]:
        made.wait_recv()

    pre = jnp.zeros((4 * ROWS, GROUP), F32)
    for slot, d in enumerate((0, 1, 3, 2)):
        cols = pl.ds(pl.multiple_of(((x + d) % 4) * WIDE, WIDE), WIDE)
        pre += dot(xm[:, :, cols].reshape(4 * ROWS, WIDE), win[slot].reshape(WIDE, GROUP))
    acted = jax.nn.gelu(pre, approximate=True).astype(BF16)
    for d in range(4):
        act[0, (x + d) % 4] = acted[d * ROWS : (d + 1) * ROWS]
    act_all.start()

    q_all.finish()
    kv_over.wait_recv()

    seen = kv.reshape(8 * ROWS, KV)
    same = dot_t(jnp.concatenate(one_hots, axis=0), seen[:, 2 * GROUP :]) > 0.5
    lanes = lax.broadcasted_iota(jnp.int32, (4 * ROWS, HEAD), 1)
    stats = jnp.zeros((4 * ROWS, HEAD), F32)
    for h in range(HEADS_HERE):
        k_cols = slice(h * HEAD, (h + 1) * HEAD)
        v_cols = slice(GROUP + h * HEAD, GROUP + (h + 1) * HEAD)
        score = dot_t(qx[:, :, k_cols].reshape(4 * ROWS, HEAD), seen[:, k_cols]) * HEAD ** (-0.5)
        score = jnp.where(same, score, -1e30)
        peak_v[...] = jnp.broadcast_to(jnp.max(score, axis=-1, keepdims=True), (4 * ROWS, HEAD)).astype(BF16)
        peak = peak_v[:, 0:1].astype(F32)
        weight = jnp.where(same, jnp.exp(score - peak), 0.0)
        total = jnp.sum(weight, axis=-1, keepdims=True)
        summed = dot(weight.astype(BF16), seen[:, v_cols])
        part = (summed / jnp.where(total > 0.0, total, 1.0)).astype(BF16)
        part_out[:, :, k_cols] = part.reshape(4, ROWS, HEAD)
        upper = total.astype(BF16).astype(F32)
        stats = jnp.where(lanes == h, peak, stats)
        stats = jnp.where(lanes == 3 + h, upper, stats)
        stats = jnp.where(lanes == 6 + h, total - upper, stats)
        if h == 0:
            wback_all.near()
            over_back[1].start()
            over_back[2].start()
        if h == 1:
            act_all.forward()
    part_out[:, :, GROUP:] = stats.astype(BF16).reshape(4, ROWS, HEAD)
    part_sent = [
        links.copy(part_out.at[2], part_in.at[2], x_far),
        links.copy(part_out.at[1], part_in.at[3], x_right),
        links.copy(part_out.at[3], part_in.at[1], x_left),
    ]
    for made in part_sent:
        made.start()
    wback_all.far()
    over_back[3].start()
    for made in over_back:
        made.wait_recv()

    def back(d):
        cols = pl.ds(pl.multiple_of(((x + d) % 4) * GROUP, GROUP), GROUP)
        return dot_t(act[d].reshape(4 * ROWS, GROUP), wback[:, :, :, cols].reshape(WIDE, GROUP))

    fed = back(0)
    act_all.near()
    fed += back(1)
    fed += back(3)
    act_all.far()
    fed += back(2)
    for b in range(4):
        mlp_out[(b - x + 4) % 4] = fed[b * ROWS : (b + 1) * ROWS].astype(BF16)
    mlp_sent = {
        3: links.copy(mlp_out.at[1], mlp_in.at[3], x_right),
        1: links.copy(mlp_out.at[3], mlp_in.at[1], x_left),
        2: links.copy(mlp_out.at[2], mlp_in.at[2], x_far),
    }
    for made in mlp_sent.values():
        made.start()

    for made in part_sent:
        made.wait_recv()
    attended = []
    for h in range(HEADS_HERE):
        cols = slice(h * HEAD, (h + 1) * HEAD)
        parts = [part_out[0]] + [part_in[d] for d in (1, 2, 3)]
        stat = [p[:, GROUP:].astype(F32) for p in parts]
        top = stat[0][:, h : h + 1]
        for other in stat[1:]:
            top = jnp.maximum(top, other[:, h : h + 1])
        total = jnp.zeros((ROWS, 1), F32)
        summed = jnp.zeros((ROWS, HEAD), F32)
        for p, st in zip(parts, stat):
            share = jnp.exp(st[:, h : h + 1] - top) * (st[:, 3 + h : 4 + h] + st[:, 6 + h : 7 + h])
            total += share
            summed += share * p[:, cols].astype(F32)
        attended.append((summed / total).astype(BF16))
    attended = jnp.concatenate(attended, axis=1)
    local[9].wait()

    base = links.used
    own_cols = pl.ds(pl.multiple_of(g * GROUP, GROUP), GROUP)
    other_cols = pl.ds(pl.multiple_of((1 - g) * GROUP, GROUP), GROUP)

    def term_copy(d, kind, step):
        return pltpu.make_async_remote_copy(
            src_ref=z_out.at[d, :, (own_cols, other_cols)[kind]],
            dst_ref=z_in.at[kind, step],
            send_sem=send_sems.at[base + 4 * kind + step],
            recv_sem=recv_sems.at[base + 4 * kind + step],
            device_id={"guide": (g, 1 - g)[kind], "tp": (t + step) % 4},
            device_id_type=pl.DeviceIdType.MESH,
        )

    for d in (0, 1, 3, 2):
        e = (x + d) % 4
        step = (x + d - t + 4) % 4
        term = dot(attended, wout_v[:, pl.ds(pl.multiple_of(e * WIDE, WIDE), WIDE)])
        if d == 0:
            term += mlp_out[0].astype(F32)
        else:
            mlp_sent[d].wait_recv()
            term += mlp_in[d].astype(F32)
        z_out[d] = term.astype(BF16)
        term_copy(d, 1, step).start()

        @pl.when(step != 0)
        def _():
            term_copy(d, 0, step).start()

    gate_sent.wait_recv()
    own_table = mod_v[2, :, pl.ds(pl.multiple_of(t * WIDE + g * GROUP, GROUP), GROUP)].astype(F32)
    other_table = gate_in[...].astype(F32)

    def gate_of(table):
        found = jnp.broadcast_to(table[0:1], (ROWS, GROUP))
        for r in range(1, REQUESTS):
            found = jnp.where(seg_cols[0] == float(r), table[r : r + 1], found)
        return found

    own_gate, other_gate = gate_of(own_table), gate_of(other_table)
    residual = raw[0, 0, :, own_cols].astype(F32)
    own_branch = z_out[(t - x + 4) % 4, :, own_cols].astype(F32)
    arrived = [term_copy(0, 0, step) for step in (1, 2, 3)] + [term_copy(0, 1, step) for step in range(4)]
    for made in arrived:
        made.wait_recv()
    for step in (1, 2, 3):
        own_branch += z_in[0, step].astype(F32)
    other_branch = z_in[1, 0].astype(F32)
    for step in (1, 2, 3):
        other_branch += z_in[1, step].astype(F32)
    mine = (residual + own_gate * own_branch).astype(BF16).astype(F32)
    theirs = (residual + other_gate * other_branch).astype(BF16).astype(F32)
    cond = jnp.where(g == 0, mine, theirs)
    uncond = jnp.where(g == 0, theirs, mine)
    result[...] = (uncond + GUIDANCE * (cond - uncond)).astype(BF16)
    for made in arrived:
        made.wait_send()
    links.drain()


def on_device(hidden, seg_ids, modulation, qk_gain, w_qkv, w_mlp_in, w_out, w_mlp_back):
    anywhere = pl.BlockSpec(memory_space=pl.ANY)
    guided = pl.pallas_call(
        body,
        out_shape=jax.ShapeDtypeStruct((ROWS, GROUP), BF16),
        in_specs=[anywhere] * 8,
        out_specs=pl.BlockSpec(memory_space=pltpu.VMEM),
        scratch_shapes=[
            pltpu.VMEM((4, 4, ROWS, WIDE), BF16),
            pltpu.VMEM((4, ROWS, D), BF16),
            pltpu.VMEM((4, 4, 2, SLAB, GROUP), BF16),
            pltpu.VMEM((4, 2, SLAB, 4 * GROUP), BF16),
            pltpu.VMEM((4, 2, ROWS, KV), BF16),
            pltpu.VMEM((3, D, GROUP), BF16),
            pltpu.VMEM((GROUP, D), BF16),
            pltpu.VMEM((3, REQUESTS, D), BF16),
            pltpu.VMEM((2, HEAD), F32),
            pltpu.VMEM((4, 1, ROWS), jnp.int32),
            pltpu.VMEM((4, ROWS, GROUP), BF16),
            pltpu.VMEM((4 * ROWS, HEAD), BF16),
            pltpu.VMEM((4, ROWS, GROUP + HEAD), BF16),
            pltpu.VMEM((4, ROWS, GROUP + HEAD), BF16),
            pltpu.VMEM((4, 4, ROWS, GROUP), BF16),
            pltpu.VMEM((4, ROWS, WIDE), BF16),
            pltpu.VMEM((4, ROWS, WIDE), BF16),
            pltpu.VMEM((4, ROWS, WIDE), BF16),
            pltpu.VMEM((2, 4, ROWS, GROUP), BF16),
            pltpu.VMEM((REQUESTS, GROUP), BF16),
            pltpu.SemaphoreType.DMA((COPIES,)),
            pltpu.SemaphoreType.DMA((COPIES,)),
            pltpu.SemaphoreType.DMA((LOCALS,)),
        ],
        compiler_params=pltpu.CompilerParams(
            collective_id=0, has_side_effects=True, vmem_limit_bytes=60 * 1024 * 1024
        ),
        name="layer",
    )(
        hidden,
        seg_ids.reshape(1, ROWS),
        jnp.transpose(modulation[0], (1, 0, 2)),
        qk_gain,
        jnp.transpose(w_qkv, (1, 0, 2)),
        w_mlp_in,
        w_out,
        w_mlp_back,
    )
    return guided.reshape(ROWS, 1, 1, GROUP)


def solution(mesh):
    in_specs = (
        P("seq", "tp"),
        P("seq"),
        P("guide", None, None, None),
        P(),
        P(None, None, "tp"),
        P("seq", "tp"),
        P("tp", None),
        P("seq", "tp"),
    )
    out_specs = P("seq", "tp", "guide", None)
    return jax.shard_map(
        on_device, mesh=mesh, in_specs=in_specs, out_specs=out_specs, check_vma=False
    )
```
